32 devices in a mesh: focus: 2 (over y), tx: 4 (over z), ty: 2 (over core), dose: 2 (over x).
Axes of the slice: x: 2, y: 2, z: 4, core: 2. Of those that a mesh axis runs over, the one named last changes fastest.
Arguments:
- aerial_image: float32 [64, 32, 256], P('focus', 'tx', 'ty'), parts along dimension 0, may hold values from 0.2 to 2
- quencher: float32 [32, 32, 256], P(None, 'tx', 'ty'), may hold values from 0.1 to 0.8
- cotangent: float32 [8, 32, 32, 256], P(('focus', 'dose'), None, 'tx', 'ty'), parts along dimension 0, may hold values from -6 to 6
- dose_levels: float32 [16], replicated, may hold values from 0.5 to 2
- dose_index: int32 [8], P(('focus', 'dose')), parts along dimension 0, may hold values from 0 to 15
Outputs:
- image_grad: float32 [64, 32, 256], P(('focus', 'dose'), 'tx', 'ty'), parts along dimension 0
The draws below stay inside these ranges and needn't reach their ends.
There are 2 independent parts, one for each index of `focus`. The reference program is written for one: setup_inputs(seed, part) draws one part's arguments, and reference() takes and returns one part's arrays. A program takes and returns all parts, laid end to end along the dimension named above; an argument that names none is the same for every part. Nothing has to cross between parts.
All inputs are finite; a program needn't handle non-finite values.
Results may differ from the reference program's by a relative error of at most 0.00002.
Values sent between devices are 32-bit elements; how exact they have to be, the bound alone decides.
No kernel may reach another device: no remote copies, remote signals or barrier semaphores. Data moves between devices by JAX's collectives and lax.ppermute only.
A program may use at most 64 MiB of HBM per device.

```python
import math
import jax
import jax.numpy as jnp
from jax import lax

Z = 32
STEPS = 4
LEVELS = 16
DOSES = 4
NX = 32
NY = 256


def draw_aerial_image(key, part):
    shift_key = jax.random.fold_in(key, 11)
    value_key = jax.random.fold_in(key, 12)
    parity_shift = jax.random.randint(shift_key, (), 0, 2)
    depth_index = lax.broadcasted_iota(jnp.int32, (Z, NX, NY), 0)
    row_index = lax.broadcasted_iota(jnp.int32, (Z, NX, NY), 1)
    column_index = lax.broadcasted_iota(jnp.int32, (Z, NX, NY), 2)
    parity = (depth_index + row_index + column_index + parity_shift) % 2
    unit_draw = jax.random.uniform(value_key, (Z, NX, NY), jnp.float32)
    high_band = 0.9 * jnp.exp(unit_draw * math.log(2.0 / 0.9))
    low_band = 0.2 * jnp.exp(unit_draw * math.log(0.45 / 0.2))
    return jnp.where(parity == 1, high_band, low_band).astype(jnp.float32)


def place_ends(values, stream_key, low, high):
    place = [jax.random.randint(jax.random.fold_in(stream_key, axis), (), 0, length) for axis, length in enumerate(values.shape)]
    widest = values.shape.index(max(values.shape))
    beside = place[:widest] + [(place[widest] + 1) % values.shape[widest]] + place[widest + 1:]
    return values.at[tuple(place)].set(low).at[tuple(beside)].set(high)


def block_levels(stream_key, extent, pieces, least, top_value):
    factor_of = 1.0
    for dim, parts in pieces:
        steps = jax.random.uniform(jax.random.fold_in(jax.random.fold_in(stream_key, 6), dim), (parts,), jnp.float32, least / len(pieces), top_value / len(pieces))
        factor_of = factor_of * jnp.repeat(jnp.exp(steps), extent[dim] // parts).reshape((-1,) + (1,) * (len(extent) - 1 - dim))
    return factor_of


def scatter_about(own_key, shape, spread, most, split=(), kind=jnp.bfloat16):
    gain = block_levels(own_key, shape, split, -0.22, 0.18) if split else 1.0
    entries = jax.random.normal(own_key, shape, jnp.float32) * spread * gain
    return jnp.minimum(jnp.maximum(entries, -most), most).astype(kind)


def setup_inputs(seed: int = 0, part: int = 0) -> dict:
    arg_keys = jax.random.split(jax.random.key(seed), 6)
    own_keys = jax.random.split(jax.random.fold_in(arg_keys[5], part), 6)
    return {
        "aerial_image": draw_aerial_image(jax.random.fold_in(jax.random.fold_in(arg_keys[5], part), 71), part),
        "quencher": jnp.clip(0.1 + 0.7 * jax.random.uniform(arg_keys[1], (Z, NX, NY), jnp.float32) ** block_levels(arg_keys[1], (Z, NX, NY), ((1, 4), (2, 2)), -0.2, 0.2), 0.1, 0.8),
        "cotangent": scatter_about(own_keys[2], (DOSES, Z, NX, NY), 1.0, 6.0, ((0, 2), (2, 4), (3, 2)), jnp.float32),
        "dose_levels": jnp.clip(jax.random.uniform(arg_keys[3], (LEVELS,), jnp.float32, 0.5, 2.0), 0.5, 2.0),
        "dose_index": place_ends(jax.random.randint(own_keys[4], (DOSES,), 0, LEVELS), jax.random.fold_in(own_keys[4], 1), 0, LEVELS - 1).astype(jnp.int32),
    }


exposure_rate = 1.0
neutral_rate = 0.8
deprotect_rate = 0.5
acid_lateral = 0.23
acid_depth = 0.02
base_lateral = 0.2
base_depth = 0.02


def lateral_part(field):
    return jnp.roll(field, 1, -2) + jnp.roll(field, -1, -2) + jnp.roll(field, 1, -1) + jnp.roll(field, -1, -1) - 4.0 * field


def depth_part(field):
    upward = jnp.concatenate((field[1:], field[-1:]), axis=0)
    downward = jnp.concatenate((field[:1], field[:-1]), axis=0)
    return upward + downward - 2.0 * field


def reference(aerial_image, quencher, cotangent, dose_levels, dose_index):
    levels = jnp.arange(LEVELS, dtype=jnp.int32)
    choose_mask = (dose_index[:, None] == levels[None, :]).astype(dose_levels.dtype)
    dose_value = jnp.sum(choose_mask * dose_levels[None, :], axis=1)

    def per_dose(summed, dose_item):
        dose_now, weight = dose_item
        absorbed = jnp.exp(-exposure_rate * dose_now * aerial_image)
        acid_now = 1.0 - absorbed
        quench_now = quencher
        protect = jnp.ones_like(aerial_image)
        history = []
        for bake_step in range(STEPS):
            history.append((acid_now, quench_now, protect))
            reaction = neutral_rate * acid_now * quench_now
            next_acid = acid_now + acid_lateral * lateral_part(acid_now) + acid_depth * depth_part(acid_now) - reaction
            next_quench = quench_now + base_lateral * lateral_part(quench_now) + base_depth * depth_part(quench_now) - reaction
            protect = protect * (1.0 - deprotect_rate * acid_now)
            acid_now, quench_now = next_acid, next_quench
        adj_acid = jnp.zeros_like(aerial_image)
        adj_quench = jnp.zeros_like(aerial_image)
        adj_protect = weight
        for bake_step in reversed(range(STEPS)):
            acid_old, quench_old, protect_old = history[bake_step]
            adj_sum = adj_acid + adj_quench
            next_acid = adj_acid + acid_lateral * lateral_part(adj_acid) + acid_depth * depth_part(adj_acid) - neutral_rate * quench_old * adj_sum - deprotect_rate * protect_old * adj_protect
            next_quench = adj_quench + base_lateral * lateral_part(adj_quench) + base_depth * depth_part(adj_quench) - neutral_rate * acid_old * adj_sum
            adj_protect = adj_protect * (1.0 - deprotect_rate * acid_old)
            adj_acid, adj_quench = next_acid, next_quench
        return summed + adj_acid * exposure_rate * dose_now * absorbed, None

    summed, unused = lax.scan(per_dose, jnp.zeros_like(aerial_image), (dose_value, cotangent))
    return summed
```

```python
import jax
import jax.numpy as jnp
from jax import lax
from jax.experimental import pallas as pl
from jax.experimental.pallas import tpu as pltpu
from jax.sharding import PartitionSpec as P

exposure_rate = 1.0
neutral_rate = 0.8
deprotect_rate = 0.5
acid_lateral = 0.23
acid_depth = 0.02
base_lateral = 0.2
base_depth = 0.02

HALO_AERIAL = 5
HALO_QUENCH = 4
HALO_COT = 3
HALO_ROWS = HALO_AERIAL + HALO_QUENCH + 2 * HALO_COT

SUB = 8


def pack_kernel(rows, depth, aerial, quench, cot, up, down, swap):
    core = lax.axis_index("ty")
    groups = depth // SUB
    area = depth * rows

    def put(dst, place, src, base, row):
        for k in range(groups):
            dst[place, k] = src[pl.ds(base + rows * k + row, SUB, stride=rows * groups), :]

    mine = core * area
    other = (1 - core) * area
    for dst, first in ((up, lambda width: rows - width), (down, lambda width: 0)):
        place = 0
        for src, base, width in (
            (cot, mine, HALO_COT),
            (aerial, 0, HALO_AERIAL),
            (quench, 0, HALO_QUENCH),
            (cot, other, HALO_COT),
        ):
            for i in range(width):
                put(dst, place, src, base, first(width) + i)
                place += 1
    for j, (src, base) in enumerate(((aerial, 0), (quench, 0), (cot, other))):
        for row in range(rows):
            put(swap, j * rows + row, src, base, row)


def main_kernel(rows, depth, doses, *refs):
    (levels, index, aerial, quench, cot, swap, before_own, after_own, before_par, after_par) = refs[:10]
    outs = refs[10 : 10 + 2 * doses]
    a0, q0, a1, q1, a2, q2, a3, ct, l3, l2, m2, l1, m1, full = refs[10 + 2 * doses :]
    core = lax.axis_index("ty")
    place = lax.axis_index("dose")
    groups = depth // SUB
    area = depth * rows
    count = 2 * groups
    lane = lax.broadcasted_iota(jnp.int32, (SUB, 128), 1)
    first_lane = lane == 0
    last_lane = lane == 127
    sub = lax.broadcasted_iota(jnp.int32, (SUB, 128), 0)
    first_sub = sub == 0
    last_sub = sub == SUB - 1
    dose = levels[index[core]]

    def source(raw, base, swap_at, halo_at_own, halo_at_par, width, row):
        if row < 0:
            own = [before_own[halo_at_own + width + row, k] for k in range(groups)]
            par = [before_par[halo_at_par + width + row, k] for k in range(groups)]
        elif row >= rows:
            own = [after_own[halo_at_own + row - rows, k] for k in range(groups)]
            par = [after_par[halo_at_par + row - rows, k] for k in range(groups)]
        else:
            own = [raw[pl.ds(base + rows * k + row, SUB, stride=rows * groups), :] for k in range(groups)]
            par = [swap[swap_at + row, k] for k in range(groups)]
        return own + par

    def load(ref, halo, row):
        return [ref[row + halo, i] for i in range(count)]

    def save(ref, halo, row, value):
        for i in range(count):
            ref[row + halo, i] = value[i]

    def sums(ref, halo, row, center):
        above = load(ref, halo, row - 1)
        below = load(ref, halo, row + 1)
        lateral, vertical = [], []
        for i in range(count):
            k = i % groups
            j = (i + groups) % count
            right = pltpu.roll(jnp.where(first_lane, center[j], center[i]), 127, 1)
            left = pltpu.roll(jnp.where(last_lane, center[j], center[i]), 1, 1)
            lateral.append((above[i] + below[i]) + (right + left))
            if k + 1 < groups:
                deeper = center[i + 1]
            else:
                deeper = jnp.where(last_sub, center[i], pltpu.roll(center[i - k], SUB - 1, 0))
            if k > 0:
                higher = center[i - 1]
            else:
                higher = jnp.where(first_sub, center[i], pltpu.roll(center[i + groups - 1], 1, 0))
            vertical.append(deeper + higher)
        return lateral, vertical

    def spread(ref, halo, row, center, along, depthwise):
        lateral, vertical = sums(ref, halo, row, center)
        keep = 1.0 - 4.0 * along - 2.0 * depthwise
        return [keep * c + along * s + depthwise * v for c, s, v in zip(center, lateral, vertical)]

    def left_over(value):
        return [1.0 - deprotect_rate * v for v in value]

    for row in range(-HALO_AERIAL, rows + HALO_AERIAL):
        light = source(aerial, 0, 0, HALO_COT, HALO_COT, HALO_AERIAL, row)
        save(a0, HALO_AERIAL, row, [1.0 - jnp.exp((-exposure_rate * dose) * v) for v in light])
    for row in range(-HALO_QUENCH, rows + HALO_QUENCH):
        at = HALO_COT + HALO_AERIAL
        save(q0, HALO_QUENCH, row, source(quench, 0, rows, at, at, HALO_QUENCH, row))
    for row in range(-HALO_COT, rows + HALO_COT):
        at = HALO_COT + HALO_AERIAL + HALO_QUENCH
        save(ct, HALO_COT, row, source(cot, core * area, 2 * rows, 0, at, HALO_COT, row))

    def forward(a_old, a_halo, q_old, q_halo, a_new, q_new):
        for row in range(1 - a_halo, rows + a_halo - 1):
            a_now = load(a_old, a_halo, row)
            q_now = load(q_old, q_halo, row)
            reaction = [neutral_rate * a * q for a, q in zip(a_now, q_now)]
            a_next = spread(a_old, a_halo, row, a_now, acid_lateral, acid_depth)
            save(a_new, a_halo - 1, row, [v - r for v, r in zip(a_next, reaction)])
            if q_new is not None and 1 - q_halo <= row < rows + q_halo - 1:
                q_next = spread(q_old, q_halo, row, q_now, base_lateral, base_depth)
                save(q_new, q_halo - 1, row, [v - r for v, r in zip(q_next, reaction)])

    forward(a0, 5, q0, 4, a1, q1)
    forward(a1, 4, q1, 3, a2, q2)
    forward(a2, 3, q2, 2, a3, None)

    def source_term(row, ones):
        value = [(-deprotect_rate) * v for v in load(ct, 3, row)]
        for ref, halo in ones:
            value = [v * m for v, m in zip(value, left_over(load(ref, halo, row)))]
        return value

    for row in range(-3, rows + 3):
        save(l3, 3, row, source_term(row, ((a0, 5), (a1, 4), (a2, 3))))
    for row in range(-2, rows + 2):
        l_old = load(l3, 3, row)
        term = source_term(row, ((a0, 5), (a1, 4), (a3, 2)))
        q_old = load(q2, 2, row)
        l_next = spread(l3, 3, row, l_old, acid_lateral, acid_depth)
        save(l2, 2, row, [v - neutral_rate * q * s + t for v, q, s, t in zip(l_next, q_old, l_old, term)])
        if -1 <= row < rows + 1:
            save(m2, 1, row, [-neutral_rate * a * s for a, s in zip(load(a2, 3, row), l_old)])
    for row in range(-1, rows + 1):
        l_old = load(l2, 2, row)
        m_old = load(m2, 1, row)
        both = [neutral_rate * (a + b) for a, b in zip(l_old, m_old)]
        term = source_term(row, ((a0, 5), (a2, 3), (a3, 2)))
        l_next = spread(l2, 2, row, l_old, acid_lateral, acid_depth)
        save(l1, 1, row, [v - q * s + t for v, q, s, t in zip(l_next, load(q1, 3, row), both, term)])
        if 0 <= row < rows:
            m_next = spread(m2, 1, row, m_old, base_lateral, base_depth)
            save(m1, 0, row, [v - a * s for v, a, s in zip(m_next, load(a1, 4, row), both)])
    for row in range(rows):
        l_old = load(l1, 1, row)
        both = [neutral_rate * (a + b) for a, b in zip(l_old, load(m1, 0, row))]
        term = source_term(row, ((a1, 4), (a2, 3), (a3, 2)))
        l_next = spread(l1, 1, row, l_old, acid_lateral, acid_depth)
        absorbed = [1.0 - a for a in load(a0, 5, row)]
        for i in range(count):
            value = l_next[i] - load(q0, 4, row)[i] * both[i] + term[i]
            value = value * ((exposure_rate * dose) * absorbed[i])
            half, k = divmod(i, groups)
            full[pl.ds(half * area + rows * k + row, SUB, stride=rows * groups), :] = value

    piece = area // doses
    for half in range(2):
        for k in range(doses):
            owner = lax.rem(place + k, doses)
            start = pl.multiple_of(half * area + owner * piece, SUB)
            outs[half * doses + k][...] = full[pl.ds(start, piece), :]


def on_device(aerial_image, quencher, cotangent, dose_levels, dose_index):
    depth, rows, lanes = aerial_image.shape
    groups = depth // SUB
    doses = lax.axis_size("dose")
    ring = lax.axis_size("tx")
    f32 = jnp.float32
    aerial = aerial_image.reshape(depth * rows, lanes)
    quench = quencher.reshape(depth * rows, lanes)
    cot = cotangent.reshape(2 * depth * rows, lanes)
    vmem = pl.BlockSpec(memory_space=pltpu.VMEM)
    smem = pl.BlockSpec(memory_space=pltpu.SMEM)

    def kernel_pack(*refs):
        pack_kernel(rows, depth, *refs)

    def field(n, parts=1):
        return jax.ShapeDtypeStruct((n, groups * parts, SUB, lanes), f32)

    up, down, swap = pl.pallas_call(
        kernel_pack,
        out_shape=(field(HALO_ROWS), field(HALO_ROWS), field(3 * rows)),
        in_specs=[vmem] * 3,
        out_specs=(vmem,) * 3,
    )(aerial, quench, cot)

    ahead = [(i, (i + 1) % ring) for i in range(ring)]
    back = [(j, i) for i, j in ahead]
    across = [(0, 1), (1, 0)]
    before_own = lax.ppermute(up, "tx", ahead)
    after_own = lax.ppermute(down, "tx", back)
    swapped = lax.ppermute(swap, "ty", across)
    before_par = lax.ppermute(before_own, "ty", across)
    after_par = lax.ppermute(after_own, "ty", across)

    def kernel_main(*refs):
        main_kernel(rows, depth, doses, *refs)

    def scratch(halo):
        return pltpu.VMEM((rows + 2 * halo, 2 * groups, SUB, lanes), f32)

    piece = depth * rows // doses
    parts = pl.pallas_call(
        kernel_main,
        out_shape=(jax.ShapeDtypeStruct((piece, lanes), f32),) * (2 * doses),
        in_specs=[smem] * 2 + [vmem] * 8,
        out_specs=(vmem,) * (2 * doses),
        scratch_shapes=[scratch(h) for h in (5, 4, 4, 3, 3, 2, 2, 3, 3, 2, 1, 1, 0)]
        + [pltpu.VMEM((2 * depth * rows, lanes), f32)],
    )(dose_levels, dose_index, aerial, quench, cot, swapped, before_own, after_own, before_par, after_par)

    total = parts[0]
    for half in range(2):
        for k in range(doses):
            if half or k:
                pairs = [(c * doses + d, (c ^ half) * doses + (d + k) % doses) for d in range(doses) for c in range(2)]
                total = total + lax.ppermute(parts[half * doses + k], ("ty", "dose"), pairs)
    return total.reshape(depth // doses, rows, lanes)


def solution(mesh):
    placed = (
        P("focus", "tx", "ty"),
        P(None, "tx", "ty"),
        P(("focus", "dose"), None, "tx", "ty"),
        P(),
        P(("focus", "dose")),
    )
    return jax.shard_map(
        on_device,
        mesh=mesh,
        in_specs=placed,
        out_specs=P(("focus", "dose"), "tx", "ty"),
        check_vma=False,
    )
```

```python
import jax
import jax.numpy as jnp
from jax import lax
from jax.experimental import pallas as pl
from jax.experimental.pallas import tpu as pltpu
from jax.sharding import PartitionSpec as P

exposure_rate = 1.0
neutral_rate = 0.8
deprotect_rate = 0.5
acid_lateral = 0.23
acid_depth = 0.02
base_lateral = 0.2
base_depth = 0.02

HALO_AERIAL = 5
HALO_QUENCH = 4
HALO_COT = 3
SUB = 8
LIMIT = 20 << 20


def chip_row(rows, row):
    return row + lax.axis_index("ty") * (rows - 1 - 2 * row)


def vector(ref, rows, groups, k, row, base=0):
    return ref[pl.ds(base + rows * k + row, SUB, stride=rows * groups), :]


def pack_image_kernel(rows, groups, aerial, quench, straight, crossed):
    place = 0
    for src, width in ((aerial, HALO_AERIAL), (quench, HALO_QUENCH)):
        for i in range(width):
            for k in range(groups):
                straight[place, k] = vector(src, rows, groups, k, chip_row(rows, rows - width + i))
                crossed[place, k] = vector(src, rows, groups, k, chip_row(rows, width - 1 - i))
            place += 1


def pack_rest_kernel(rows, groups, local, aerial, quench, cot, straight, crossed, swap):
    area = rows * groups * SUB
    inner = rows // 2 + HALO_COT
    for d in range(local):
        for i in range(HALO_COT):
            for k in range(groups):
                place = d * HALO_COT + i
                straight[place, k] = vector(cot, rows, groups, k, chip_row(rows, rows - HALO_COT + i), d * area)
                crossed[place, k] = vector(cot, rows, groups, k, chip_row(rows, HALO_COT - 1 - i), d * area)
    place = 0
    parts = [(aerial, 0, rows), (quench, 0, rows)] + [(cot, d * area, inner) for d in range(local)]
    for src, base, width in parts:
        for i in range(width):
            for k in range(groups):
                swap[place, k] = vector(src, rows, groups, k, chip_row(rows, rows - 1 - i), base)
            place += 1


def load(ref, halo, row):
    return [ref[row + halo, i] for i in range(ref.shape[1])]


def save(ref, halo, row, value):
    for i in range(len(value)):
        ref[row + halo, i] = value[i]


def make_spread():
    lane = lax.broadcasted_iota(jnp.int32, (SUB, 128), 1)
    sub = lax.broadcasted_iota(jnp.int32, (SUB, 128), 0)
    first_lane = lane == 0
    last_lane = lane == 127
    first_sub = sub == 0
    last_sub = sub == SUB - 1

    def spread(ref, halo, row, center, along, depthwise):
        above = load(ref, halo, row - 1)
        below = load(ref, halo, row + 1)
        count = len(center)
        groups = count // 2
        keep = 1.0 - 4.0 * along - 2.0 * depthwise
        result = []
        for i in range(count):
            k = i % groups
            j = (i + groups) % count
            right = pltpu.roll(jnp.where(first_lane, center[j], center[i]), 127, 1)
            left = pltpu.roll(jnp.where(last_lane, center[j], center[i]), 1, 1)
            lateral = (above[i] + below[i]) + (right + left)
            if k + 1 < groups:
                deeper = center[i + 1]
            else:
                deeper = jnp.where(last_sub, center[i], pltpu.roll(center[i - k], SUB - 1, 0))
            if k > 0:
                higher = center[i - 1]
            else:
                higher = jnp.where(first_sub, center[i], pltpu.roll(center[i + groups - 1], 1, 0))
            result.append(keep * center[i] + along * lateral + depthwise * (deeper + higher))
        return result

    return spread


def history_rows(half):
    halos = {"c3": 3, "c2": 2, "c1": 1, "c0": 0, "q2": 2, "q1": 1, "q0": 0, "a2": 1, "a1": 0, "e": 0}
    places, total = {}, 0
    for name, halo in halos.items():
        places[name] = (halo, total)
        total += half + 2 * halo
    return places, total


def forward_kernel(rows, groups, local, levels, index, aerial, quench, swap, img_s, img_c, extra, hist, *scratch):
    a0, q0, a1, q1, a2, q2, a3 = scratch
    half = rows // 2
    places, total = history_rows(half)
    spread = make_spread()

    def source(raw, swap_at, halo_at, width, row):
        if row < 0:
            place = halo_at + width + row
            return [img_s[place, k] for k in range(groups)] + [img_c[place, k] for k in range(groups)]
        if row >= rows:
            return [extra[0, k] for k in range(groups)] + [extra[1, k] for k in range(groups)]
        own = [vector(raw, rows, groups, k, chip_row(rows, row)) for k in range(groups)]
        return own + [swap[swap_at + row, k] for k in range(groups)]

    for row in range(-HALO_QUENCH, half + HALO_QUENCH):
        save(q0, HALO_QUENCH, row, source(quench, rows, HALO_AERIAL, HALO_QUENCH, row))

    for d in range(local):
        dose = levels[index[d]]

        def keep(name, row, value):
            halo, place = places[name]
            save(hist, d * total + place + halo, row, value)

        for row in range(-HALO_AERIAL, half + HALO_AERIAL):
            light = source(aerial, 0, 0, HALO_AERIAL, row)
            absorbed = [jnp.exp((-exposure_rate * dose) * v) for v in light]
            save(a0, HALO_AERIAL, row, [1.0 - v for v in absorbed])
            if 0 <= row < half:
                keep("e", row, [(exposure_rate * dose) * v for v in absorbed])
                keep("q0", row, [neutral_rate * v for v in load(q0, HALO_QUENCH, row)])

        def forward(a_old, a_halo, q_old, q_halo, a_new, q_new):
            for row in range(1 - a_halo, half + a_halo - 1):
                a_now = load(a_old, a_halo, row)
                q_now = load(q_old, q_halo, row)
                reaction = [neutral_rate * a * q for a, q in zip(a_now, q_now)]
                a_next = spread(a_old, a_halo, row, a_now, acid_lateral, acid_depth)
                save(a_new, a_halo - 1, row, [v - r for v, r in zip(a_next, reaction)])
                if q_new is not None and 1 - q_halo <= row < half + q_halo - 1:
                    q_next = spread(q_old, q_halo, row, q_now, base_lateral, base_depth)
                    save(q_new, q_halo - 1, row, [v - r for v, r in zip(q_next, reaction)])

        forward(a0, 5, q0, 4, a1, q1)
        forward(a1, 4, q1, 3, a2, q2)
        forward(a2, 3, q2, 2, a3, None)

        for row in range(-3, half + 3):
            acids = {0: load(a0, 5, row), 1: load(a1, 4, row), 2: load(a2, 3, row)}
            if -2 <= row < half + 2:
                acids[3] = load(a3, 2, row)
            left = {n: [1.0 - deprotect_rate * v for v in value] for n, value in acids.items()}

            def times(*names):
                value = [(-deprotect_rate) * v for v in left[names[0]]]
                for n in names[1:]:
                    value = [v * m for v, m in zip(value, left[n])]
                return value

            keep("c3", row, times(0, 1, 2))
            if -2 <= row < half + 2:
                keep("c2", row, times(0, 1, 3))
                keep("q2", row, [neutral_rate * v for v in load(q2, 2, row)])
            if -1 <= row < half + 1:
                keep("c1", row, times(0, 2, 3))
                keep("q1", row, [neutral_rate * v for v in load(q1, 3, row)])
                keep("a2", row, [neutral_rate * v for v in acids[2]])
            if 0 <= row < half:
                keep("c0", row, times(1, 2, 3))
                keep("a1", row, [neutral_rate * v for v in acids[1]])


def backward_kernel(rows, groups, local, doses, hist, cot, swap, cot_s, cot_c, *refs):
    outs = refs[: 2 * doses]
    ct, l3, l2, m2, l1, m1, acc, full = refs[2 * doses :]
    half = rows // 2
    area = rows * groups * SUB
    depth = groups * SUB
    inner = half + HALO_COT
    place = lax.axis_index("dose")
    places, total = history_rows(half)
    spread = make_spread()

    for d in range(local):

        def past(name, row):
            halo, at = places[name]
            return load(hist, d * total + at + halo, row)

        for row in range(-3, half + 3):
            if row < 0:
                at = d * HALO_COT + HALO_COT + row
                value = [cot_s[at, k] for k in range(groups)] + [cot_c[at, k] for k in range(groups)]
            else:
                value = [vector(cot, rows, groups, k, chip_row(rows, row), d * area) for k in range(groups)]
                value += [swap[2 * rows + d * inner + row, k] for k in range(groups)]
            save(ct, 3, row, value)
            save(l3, 3, row, [c * v for c, v in zip(past("c3", row), value)])

        for row in range(-2, half + 2):
            old = load(l3, 3, row)
            new = spread(l3, 3, row, old, acid_lateral, acid_depth)
            parts = zip(new, past("q2", row), old, past("c2", row), load(ct, 3, row))
            save(l2, 2, row, [v - q * s + c * t for v, q, s, c, t in parts])
            if -1 <= row < half + 1:
                save(m2, 1, row, [-(a * s) for a, s in zip(past("a2", row), old)])
        for row in range(-1, half + 1):
            old = load(l2, 2, row)
            base = load(m2, 1, row)
            both = [a + b for a, b in zip(old, base)]
            new = spread(l2, 2, row, old, acid_lateral, acid_depth)
            parts = zip(new, past("q1", row), both, past("c1", row), load(ct, 3, row))
            save(l1, 1, row, [v - q * s + c * t for v, q, s, c, t in parts])
            if 0 <= row < half:
                new = spread(m2, 1, row, base, base_lateral, base_depth)
                save(m1, 0, row, [v - a * s for v, a, s in zip(new, past("a1", row), both)])
        for row in range(half):
            old = load(l1, 1, row)
            both = [a + b for a, b in zip(old, load(m1, 0, row))]
            new = spread(l1, 1, row, old, acid_lateral, acid_depth)
            parts = zip(new, past("q0", row), both, past("c0", row), load(ct, 3, row), past("e", row))
            value = [(v - q * s + c * t) * e for v, q, s, c, t, e in parts]
            if d > 0:
                value = [v + w for v, w in zip(value, load(acc, 0, row))]
            if d + 1 < local:
                save(acc, 0, row, value)
            else:
                for i in range(2 * groups):
                    side, k = divmod(i, groups)
                    full[side, row, pl.ds(k, SUB, stride=groups), :] = value[i]

    piece = depth // doses
    for side in range(2):
        for k in range(doses):
            start = pl.multiple_of(lax.rem(place + k, doses) * piece, SUB)
            for row in range(half):
                outs[side * doses + k][row] = full[side, row, pl.ds(start, piece), :]


def join_kernel(rows, piece, doses, *refs):
    parts, out = refs[:-1], refs[-1]
    half = rows // 2
    core = lax.axis_index("ty")
    for side in range(2):
        for row in range(half):
            owner = core + side * (1 - 2 * core)
            at = row + owner * (rows - 1 - 2 * row)
            for g in range(piece // SUB):
                value = parts[side * doses][row, pl.ds(g * SUB, SUB), :]
                for k in range(1, doses):
                    value = value + parts[side * doses + k][row, pl.ds(g * SUB, SUB), :]
                out[pl.ds(g * SUB * rows + at, SUB, stride=rows), :] = value


def on_device(aerial_image, quencher, cotangent, dose_levels, dose_index):
    depth, rows, lanes = aerial_image.shape
    local = cotangent.shape[0]
    groups = depth // SUB
    half = rows // 2
    doses = lax.axis_size("dose")
    ring = lax.axis_size("tx")
    f32 = jnp.float32
    aerial = aerial_image.reshape(depth * rows, lanes)
    quench = quencher.reshape(depth * rows, lanes)
    cot = cotangent.reshape(local * depth * rows, lanes)
    vmem = pl.BlockSpec(memory_space=pltpu.VMEM)
    smem = pl.BlockSpec(memory_space=pltpu.SMEM)

    def call(kernel, fixed, args, outs, scratch=(), scalars=0, flops=0):
        def body(*refs):
            kernel(*fixed, *refs)

        moved = sum(4 * x.size for x in list(args) + list(outs))
        return pl.pallas_call(
            body,
            name=kernel.__name__,
            out_shape=tuple(outs),
            in_specs=[smem] * scalars + [vmem] * (len(args) - scalars),
            out_specs=(vmem,) * len(outs),
            scratch_shapes=list(scratch),
            compiler_params=pltpu.CompilerParams(vmem_limit_bytes=LIMIT),
            cost_estimate=pl.CostEstimate(flops=flops, bytes_accessed=moved, transcendentals=0),
        )(*args)

    def field(n, vectors=groups):
        return jax.ShapeDtypeStruct((n, vectors, SUB, lanes), f32)

    def scratch(halo):
        return pltpu.VMEM((half + 2 * halo, 2 * groups, SUB, lanes), f32)

    def device(t, c):
        return (t % ring) * 2 + c

    straight = [(device(t, c), device(t + 1 - 2 * c, c)) for t in range(ring) for c in range(2)]
    crossed = [(device(t, c), device(t - 1 + 2 * c, 1 - c)) for t in range(ring) for c in range(2)]
    across = [(0, 1), (1, 0)]

    def along(value, pairs):
        return lax.ppermute(value, ("tx", "ty"), pairs)

    n_image = HALO_AERIAL + HALO_QUENCH
    n_cot = local * HALO_COT
    n_swap = 2 * rows + local * (half + HALO_COT)
    send_s, send_c = call(pack_image_kernel, (rows, groups), (aerial, quench), (field(n_image), field(n_image)))
    img_s = along(send_s, straight)
    img_c = along(send_c, crossed)
    send_s, send_c, swap = call(
        pack_rest_kernel, (rows, groups, local), (aerial, quench, cot), (field(n_cot), field(n_cot), field(n_swap))
    )
    swap = lax.ppermute(swap, "ty", across)
    cot_s = along(send_s, straight)
    cot_c = along(send_c, crossed)
    last = HALO_AERIAL - 1
    extra = jnp.concatenate((img_c[last : last + 1], img_s[last : last + 1]), axis=0)
    extra = lax.ppermute(extra, "ty", across)

    places, total = history_rows(half)
    (hist,) = call(
        forward_kernel,
        (rows, groups, local),
        (dose_levels, dose_index, aerial, quench, swap, img_s, img_c, extra),
        (field(local * total, 2 * groups),),
        [scratch(h) for h in (5, 4, 4, 3, 3, 2, 2)],
        scalars=2,
        flops=20_000_000,
    )
    piece = depth // doses
    parts = call(
        backward_kernel,
        (rows, groups, local, doses),
        (hist, cot, swap, cot_s, cot_c),
        (jax.ShapeDtypeStruct((half, piece, lanes), f32),) * (2 * doses),
        [scratch(h) for h in (3, 3, 2, 1, 1, 0, 0)] + [pltpu.VMEM((2, half, depth, lanes), f32)],
        flops=10_000_000,
    )

    arrived = []
    for side in range(2):
        for k in range(doses):
            part = parts[side * doses + k]
            if side or k:
                pairs = [(c * doses + d, (c ^ side) * doses + (d + k) % doses) for d in range(doses) for c in range(2)]
                part = lax.ppermute(part, ("ty", "dose"), pairs)
            arrived.append(part)
    (out,) = call(join_kernel, (rows, piece, doses), arrived, (jax.ShapeDtypeStruct((piece * rows, lanes), f32),))
    return out.reshape(piece, rows, lanes)


def solution(mesh):
    placed = (
        P("focus", "tx", "ty"),
        P(None, "tx", "ty"),
        P(("focus", "dose"), None, "tx", "ty"),
        P(),
        P(("focus", "dose")),
    )
    return jax.shard_map(
        on_device,
        mesh=mesh,
        in_specs=placed,
        out_specs=P(("focus", "dose"), "tx", "ty"),
        check_vma=False,
    )
```

```python
import jax
import jax.numpy as jnp
from jax import lax
from jax.experimental import pallas as pl
from jax.experimental.pallas import tpu as pltpu
from jax.sharding import PartitionSpec as P


exposure_rate = 1.0
neutral_rate = 0.8
deprotect_rate = 0.5
acid_lateral = 0.23
acid_depth = 0.02
base_lateral = 0.2
base_depth = 0.02

HALO_AERIAL = 5
HALO_QUENCH = 4
HALO_COT = 3
SUB = 8
LIMIT = 20 << 20


def chip_row(rows, row):
    return row + lax.axis_index("ty") * (rows - 1 - 2 * row)


def vector(ref, rows, groups, k, row, base=0):
    return ref[pl.ds(base + rows * k + row, SUB, stride=rows * groups), :]


def pack_kernel(rows, groups, local, *refs):
    image_hbm, quench_hbm, cot_hbm = refs[:3]
    image_s, image_c, cot_s, cot_c, swap, aerial, quench, cot = refs[3:11]
    sems = refs[11]
    pairs = ((image_hbm, aerial), (quench_hbm, quench), (cot_hbm, cot))
    copies = [pltpu.make_async_copy(src, dst, sems.at[i]) for i, (src, dst) in enumerate(pairs)]
    for copy in copies:
        copy.start()
    area = rows * groups * SUB
    inner = rows // 2 + HALO_COT
    copies[0].wait()
    copies[1].wait()
    place = 0
    for src, width in ((aerial, HALO_AERIAL), (quench, HALO_QUENCH)):
        for i in range(width):
            for k in range(groups):
                image_s[place, k] = vector(src, rows, groups, k, chip_row(rows, rows - width + i))
                image_c[place, k] = vector(src, rows, groups, k, chip_row(rows, width - 1 - i))
            place += 1
    copies[2].wait()
    for d in range(local):
        for i in range(HALO_COT):
            for k in range(groups):
                place = d * HALO_COT + i
                cot_s[place, k] = vector(cot, rows, groups, k, chip_row(rows, rows - HALO_COT + i), d * area)
                cot_c[place, k] = vector(cot, rows, groups, k, chip_row(rows, HALO_COT - 1 - i), d * area)
    place = 0
    parts = [(aerial, 0, rows), (quench, 0, rows)] + [(cot, d * area, inner) for d in range(local)]
    for src, base, width in parts:
        for i in range(width):
            for k in range(groups):
                swap[place, k] = vector(src, rows, groups, k, chip_row(rows, rows - 1 - i), base)
            place += 1


def load(ref, halo, row):
    return [ref[row + halo, i] for i in range(ref.shape[1])]


def save(ref, halo, row, value):
    for i in range(len(value)):
        ref[row + halo, i] = value[i]


def make_spread():
    lane = lax.broadcasted_iota(jnp.int32, (SUB, 128), 1)
    sub = lax.broadcasted_iota(jnp.int32, (SUB, 128), 0)
    first_lane = lane == 0
    last_lane = lane == 127
    first_sub = sub == 0
    last_sub = sub == SUB - 1

    def spread(above, center, below, along, depthwise):
        count = len(center)
        groups = count // 2
        keep = 1.0 - 4.0 * along - 2.0 * depthwise
        result = []
        for i in range(count):
            k = i % groups
            j = (i + groups) % count
            right = pltpu.roll(jnp.where(first_lane, center[j], center[i]), 127, 1)
            left = pltpu.roll(jnp.where(last_lane, center[j], center[i]), 1, 1)
            lateral = (above[i] + below[i]) + (right + left)
            if k + 1 < groups:
                deeper = center[i + 1]
            else:
                deeper = jnp.where(last_sub, center[i], pltpu.roll(center[i - k], SUB - 1, 0))
            if k > 0:
                higher = center[i - 1]
            else:
                higher = jnp.where(first_sub, center[i], pltpu.roll(center[i + groups - 1], 1, 0))
            result.append(keep * center[i] + along * lateral + depthwise * (deeper + higher))
        return result

    return spread


def near_rows(rows):
    half = rows // 2
    return {
        "q0": (0, rows),
        "a0": (0, rows),
        "a1": (1, rows - 1),
        "a2": (2, rows - 2),
        "a3": (3, rows - 3),
        "q1": (1, rows - 1),
        "q2": (2, rows - 2),
        "c3": (2, half + 3),
        "c2": (3, half + 2),
        "c1": (3, half + 1),
        "c0": (3, half),
        "e": (0, half),
        "dose": (0, 1),
    }


def far_rows():
    return {
        "q0": (-4, 0),
        "a0": (-5, 0),
        "a1": (-4, 1),
        "a2": (-3, 2),
        "a3": (-2, 3),
        "q1": (-3, 1),
        "q2": (-2, 2),
        "c3": (-3, 2),
        "c2": (-2, 3),
        "c1": (-1, 3),
        "c0": (0, 3),
    }


def places_of(table, local):
    places, total = {}, 0
    for name, (first, end) in table.items():
        for d in range(local):
            for row in range(first, end):
                if name == "q0" and d > 0:
                    places[name, d, row] = places[name, 0, row]
                else:
                    places[name, d, row] = total
                    total += 1
    return places, total


class Fields:
    def __init__(self, rows, local, near, far=None, more=None):
        self.stores = [(near, places_of(near_rows(rows), local)[0])]
        if far is not None:
            self.stores.append((far, places_of(far_rows(), local)[0]))
        self.more = {} if more is None else more

    def get(self, name, d, row):
        if (name, d, row) in self.more:
            return self.more[name, d, row]
        for ref, places in self.stores:
            if (name, d, row) in places:
                at = places[name, d, row]
                return [ref[at, i] for i in range(ref.shape[1])]
        raise KeyError((name, row))

    def put(self, name, d, row, value):
        ref, places = self.stores[-1]
        at = places[name, d, row]
        for i in range(len(value)):
            ref[at, i] = value[i]


def left_of(acid):
    return [1.0 - deprotect_rate * v for v in acid]


def next_acid(spread, fields, d, n, row):
    name = "a%d" % n
    above, center, below = (fields.get(name, d, row + i) for i in (-1, 0, 1))
    quench = fields.get("q%d" % n, d, row)
    new = spread(above, center, below, acid_lateral, acid_depth)
    reaction = [neutral_rate * a * q for a, q in zip(center, quench)]
    return [v - r for v, r in zip(new, reaction)], reaction


def forward_rows(spread, fields, d, table):
    for n in range(3):
        first, end = table["a%d" % (n + 1)]
        for row in range(first, end):
            new, reaction = next_acid(spread, fields, d, n, row)
            fields.put("a%d" % (n + 1), d, row, new)
            if n < 2:
                q_first, q_end = table["q%d" % (n + 1)]
                if q_first <= row < q_end:
                    name = "q%d" % n
                    above, center, below = (fields.get(name, d, row + i) for i in (-1, 0, 1))
                    new = spread(above, center, below, base_lateral, base_depth)
                    fields.put("q%d" % (n + 1), d, row, [v - r for v, r in zip(new, reaction)])

    first = min(table[c][0] for c in ("c3", "c2", "c1", "c0"))
    end = max(table[c][1] for c in ("c3", "c2", "c1", "c0"))
    for row in range(first, end):
        wanted = [n for n in range(4) if table["c%d" % n][0] <= row < table["c%d" % n][1]]
        left = {}

        def of(n):
            if n not in left:
                left[n] = left_of(fields.get("a%d" % n, d, row))
            return left[n]

        for n in wanted:
            parts = [m for m in range(4) if m != n]
            if n >= 2 and table["e"][1] > 0 and row == table["c%d" % n][1] - 1:
                parts = parts[:2]
            value = [(-deprotect_rate) * v for v in of(parts[0])]
            for m in parts[1:]:
                value = [v * w for v, w in zip(value, of(m))]
            fields.put("c%d" % n, d, row, value)


def near_kernel(rows, groups, local, levels, index, aerial, quench, swap, near):
    half = rows // 2
    spread = make_spread()
    fields = Fields(rows, local, near)

    def source(raw, at, row):
        own = [vector(raw, rows, groups, k, chip_row(rows, row)) for k in range(groups)]
        return own + [swap[at + row, k] for k in range(groups)]

    for row in range(rows):
        fields.put("q0", 0, row, source(quench, rows, row))
    for d in range(local):
        dose = jnp.full((SUB, near.shape[3]), levels[index[d]], jnp.float32)
        fields.put("dose", d, 0, [dose] * (2 * groups))
        rate = -exposure_rate * dose
        for row in range(rows):
            absorbed = [jnp.exp(rate * v) for v in source(aerial, 0, row)]
            fields.put("a0", d, row, [1.0 - v for v in absorbed])
            if row < half:
                fields.put("e", d, row, [exposure_rate * dose * v for v in absorbed])
        forward_rows(spread, fields, d, near_rows(rows))


def far_kernel(rows, groups, local, near, image_s, image_c, far):
    spread = make_spread()
    fields = Fields(rows, local, near, far)
    table = dict(far_rows(), e=(0, 0))

    def source(at, row):
        return [image_s[at + row, k] for k in range(groups)] + [image_c[at + row, k] for k in range(groups)]

    for row in range(-HALO_QUENCH, 0):
        fields.put("q0", 0, row, source(HALO_AERIAL + HALO_QUENCH, row))
    for d in range(local):
        rate = -exposure_rate * fields.get("dose", d, 0)[0]
        for row in range(-HALO_AERIAL, 0):
            fields.put("a0", d, row, [1.0 - jnp.exp(rate * v) for v in source(HALO_AERIAL, row)])
        forward_rows(spread, fields, d, table)


def backward_kernel(rows, groups, local, doses, near, far, extra, cot, swap, cot_s, cot_c, *refs):
    outs = refs[: 2 * doses]
    ct, l3, l2, m2, l1, m1, acc, full = refs[2 * doses :]
    half = rows // 2
    area = rows * groups * SUB
    depth = groups * SUB
    inner = half + HALO_COT
    place = lax.axis_index("dose")
    spread = make_spread()

    def around(ref, halo, row):
        return [load(ref, halo, row + i) for i in (-1, 0, 1)]

    for d in range(local):
        more = {}
        fields = Fields(rows, local, near, far, more)
        rate = -exposure_rate * fields.get("dose", d, 0)[0]
        light = [extra[side, k] for side in range(2) for k in range(groups)]
        more["a0", d, rows] = [1.0 - jnp.exp(rate * v) for v in light]
        for n in range(3):
            row = rows - 1 - n
            more["a%d" % (n + 1), d, row] = next_acid(spread, fields, d, n, row)[0]
        for n, row in ((3, half + 2), (2, half + 1)):
            left = left_of(fields.get("a%d" % (5 - n), d, row))
            more["c%d" % n, d, row] = [v * m for v, m in zip(fields.get("c%d" % n, d, row), left)]

        for row in range(-3, half + 3):
            if row < 0:
                at = d * HALO_COT + HALO_COT + row
                value = [cot_s[at, k] for k in range(groups)] + [cot_c[at, k] for k in range(groups)]
            else:
                value = [vector(cot, rows, groups, k, chip_row(rows, row), d * area) for k in range(groups)]
                value += [swap[2 * rows + d * inner + row, k] for k in range(groups)]
            save(ct, 3, row, value)
            save(l3, 3, row, [c * v for c, v in zip(fields.get("c3", d, row), value)])

        def step(ref, halo, row, both, n):
            above, center, below = around(ref, halo, row)
            new = spread(above, center, below, acid_lateral, acid_depth)
            parts = zip(new, fields.get("q%d" % n, d, row), both, fields.get("c%d" % n, d, row), load(ct, 3, row))
            return [v - q * (neutral_rate * s) + c * t for v, q, s, c, t in parts]

        for row in range(-2, half + 2):
            old = load(l3, 3, row)
            save(l2, 2, row, step(l3, 3, row, old, 2))
            if -1 <= row < half + 1:
                save(m2, 1, row, [-(neutral_rate * a * s) for a, s in zip(fields.get("a2", d, row), old)])
        for row in range(-1, half + 1):
            both = [a + b for a, b in zip(load(l2, 2, row), load(m2, 1, row))]
            save(l1, 1, row, step(l2, 2, row, both, 1))
            if 0 <= row < half:
                new = spread(*around(m2, 1, row), base_lateral, base_depth)
                parts = zip(new, fields.get("a1", d, row), both)
                save(m1, 0, row, [v - a * (neutral_rate * s) for v, a, s in parts])
        for row in range(half):
            both = [a + b for a, b in zip(load(l1, 1, row), load(m1, 0, row))]
            value = [v * e for v, e in zip(step(l1, 1, row, both, 0), fields.get("e", d, row))]
            if d > 0:
                value = [v + w for v, w in zip(value, load(acc, 0, row))]
            if d + 1 < local:
                save(acc, 0, row, value)
            else:
                for i in range(2 * groups):
                    side, k = divmod(i, groups)
                    full[side, row, pl.ds(k, SUB, stride=groups), :] = value[i]

    piece = depth // doses
    for side in range(2):
        for k in range(doses):
            start = pl.multiple_of(lax.rem(place + k, doses) * piece, SUB)
            for row in range(half):
                outs[side * doses + k][row] = full[side, row, pl.ds(start, piece), :]


def join_kernel(rows, piece, doses, *refs):
    parts, out = refs[:-1], refs[-1]
    half = rows // 2
    core = lax.axis_index("ty")
    for side in range(2):
        for row in range(half):
            owner = core + side * (1 - 2 * core)
            at = row + owner * (rows - 1 - 2 * row)
            for g in range(piece // SUB):
                value = parts[side * doses][row, pl.ds(g * SUB, SUB), :]
                for k in range(1, doses):
                    value = value + parts[side * doses + k][row, pl.ds(g * SUB, SUB), :]
                out[pl.ds(g * SUB * rows + at, SUB, stride=rows), :] = value


def gradient(aerial_image, quencher, cotangent, dose_levels, dose_index):
    depth, rows, lanes = aerial_image.shape
    local = cotangent.shape[0]
    groups = depth // SUB
    half = rows // 2
    doses = lax.axis_size("dose")
    ring = lax.axis_size("tx")
    assert rows == half + HALO_QUENCH and HALO_AERIAL == HALO_QUENCH + 1
    f32 = jnp.float32
    aerial = aerial_image.reshape(depth * rows, lanes)
    quench = quencher.reshape(depth * rows, lanes)
    cot = cotangent.reshape(local * depth * rows, lanes)
    vmem = pl.BlockSpec(memory_space=pltpu.VMEM)
    smem = pl.BlockSpec(memory_space=pltpu.SMEM)

    def call(kernel, fixed, args, outs, scratch=(), scalars=0, flops=0, space=pltpu.VMEM):
        def body(*refs):
            kernel(*fixed, *refs)

        moved = sum(4 * x.size for x in list(args) + list(outs))
        return pl.pallas_call(
            body,
            out_shape=tuple(outs),
            in_specs=[smem] * scalars + [pl.BlockSpec(memory_space=space)] * (len(args) - scalars),
            out_specs=(vmem,) * len(outs),
            scratch_shapes=list(scratch),
            compiler_params=pltpu.CompilerParams(vmem_limit_bytes=LIMIT),
            cost_estimate=pl.CostEstimate(flops=flops, bytes_accessed=moved, transcendentals=0),
        )(*args)

    def field(n, vectors=groups):
        return jax.ShapeDtypeStruct((n, vectors, SUB, lanes), f32)

    def scratch(halo):
        return pltpu.VMEM((half + 2 * halo, 2 * groups, SUB, lanes), f32)

    def device(t, c):
        return (t % ring) * 2 + c

    straight = [(device(t, c), device(t + 1 - 2 * c, c)) for t in range(ring) for c in range(2)]
    crossed = [(device(t, c), device(t - 1 + 2 * c, 1 - c)) for t in range(ring) for c in range(2)]
    across = [(0, 1), (1, 0)]

    def along(value, pairs):
        return lax.ppermute(value, ("tx", "ty"), pairs)

    n_image = HALO_AERIAL + HALO_QUENCH
    n_cot = local * HALO_COT
    n_swap = 2 * rows + local * (half + HALO_COT)
    flat = [jax.ShapeDtypeStruct(x.shape, f32) for x in (aerial, quench, cot)]
    sends = [field(n) for n in (n_image, n_image, n_cot, n_cot, n_swap)]
    image_s, image_c, cot_s, cot_c, swap, aerial, quench, cot = call(
        pack_kernel,
        (rows, groups, local),
        [pltpu.with_memory_space_constraint(x, pltpu.HBM) for x in (aerial, quench, cot)],
        sends + flat,
        [pltpu.SemaphoreType.DMA((3,))],
        space=pltpu.HBM,
    )
    image_s = along(image_s, straight)
    image_c = along(image_c, crossed)
    swap = lax.ppermute(swap, "ty", across)
    cot_s = along(cot_s, straight)
    cot_c = along(cot_c, crossed)

    (near,) = call(
        near_kernel,
        (rows, groups, local),
        (dose_levels, dose_index, aerial, quench, swap),
        (field(places_of(near_rows(rows), local)[1], 2 * groups),),
        scalars=2,
        flops=10_000_000,
    )
    last = HALO_AERIAL - 1
    extra = jnp.concatenate((image_c[last : last + 1], image_s[last : last + 1]), axis=0)
    extra = lax.ppermute(extra, "ty", across)
    (far,) = call(
        far_kernel,
        (rows, groups, local),
        (near, image_s, image_c),
        (field(places_of(far_rows(), local)[1], 2 * groups),),
        flops=10_000_000,
    )
    piece = depth // doses
    parts = call(
        backward_kernel,
        (rows, groups, local, doses),
        (near, far, extra, cot, swap, cot_s, cot_c),
        (jax.ShapeDtypeStruct((half, piece, lanes), f32),) * (2 * doses),
        [scratch(h) for h in (3, 3, 2, 1, 1, 0, 0)] + [pltpu.VMEM((2, half, depth, lanes), f32)],
        flops=10_000_000,
    )

    arrived = []
    for side in range(2):
        for k in range(doses):
            part = parts[side * doses + k]
            if side or k:
                pairs = [(c * doses + d, (c ^ side) * doses + (d + k) % doses) for d in range(doses) for c in range(2)]
                part = lax.ppermute(part, ("ty", "dose"), pairs)
            arrived.append(part)
    (out,) = call(join_kernel, (rows, piece, doses), arrived, (jax.ShapeDtypeStruct((piece * rows, lanes), f32),))
    return out.reshape(piece, rows, lanes)


def solution(mesh):
    placed = (
        P("focus", "tx", "ty"),
        P(None, "tx", "ty"),
        P(("focus", "dose"), None, "tx", "ty"),
        P(),
        P(("focus", "dose")),
    )
    return jax.shard_map(
        gradient,
        mesh=mesh,
        in_specs=placed,
        out_specs=P(("focus", "dose"), "tx", "ty"),
        check_vma=False,
    )
```

```python
import jax
import jax.numpy as jnp
from jax import lax
from jax.experimental import pallas as pl
from jax.experimental.pallas import tpu as pltpu
from jax.sharding import PartitionSpec as P


exposure_rate = 1.0
neutral_rate = 0.8
deprotect_rate = 0.5
acid_lateral = 0.23
acid_depth = 0.02
base_lateral = 0.2
base_depth = 0.02

HALO_AERIAL = 5
HALO_QUENCH = 4
HALO_COT = 3
SUB = 8
LIMIT = 20 << 20


def chip_row(rows, row):
    return row + lax.axis_index("ty") * (rows - 1 - 2 * row)


def vector(ref, rows, groups, k, row, base=0):
    return ref[pl.ds(base + rows * k + row, SUB, stride=rows * groups), :]


def image_kernel(rows, groups, image_hbm, quench_hbm, cot_hbm, image_s, image_c, aerial, quench, cot, sems):
    pairs = ((image_hbm, aerial), (quench_hbm, quench), (cot_hbm, cot))
    copies = [pltpu.make_async_copy(src, dst, sems.at[i]) for i, (src, dst) in enumerate(pairs)]
    for copy in copies:
        copy.start()
    copies[0].wait()
    copies[1].wait()
    place = 0
    for src, width in ((aerial, HALO_AERIAL), (quench, HALO_QUENCH)):
        for i in range(width):
            for k in range(groups):
                image_s[place, k] = vector(src, rows, groups, k, chip_row(rows, rows - width + i))
                image_c[place, k] = vector(src, rows, groups, k, chip_row(rows, width - 1 - i))
            place += 1
    copies[2].wait()


def rest_kernel(rows, groups, local, aerial, quench, cot, cot_s, cot_c, swap):
    area = rows * groups * SUB
    inner = rows // 2 + HALO_COT
    for d in range(local):
        for i in range(HALO_COT):
            for k in range(groups):
                place = d * HALO_COT + i
                cot_s[place, k] = vector(cot, rows, groups, k, chip_row(rows, rows - HALO_COT + i), d * area)
                cot_c[place, k] = vector(cot, rows, groups, k, chip_row(rows, HALO_COT - 1 - i), d * area)
    place = 0
    parts = [(aerial, 0, rows), (quench, 0, rows)] + [(cot, d * area, inner) for d in range(local)]
    for src, base, width in parts:
        for i in range(width):
            for k in range(groups):
                swap[place, k] = vector(src, rows, groups, k, chip_row(rows, rows - 1 - i), base)
            place += 1


def make_spread():
    lane = lax.broadcasted_iota(jnp.int32, (SUB, 128), 1)
    sub = lax.broadcasted_iota(jnp.int32, (SUB, 128), 0)
    first_lane = lane == 0
    last_lane = lane == 127
    first_sub = sub == 0
    last_sub = sub == SUB - 1

    def spread(above, center, below, along, depthwise):
        count = len(center)
        groups = count // 2
        keep = 1.0 - 4.0 * along - 2.0 * depthwise
        result = []
        for i in range(count):
            k = i % groups
            j = (i + groups) % count
            right = pltpu.roll(jnp.where(first_lane, center[j], center[i]), 127, 1)
            left = pltpu.roll(jnp.where(last_lane, center[j], center[i]), 1, 1)
            lateral = (above[i] + below[i]) + (right + left)
            if k + 1 < groups:
                deeper = center[i + 1]
            else:
                deeper = jnp.where(last_sub, center[i], pltpu.roll(center[i - k], SUB - 1, 0))
            if k > 0:
                higher = center[i - 1]
            else:
                higher = jnp.where(first_sub, center[i], pltpu.roll(center[i + groups - 1], 1, 0))
            result.append(keep * center[i] + along * lateral + depthwise * (deeper + higher))
        return result

    return spread


def near_rows(rows):
    half = rows // 2
    return {
        "q0": (0, rows),
        "a0": (0, rows),
        "a1": (1, rows - 1),
        "a2": (2, rows - 2),
        "a3": (3, rows - 3),
        "q1": (1, rows - 1),
        "q2": (2, rows - 2),
        "c3": (2, half + 3),
        "c2": (3, half + 2),
        "c1": (3, half + 1),
        "c0": (3, half),
        "e": (0, half),
        "dose": (0, 1),
    }


def far_rows(rows):
    return {
        "q0": (-4, 0),
        "a0": (-5, 0),
        "a1": (-4, 1),
        "a2": (-3, 2),
        "a3": (-2, 3),
        "q1": (-3, 1),
        "q2": (-2, 2),
        "c3": (-3, 2),
        "c2": (-2, 3),
        "c1": (-1, 3),
        "c0": (0, 3),
    }


def places_of(table, local):
    places, total = {}, 0
    for name, (first, end) in table.items():
        for d in range(local):
            for row in range(first, end):
                if name == "q0" and d > 0:
                    places[name, d, row] = places[name, 0, row]
                else:
                    places[name, d, row] = total
                    total += 1
    return places, total


def back_near_rows(rows):
    half = rows // 2
    return {
        "ct": (0, half + 3),
        "l3": (0, half + 3),
        "l2": (1, half + 2),
        "m2": (0, half + 1),
        "l1": (2, half + 1),
        "m1": (1, half),
        "g": (3, half),
    }


def back_far_rows(rows):
    return {
        "ct": (-3, 0),
        "l3": (-3, 0),
        "l2": (-2, 1),
        "m2": (-1, 0),
        "l1": (-1, 2),
        "m1": (0, 1),
        "g": (0, 3),
    }


class Fields:
    def __init__(self, rows, local, *stores):
        self.stores = [(ref, places_of(table(rows), local)[0]) for ref, table in stores]
        self.more = {}

    def get(self, name, d, row):
        if (name, d, row) in self.more:
            return self.more[name, d, row]
        for ref, places in self.stores:
            if (name, d, row) in places:
                at = places[name, d, row]
                return [ref[at, i] for i in range(ref.shape[1])]
        raise KeyError((name, row))

    def around(self, name, d, row):
        return [self.get(name, d, row + i) for i in (-1, 0, 1)]

    def put(self, name, d, row, value):
        ref, places = self.stores[-1]
        at = places[name, d, row]
        for i in range(len(value)):
            ref[at, i] = value[i]


def left_of(acid):
    return [1.0 - deprotect_rate * v for v in acid]


def next_acid(spread, fields, d, n, row):
    name = "a%d" % n
    above, center, below = fields.around(name, d, row)
    quench = fields.get("q%d" % n, d, row)
    new = spread(above, center, below, acid_lateral, acid_depth)
    reaction = [neutral_rate * a * q for a, q in zip(center, quench)]
    return [v - r for v, r in zip(new, reaction)], reaction


def forward_rows(spread, fields, d, table):
    for n in range(3):
        first, end = table["a%d" % (n + 1)]
        for row in range(first, end):
            new, reaction = next_acid(spread, fields, d, n, row)
            fields.put("a%d" % (n + 1), d, row, new)
            if n < 2:
                q_first, q_end = table["q%d" % (n + 1)]
                if q_first <= row < q_end:
                    name = "q%d" % n
                    new = spread(*fields.around(name, d, row), base_lateral, base_depth)
                    fields.put("q%d" % (n + 1), d, row, [v - r for v, r in zip(new, reaction)])

    first = min(table[c][0] for c in ("c3", "c2", "c1", "c0"))
    end = max(table[c][1] for c in ("c3", "c2", "c1", "c0"))
    for row in range(first, end):
        wanted = [n for n in range(4) if table["c%d" % n][0] <= row < table["c%d" % n][1]]
        left = {}

        def of(n):
            if n not in left:
                left[n] = left_of(fields.get("a%d" % n, d, row))
            return left[n]

        for n in wanted:
            parts = [m for m in range(4) if m != n]
            if n >= 2 and table["e"][1] > 0 and row == table["c%d" % n][1] - 1:
                parts = parts[:2]
            value = [(-deprotect_rate) * v for v in of(parts[0])]
            for m in parts[1:]:
                value = [v * w for v, w in zip(value, of(m))]
            fields.put("c%d" % n, d, row, value)


def near_kernel(rows, groups, local, levels, index, aerial, quench, swap, near):
    half = rows // 2
    spread = make_spread()
    fields = Fields(rows, local, (near, near_rows))

    def source(raw, at, row):
        own = [vector(raw, rows, groups, k, chip_row(rows, row)) for k in range(groups)]
        return own + [swap[at + row, k] for k in range(groups)]

    for row in range(rows):
        fields.put("q0", 0, row, source(quench, rows, row))
    for d in range(local):
        dose = jnp.full((SUB, near.shape[3]), levels[index[d]], jnp.float32)
        fields.put("dose", d, 0, [dose] * (2 * groups))
        rate = -exposure_rate * dose
        for row in range(rows):
            absorbed = [jnp.exp(rate * v) for v in source(aerial, 0, row)]
            fields.put("a0", d, row, [1.0 - v for v in absorbed])
            if row < half:
                fields.put("e", d, row, [exposure_rate * dose * v for v in absorbed])
        forward_rows(spread, fields, d, near_rows(rows))


def far_kernel(rows, groups, local, near, image_s, image_c, far):
    spread = make_spread()
    fields = Fields(rows, local, (near, near_rows), (far, far_rows))
    table = dict(far_rows(rows), e=(0, 0))

    def source(at, row):
        return [image_s[at + row, k] for k in range(groups)] + [image_c[at + row, k] for k in range(groups)]

    for row in range(-HALO_QUENCH, 0):
        fields.put("q0", 0, row, source(HALO_AERIAL + HALO_QUENCH, row))
    for d in range(local):
        rate = -exposure_rate * fields.get("dose", d, 0)[0]
        for row in range(-HALO_AERIAL, 0):
            fields.put("a0", d, row, [1.0 - jnp.exp(rate * v) for v in source(HALO_AERIAL, row)])
        forward_rows(spread, fields, d, table)


def backward_rows(spread, past, back, d, table):
    def step(name, row, both, n):
        new = spread(*back.around(name, d, row), acid_lateral, acid_depth)
        parts = zip(new, past.get("q%d" % n, d, row), both, past.get("c%d" % n, d, row), back.get("ct", d, row))
        return [v - q * (neutral_rate * s) + c * t for v, q, s, c, t in parts]

    for row in range(*table["l3"]):
        back.put("l3", d, row, [c * v for c, v in zip(past.get("c3", d, row), back.get("ct", d, row))])
    for row in range(*table["m2"]):
        parts = zip(past.get("a2", d, row), back.get("l3", d, row))
        back.put("m2", d, row, [-(neutral_rate * a * s) for a, s in parts])
    for row in range(*table["l2"]):
        back.put("l2", d, row, step("l3", row, back.get("l3", d, row), 2))
    for n, name in ((1, "l1"), (0, "g")):
        old, side = ("l2", "m2") if n else ("l1", "m1")
        wanted = set(range(*table[name]))
        if n:
            wanted |= set(range(*table["m1"]))
        for row in sorted(wanted):
            both = [a + b for a, b in zip(back.get(old, d, row), back.get(side, d, row))]
            if row in range(*table[name]):
                new = step(old, row, both, n)
                if n == 0:
                    new = [v * e for v, e in zip(new, past.get("e", d, row))]
                back.put(name, d, row, new)
            if n and row in range(*table["m1"]):
                new = spread(*back.around("m2", d, row), base_lateral, base_depth)
                parts = zip(new, past.get("a1", d, row), both)
                back.put("m1", d, row, [v - a * (neutral_rate * s) for v, a, s in parts])


def back_near_kernel(rows, groups, local, near, far, extra, cot, swap, back_near):
    half = rows // 2
    area = rows * groups * SUB
    inner = half + HALO_COT
    spread = make_spread()
    for d in range(local):
        past = Fields(rows, local, (near, near_rows), (far, far_rows))
        rate = -exposure_rate * past.get("dose", d, 0)[0]
        light = [extra[side, k] for side in range(2) for k in range(groups)]
        past.more["a0", d, rows] = [1.0 - jnp.exp(rate * v) for v in light]
        for n in range(3):
            row = rows - 1 - n
            past.more["a%d" % (n + 1), d, row] = next_acid(spread, past, d, n, row)[0]
        for n, row in ((3, half + 2), (2, half + 1)):
            left = left_of(past.get("a%d" % (5 - n), d, row))
            past.more["c%d" % n, d, row] = [v * m for v, m in zip(past.get("c%d" % n, d, row), left)]
        back = Fields(rows, local, (back_near, back_near_rows))
        table = back_near_rows(rows)
        for row in range(*table["ct"]):
            value = [vector(cot, rows, groups, k, chip_row(rows, row), d * area) for k in range(groups)]
            back.put("ct", d, row, value + [swap[2 * rows + d * inner + row, k] for k in range(groups)])
        backward_rows(spread, past, back, d, table)


def back_far_kernel(rows, groups, local, doses, near, far, back_near, cot_s, cot_c, *refs):
    outs = refs[: 2 * doses]
    store, full = refs[2 * doses :]
    half = rows // 2
    depth = groups * SUB
    place = lax.axis_index("dose")
    spread = make_spread()
    past = Fields(rows, local, (near, near_rows), (far, far_rows))
    back = Fields(rows, local, (back_near, back_near_rows), (store, back_far_rows))
    table = back_far_rows(rows)
    for d in range(local):
        for row in range(*table["ct"]):
            at = d * HALO_COT + HALO_COT + row
            value = [cot_s[at, k] for k in range(groups)] + [cot_c[at, k] for k in range(groups)]
            back.put("ct", d, row, value)
        backward_rows(spread, past, back, d, table)
    for row in range(half):
        value = back.get("g", 0, row)
        for d in range(1, local):
            value = [v + w for v, w in zip(value, back.get("g", d, row))]
        for i in range(2 * groups):
            side, k = divmod(i, groups)
            full[side, row, pl.ds(k, SUB, stride=groups), :] = value[i]
    piece = depth // doses
    for side in range(2):
        for k in range(doses):
            start = pl.multiple_of(lax.rem(place + k, doses) * piece, SUB)
            for row in range(half):
                outs[side * doses + k][row] = full[side, row, pl.ds(start, piece), :]


def join_kernel(rows, piece, doses, *refs):
    parts, out = refs[:-1], refs[-1]
    half = rows // 2
    core = lax.axis_index("ty")
    for side in range(2):
        for row in range(half):
            owner = core + side * (1 - 2 * core)
            at = row + owner * (rows - 1 - 2 * row)
            for g in range(piece // SUB):
                value = parts[side * doses][row, pl.ds(g * SUB, SUB), :]
                for k in range(1, doses):
                    value = value + parts[side * doses + k][row, pl.ds(g * SUB, SUB), :]
                out[pl.ds(g * SUB * rows + at, SUB, stride=rows), :] = value


def gradient(aerial_image, quencher, cotangent, dose_levels, dose_index):
    depth, rows, lanes = aerial_image.shape
    local = cotangent.shape[0]
    groups = depth // SUB
    half = rows // 2
    doses = lax.axis_size("dose")
    ring = lax.axis_size("tx")
    assert rows == half + HALO_QUENCH and HALO_AERIAL == HALO_QUENCH + 1
    f32 = jnp.float32
    aerial = aerial_image.reshape(depth * rows, lanes)
    quench = quencher.reshape(depth * rows, lanes)
    cot = cotangent.reshape(local * depth * rows, lanes)
    vmem = pl.BlockSpec(memory_space=pltpu.VMEM)
    smem = pl.BlockSpec(memory_space=pltpu.SMEM)

    def call(kernel, fixed, args, outs, scratch=(), scalars=0, flops=0, space=pltpu.VMEM):
        def body(*refs):
            kernel(*fixed, *refs)

        moved = sum(4 * x.size for x in list(args) + list(outs))
        return pl.pallas_call(
            body,
            out_shape=tuple(outs),
            in_specs=[smem] * scalars + [pl.BlockSpec(memory_space=space)] * (len(args) - scalars),
            out_specs=(vmem,) * len(outs),
            scratch_shapes=list(scratch),
            compiler_params=pltpu.CompilerParams(vmem_limit_bytes=LIMIT),
            cost_estimate=pl.CostEstimate(flops=flops, bytes_accessed=moved, transcendentals=0),
        )(*args)

    def field(n, vectors=groups):
        return jax.ShapeDtypeStruct((n, vectors, SUB, lanes), f32)

    def device(t, c):
        return (t % ring) * 2 + c

    straight = [(device(t, c), device(t + 1 - 2 * c, c)) for t in range(ring) for c in range(2)]
    crossed = [(device(t, c), device(t - 1 + 2 * c, 1 - c)) for t in range(ring) for c in range(2)]
    across = [(0, 1), (1, 0)]

    def along(value, pairs):
        return lax.ppermute(value, ("tx", "ty"), pairs)

    n_image = HALO_AERIAL + HALO_QUENCH
    n_cot = local * HALO_COT
    n_swap = 2 * rows + local * (half + HALO_COT)
    flat = [jax.ShapeDtypeStruct(x.shape, f32) for x in (aerial, quench, cot)]
    image_s, image_c, aerial, quench, cot = call(
        image_kernel,
        (rows, groups),
        [pltpu.with_memory_space_constraint(x, pltpu.HBM) for x in (aerial, quench, cot)],
        [field(n_image), field(n_image)] + flat,
        [pltpu.SemaphoreType.DMA((3,))],
        space=pltpu.HBM,
    )
    image_s = along(image_s, straight)
    image_c = along(image_c, crossed)
    sends = [field(n) for n in (n_cot, n_cot, n_swap)]
    cot_s, cot_c, swap = call(rest_kernel, (rows, groups, local), (aerial, quench, cot), sends)
    swap = lax.ppermute(swap, "ty", across)
    cot_s = along(cot_s, straight)
    cot_c = along(cot_c, crossed)

    (near,) = call(
        near_kernel,
        (rows, groups, local),
        (dose_levels, dose_index, aerial, quench, swap),
        (field(places_of(near_rows(rows), local)[1], 2 * groups),),
        scalars=2,
        flops=10_000_000,
    )
    last = HALO_AERIAL - 1
    extra = jnp.concatenate((image_c[last : last + 1], image_s[last : last + 1]), axis=0)
    extra = lax.ppermute(extra, "ty", across)
    (far,) = call(
        far_kernel,
        (rows, groups, local),
        (near, image_s, image_c),
        (field(places_of(far_rows(rows), local)[1], 2 * groups),),
        flops=10_000_000,
    )
    (back_near,) = call(
        back_near_kernel,
        (rows, groups, local),
        (near, far, extra, cot, swap),
        (field(places_of(back_near_rows(rows), local)[1], 2 * groups),),
        flops=10_000_000,
    )
    piece = depth // doses
    parts = call(
        back_far_kernel,
        (rows, groups, local, doses),
        (near, far, back_near, cot_s, cot_c),
        (jax.ShapeDtypeStruct((half, piece, lanes), f32),) * (2 * doses),
        [
            pltpu.VMEM((places_of(back_far_rows(rows), local)[1], 2 * groups, SUB, lanes), f32),
            pltpu.VMEM((2, half, depth, lanes), f32),
        ],
        flops=10_000_000,
    )

    arrived = []
    for side in range(2):
        for k in range(doses):
            part = parts[side * doses + k]
            if side or k:
                pairs = [(c * doses + d, (c ^ side) * doses + (d + k) % doses) for d in range(doses) for c in range(2)]
                part = lax.ppermute(part, ("ty", "dose"), pairs)
            arrived.append(part)
    (out,) = call(join_kernel, (rows, piece, doses), arrived, (jax.ShapeDtypeStruct((piece * rows, lanes), f32),))
    return out.reshape(piece, rows, lanes)


def solution(mesh):
    placed = (
        P("focus", "tx", "ty"),
        P(None, "tx", "ty"),
        P(("focus", "dose"), None, "tx", "ty"),
        P(),
        P(("focus", "dose")),
    )
    return jax.shard_map(
        gradient,
        mesh=mesh,
        in_specs=placed,
        out_specs=P(("focus", "dose"), "tx", "ty"),
        check_vma=False,
    )
```

```python
import jax
import jax.numpy as jnp
from jax import lax
from jax.experimental import pallas as pl
from jax.experimental.pallas import tpu as pltpu
from jax.sharding import PartitionSpec as P


exposure_rate = 1.0
neutral_rate = 0.8
deprotect_rate = 0.5
acid_lateral = 0.23
acid_depth = 0.02
base_lateral = 0.2
base_depth = 0.02

HALO_AERIAL = 5
HALO_QUENCH = 4
HALO_COT = 3
SUB = 8
LIMIT = 20 << 20


class Window:
    def __init__(self, depth, doses):
        self.depth, self.doses = depth, doses
        self.piece = depth // doses
        self.ends = 0 if doses == 1 else 1 if doses == 2 else 2
        self.size = min(depth, self.piece + SUB * self.ends)
        self.groups = self.size // SUB

    def layers(self, halo):
        return min(self.depth, self.piece + halo * self.ends)

    def clamp(self, owner, halo, size):
        return jnp.minimum(jnp.maximum(owner * self.piece - halo, 0), self.depth - size)

    def start(self, owner):
        return self.clamp(owner, SUB, self.size)

    def sent(self, owner, halo):
        return self.clamp(owner, halo, self.layers(halo))


def dense_places(window, parts):
    places, at = [], window.size - window.layers(parts[0][0])
    for halo, count in parts:
        places.append(at)
        at += count * window.layers(halo)
    at += window.size - window.layers(parts[-1][0])
    return places, -(-at // SUB) * SUB


def image_parts():
    return ((HALO_AERIAL, HALO_AERIAL), (HALO_QUENCH, HALO_QUENCH))


def cot_parts(count):
    return ((HALO_COT, count),)


def chip_row(rows, row):
    return row + lax.axis_index("ty") * (rows - 1 - 2 * row)


def vector(ref, rows, groups, first, row, base=0):
    return ref[pl.ds(base + rows * first + row, SUB, stride=rows * groups), :]


def put_dense(dst, at, src, base, rows, row, first, layers):
    for g in range(0, layers, SUB):
        n = min(SUB, layers - g)
        dst[pl.ds(at + g, n), :] = src[pl.ds(base + rows * (first + g) + row, n, stride=rows), :]


def clear_ends(dst):
    zero = jnp.zeros((SUB, dst.shape[1]), jnp.float32)
    dst[pl.ds(0, SUB), :] = zero
    dst[pl.ds(dst.shape[0] - SUB, SUB), :] = zero


def from_dense(src, at, window, owner, halo):
    start = at - (window.sent(owner, halo) - window.start(owner))
    return [src[pl.ds(start + k, SUB, stride=window.groups), :] for k in range(window.groups)]


def image_kernel(rows, window, local, *refs):
    image_hbm, quench_hbm, cot_hbm, levels_hbm, index_hbm = refs[:5]
    image_s, image_c, dose, aerial, quench, cot, levels, index, sems = refs[5:]
    pairs = ((image_hbm, aerial), (quench_hbm, quench), (cot_hbm, cot), (levels_hbm, levels), (index_hbm, index))
    copies = [pltpu.make_async_copy(src, dst, sems.at[i]) for i, (src, dst) in enumerate(pairs)]
    for copy in copies:
        copy.start()
    clear_ends(image_s)
    clear_ends(image_c)
    owner = lax.axis_index("dose")
    places, _ = dense_places(window, image_parts())
    copies[0].wait()
    copies[1].wait()
    for src, at, width in ((aerial, places[0], HALO_AERIAL), (quench, places[1], HALO_QUENCH)):
        layers, first = window.layers(width), window.sent(owner, width)
        for i in range(width):
            for dst, row in ((image_s, rows - width + i), (image_c, width - 1 - i)):
                put_dense(dst, at + i * layers, src, 0, rows, chip_row(rows, row), first, layers)
    for copy in copies[2:]:
        copy.wait()
    for d in range(local):
        dose[d] = jnp.full(dose.shape[1:], levels[index[d]], jnp.float32)


def rest_kernel(rows, window, local, aerial, quench, cot, swap, *dense):
    depth, groups, doses = window.depth, window.groups, window.doses
    area = rows * depth
    inner = rows // 2 + HALO_COT
    owner = lax.axis_index("dose")
    layers = window.layers(HALO_COT)
    sends = dense[: 2 * doses]
    wholes = dense[2 * doses :]
    for ref in dense:
        clear_ends(ref)
    lead = window.size - layers
    for k in range(doses):
        first = window.sent(lax.rem(owner + k, doses), HALO_COT)
        for d in range(local):
            for i in range(HALO_COT):
                at = lead + (d * HALO_COT + i) * layers
                put_dense(sends[2 * k], at, cot, d * area, rows, chip_row(rows, rows - HALO_COT + i), first, layers)
                put_dense(sends[2 * k + 1], at, cot, d * area, rows, chip_row(rows, HALO_COT - 1 - i), first, layers)
            if k:
                for row in range(rows):
                    at = lead + (d * rows + row) * layers
                    put_dense(wholes[k - 1], at, cot, d * area, rows, row, first, layers)
    place = 0
    parts = [(aerial, 0, rows), (quench, 0, rows)] + [(cot, d * area, inner) for d in range(local)]
    start = window.start(owner)
    for src, base, width in parts:
        for i in range(width):
            for k in range(groups):
                swap[place, k] = vector(src, rows, groups, start + k, chip_row(rows, rows - 1 - i), base)
            place += 1


def make_spread():
    lane = lax.broadcasted_iota(jnp.int32, (SUB, 128), 1)
    sub = lax.broadcasted_iota(jnp.int32, (SUB, 128), 0)
    first_lane = lane == 0
    last_lane = lane == 127
    first_sub = sub == 0
    last_sub = sub == SUB - 1

    def spread(above, center, below, along, depthwise):
        count = len(center)
        groups = count // 2
        keep = 1.0 - 4.0 * along - 2.0 * depthwise
        result = []
        for i in range(count):
            k = i % groups
            j = (i + groups) % count
            right = pltpu.roll(jnp.where(first_lane, center[j], center[i]), 127, 1)
            left = pltpu.roll(jnp.where(last_lane, center[j], center[i]), 1, 1)
            lateral = (above[i] + below[i]) + (right + left)
            if k + 1 < groups:
                deeper = center[i + 1]
            else:
                deeper = jnp.where(last_sub, center[i], pltpu.roll(center[i - k], SUB - 1, 0))
            if k > 0:
                higher = center[i - 1]
            else:
                higher = jnp.where(first_sub, center[i], pltpu.roll(center[i + groups - 1], 1, 0))
            result.append(keep * center[i] + along * lateral + depthwise * (deeper + higher))
        return result

    return spread


def near_rows(rows):
    half = rows // 2
    return {
        "q0": (0, rows),
        "a0": (0, rows),
        "a1": (1, rows - 1),
        "a2": (2, rows - 2),
        "a3": (3, rows - 3),
        "q1": (1, rows - 1),
        "q2": (2, rows - 2),
        "c3": (2, half + 3),
        "c2": (3, half + 2),
        "c1": (3, half + 1),
        "c0": (3, half),
        "e": (0, half),
        "dose": (0, 1),
    }


def far_rows(rows):
    return {
        "q0": (-4, 0),
        "a0": (-5, 0),
        "a1": (-4, 1),
        "a2": (-3, 2),
        "a3": (-2, 3),
        "q1": (-3, 1),
        "q2": (-2, 2),
        "c3": (-3, 2),
        "c2": (-2, 3),
        "c1": (-1, 3),
        "c0": (0, 3),
    }


def places_of(table, local):
    places, total = {}, 0
    for name, (first, end) in table.items():
        for d in range(local):
            for row in range(first, end):
                if name == "q0" and d > 0:
                    places[name, d, row] = places[name, 0, row]
                else:
                    places[name, d, row] = total
                    total += 1
    return places, total


def back_near_rows(rows):
    half = rows // 2
    return {
        "ct": (0, half + 3),
        "l3": (0, half + 3),
        "l2": (1, half + 2),
        "m2": (0, half + 1),
        "l1": (2, half + 1),
        "m1": (1, half),
        "g": (3, half),
    }


def back_far_rows(rows):
    return {
        "ct": (-3, 0),
        "l3": (-3, 0),
        "l2": (-2, 1),
        "m2": (-1, 0),
        "l1": (-1, 2),
        "m1": (0, 1),
        "g": (0, 3),
    }


class Fields:
    def __init__(self, rows, local, *stores):
        self.stores = [(ref, places_of(table(rows), local)[0]) for ref, table in stores]
        self.more = {}

    def get(self, name, d, row):
        if (name, d, row) in self.more:
            return self.more[name, d, row]
        for ref, places in self.stores:
            if (name, d, row) in places:
                at = places[name, d, row]
                return [ref[at, i] for i in range(ref.shape[1])]
        raise KeyError((name, row))

    def around(self, name, d, row):
        return [self.get(name, d, row + i) for i in (-1, 0, 1)]

    def put(self, name, d, row, value):
        ref, places = self.stores[-1]
        at = places[name, d, row]
        for i in range(len(value)):
            ref[at, i] = value[i]


def left_of(acid):
    return [1.0 - deprotect_rate * v for v in acid]


def next_acid(spread, fields, d, n, row):
    name = "a%d" % n
    above, center, below = fields.around(name, d, row)
    quench = fields.get("q%d" % n, d, row)
    new = spread(above, center, below, acid_lateral, acid_depth)
    reaction = [neutral_rate * a * q for a, q in zip(center, quench)]
    return [v - r for v, r in zip(new, reaction)], reaction


def forward_rows(spread, fields, d, table):
    for n in range(3):
        first, end = table["a%d" % (n + 1)]
        for row in range(first, end):
            new, reaction = next_acid(spread, fields, d, n, row)
            fields.put("a%d" % (n + 1), d, row, new)
            if n < 2:
                q_first, q_end = table["q%d" % (n + 1)]
                if q_first <= row < q_end:
                    name = "q%d" % n
                    new = spread(*fields.around(name, d, row), base_lateral, base_depth)
                    fields.put("q%d" % (n + 1), d, row, [v - r for v, r in zip(new, reaction)])

    first = min(table[c][0] for c in ("c3", "c2", "c1", "c0"))
    end = max(table[c][1] for c in ("c3", "c2", "c1", "c0"))
    for row in range(first, end):
        wanted = [n for n in range(4) if table["c%d" % n][0] <= row < table["c%d" % n][1]]
        left = {}

        def of(n):
            if n not in left:
                left[n] = left_of(fields.get("a%d" % n, d, row))
            return left[n]

        for n in wanted:
            parts = [m for m in range(4) if m != n]
            if n >= 2 and table["e"][1] > 0 and row == table["c%d" % n][1] - 1:
                parts = parts[:2]
            value = [(-deprotect_rate) * v for v in of(parts[0])]
            for m in parts[1:]:
                value = [v * w for v, w in zip(value, of(m))]
            fields.put("c%d" % n, d, row, value)


def near_kernel(rows, window, local, *refs):
    doses, groups = window.doses, window.groups
    dose_refs, (aerial, quench, swap, near) = refs[:doses], refs[doses:]
    half = rows // 2
    spread = make_spread()
    total = local * doses
    fields = Fields(rows, total, (near, near_rows))
    start = window.start(lax.axis_index("dose"))

    def source(raw, at, row):
        own = [vector(raw, rows, groups, start + k, chip_row(rows, row)) for k in range(groups)]
        return own + [swap[at + row, k] for k in range(groups)]

    for row in range(rows):
        fields.put("q0", 0, row, source(quench, rows, row))
    for d in range(total):
        dose = dose_refs[d // local][d % local]
        fields.put("dose", d, 0, [dose] * (2 * groups))
        rate = -exposure_rate * dose
        for row in range(rows):
            absorbed = [jnp.exp(rate * v) for v in source(aerial, 0, row)]
            fields.put("a0", d, row, [1.0 - v for v in absorbed])
            if row < half:
                fields.put("e", d, row, [exposure_rate * dose * v for v in absorbed])
        forward_rows(spread, fields, d, near_rows(rows))


def far_kernel(rows, window, total, near, image_s, image_c, far):
    spread = make_spread()
    fields = Fields(rows, total, (near, near_rows), (far, far_rows))
    table = dict(far_rows(rows), e=(0, 0))
    owner = lax.axis_index("dose")
    places, _ = dense_places(window, image_parts())

    def source(part, halo, row):
        at = places[part] + (halo + row) * window.layers(halo)
        return [v for src in (image_s, image_c) for v in from_dense(src, at, window, owner, halo)]

    for row in range(-HALO_QUENCH, 0):
        fields.put("q0", 0, row, source(1, HALO_QUENCH, row))
    for d in range(total):
        rate = -exposure_rate * fields.get("dose", d, 0)[0]
        for row in range(-HALO_AERIAL, 0):
            fields.put("a0", d, row, [1.0 - jnp.exp(rate * v) for v in source(0, HALO_AERIAL, row)])
        forward_rows(spread, fields, d, table)


def backward_rows(spread, past, back, d, table):
    def step(name, row, both, n):
        new = spread(*back.around(name, d, row), acid_lateral, acid_depth)
        parts = zip(new, past.get("q%d" % n, d, row), both, past.get("c%d" % n, d, row), back.get("ct", d, row))
        return [v - q * (neutral_rate * s) + c * t for v, q, s, c, t in parts]

    for row in range(*table["l3"]):
        back.put("l3", d, row, [c * v for c, v in zip(past.get("c3", d, row), back.get("ct", d, row))])
    for row in range(*table["m2"]):
        parts = zip(past.get("a2", d, row), back.get("l3", d, row))
        back.put("m2", d, row, [-(neutral_rate * a * s) for a, s in parts])
    for row in range(*table["l2"]):
        back.put("l2", d, row, step("l3", row, back.get("l3", d, row), 2))
    for n, name in ((1, "l1"), (0, "g")):
        old, side = ("l2", "m2") if n else ("l1", "m1")
        wanted = set(range(*table[name]))
        if n:
            wanted |= set(range(*table["m1"]))
        for row in sorted(wanted):
            both = [a + b for a, b in zip(back.get(old, d, row), back.get(side, d, row))]
            if row in range(*table[name]):
                new = step(old, row, both, n)
                if n == 0:
                    new = [v * e for v, e in zip(new, past.get("e", d, row))]
                back.put(name, d, row, new)
            if n and row in range(*table["m1"]):
                new = spread(*back.around("m2", d, row), base_lateral, base_depth)
                parts = zip(new, past.get("a1", d, row), both)
                back.put("m1", d, row, [v - a * (neutral_rate * s) for v, a, s in parts])


def back_near_kernel(rows, window, local, near, far, extra_own, extra_par, cot, swap, *refs):
    doses, groups = window.doses, window.groups
    wholes, back_near = refs[:-1], refs[-1]
    half = rows // 2
    area = rows * window.depth
    inner = half + HALO_COT
    total = local * doses
    spread = make_spread()
    owner = lax.axis_index("dose")
    start = window.start(owner)
    layers = window.layers(HALO_COT)
    lead = window.size - layers
    places, _ = dense_places(window, image_parts())
    last = places[0] + (HALO_AERIAL - 1) * window.layers(HALO_AERIAL)
    for d in range(total):
        past = Fields(rows, total, (near, near_rows), (far, far_rows))
        rate = -exposure_rate * past.get("dose", d, 0)[0]
        light = [v for src in (extra_own, extra_par) for v in from_dense(src, last, window, owner, HALO_AERIAL)]
        past.more["a0", d, rows] = [1.0 - jnp.exp(rate * v) for v in light]
        for n in range(3):
            row = rows - 1 - n
            past.more["a%d" % (n + 1), d, row] = next_acid(spread, past, d, n, row)[0]
        for n, row in ((3, half + 2), (2, half + 1)):
            left = left_of(past.get("a%d" % (5 - n), d, row))
            past.more["c%d" % n, d, row] = [v * m for v, m in zip(past.get("c%d" % n, d, row), left)]
        back = Fields(rows, total, (back_near, back_near_rows))
        table = back_near_rows(rows)
        k, i = divmod(d, local)
        for row in range(*table["ct"]):
            if k == 0:
                value = [vector(cot, rows, groups, start + g, chip_row(rows, row), i * area) for g in range(groups)]
                value += [swap[2 * rows + i * inner + row, g] for g in range(groups)]
            else:
                at = lead + (i * rows + chip_row(rows, row)) * layers
                sides = (wholes[2 * k - 2], wholes[2 * k - 1])
                value = [v for src in sides for v in from_dense(src, at, window, owner, HALO_COT)]
            back.put("ct", d, row, value)
        backward_rows(spread, past, back, d, table)


def back_far_kernel(rows, window, local, near, far, back_near, *refs):
    doses, groups = window.doses, window.groups
    sends = refs[: 2 * doses]
    mine, other, store, full = refs[2 * doses :]
    half = rows // 2
    total = local * doses
    owner = lax.axis_index("dose")
    layers = window.layers(HALO_COT)
    lead = window.size - layers
    spread = make_spread()
    past = Fields(rows, total, (near, near_rows), (far, far_rows))
    back = Fields(rows, total, (back_near, back_near_rows), (store, back_far_rows))
    table = back_far_rows(rows)
    for d in range(total):
        k, i = divmod(d, local)
        for row in range(*table["ct"]):
            at = lead + (i * HALO_COT + HALO_COT + row) * layers
            sides = (sends[2 * k], sends[2 * k + 1])
            back.put("ct", d, row, [v for src in sides for v in from_dense(src, at, window, owner, HALO_COT)])
        backward_rows(spread, past, back, d, table)
    for row in range(half):
        value = back.get("g", 0, row)
        for d in range(1, total):
            value = [v + w for v, w in zip(value, back.get("g", d, row))]
        for i in range(2 * groups):
            side, k = divmod(i, groups)
            full[side, row, pl.ds(k, SUB, stride=groups), :] = value[i]
    start = pl.multiple_of(owner * window.piece - window.start(owner), SUB)
    for side, out in enumerate((mine, other)):
        for row in range(half):
            out[row] = full[side, row, pl.ds(start, window.piece), :]


def join_kernel(rows, piece, mine, other, out):
    core = lax.axis_index("ty")
    for owner, part in ((core, mine), (1 - core, other)):
        for row in range(rows // 2):
            at = row + owner * (rows - 1 - 2 * row)
            for g in range(0, piece, SUB):
                out[pl.ds(g * rows + at, SUB, stride=rows), :] = part[row, pl.ds(g, SUB), :]


def gradient(aerial_image, quencher, cotangent, dose_levels, dose_index):
    depth, rows, lanes = aerial_image.shape
    local = cotangent.shape[0]
    half = rows // 2
    doses = lax.axis_size("dose")
    ring = lax.axis_size("tx")
    assert rows == half + HALO_QUENCH and HALO_AERIAL == HALO_QUENCH + 1
    window = Window(depth, doses)
    groups, piece = window.groups, window.piece
    total = local * doses
    f32 = jnp.float32
    aerial = aerial_image.reshape(depth * rows, lanes)
    quench = quencher.reshape(depth * rows, lanes)
    cot = cotangent.reshape(local * depth * rows, lanes)

    def call(kernel, fixed, args, outs, scratch=(), flops=0, space=pltpu.VMEM):
        def body(*refs):
            kernel(*fixed, *refs)

        moved = sum(4 * x.size for x in list(args) + list(outs))
        return pl.pallas_call(
            body,
            out_shape=tuple(outs),
            in_specs=[pl.BlockSpec(memory_space=space)] * len(args),
            out_specs=(pl.BlockSpec(memory_space=pltpu.VMEM),) * len(outs),
            scratch_shapes=list(scratch),
            compiler_params=pltpu.CompilerParams(vmem_limit_bytes=LIMIT),
            cost_estimate=pl.CostEstimate(flops=flops, bytes_accessed=moved, transcendentals=0),
        )(*args)

    def array(*shape):
        return jax.ShapeDtypeStruct(shape + (lanes,), f32)

    def store(table):
        return (places_of(table(rows), total)[1], 2 * groups, SUB)

    def along(value, cross=0, step=1, k=0):
        pairs = []
        for t in range(ring):
            for c in range(2):
                for d in range(doses):
                    up = step * (1 - 2 * (c ^ cross))
                    target = (((t + up) % ring) * 2 + (c ^ cross)) * doses + (d + k) % doses
                    pairs.append(((t * 2 + c) * doses + d, target))
        return lax.ppermute(value, ("tx", "ty", "dose"), pairs)

    def across(value):
        return along(value, cross=1, step=0)

    images = array(dense_places(window, image_parts())[1])
    halos = array(dense_places(window, cot_parts(local * HALO_COT))[1])
    whole = array(dense_places(window, cot_parts(local * rows))[1])
    flat = [jax.ShapeDtypeStruct(x.shape, f32) for x in (aerial, quench, cot)]
    image_s, image_c, dose, aerial, quench, cot = call(
        image_kernel,
        (rows, window, local),
        [pltpu.with_memory_space_constraint(x, pltpu.HBM) for x in (aerial, quench, cot, dose_levels, dose_index)],
        [images, images, array(local, SUB)] + flat,
        [
            pltpu.SMEM(dose_levels.shape, f32),
            pltpu.SMEM(dose_index.shape, jnp.int32),
            pltpu.SemaphoreType.DMA((5,)),
        ],
        space=pltpu.HBM,
    )
    image_s = along(image_s)
    image_c = along(image_c, cross=1)
    swap_rows = 2 * rows + local * (half + HALO_COT)
    rest = call(
        rest_kernel,
        (rows, window, local),
        (aerial, quench, cot),
        [array(swap_rows, groups, SUB)] + [halos] * (2 * doses) + [whole] * (doses - 1),
    )
    swap = across(rest[0])
    values = [dose] + [along(dose, step=0, k=k) for k in range(1, doses)]
    wholes = []
    for k in range(1, doses):
        arrived = along(rest[2 * doses + k], step=0, k=k)
        wholes += [arrived, across(arrived)]
    sends = []
    for k in range(doses):
        sends.append(along(rest[1 + 2 * k], k=k))
        sends.append(along(rest[2 + 2 * k], cross=1, k=k))

    (near,) = call(
        near_kernel, (rows, window, local), values + [aerial, quench, swap], [array(*store(near_rows))], flops=10_000_000
    )
    extra_own = across(image_c)
    extra_par = across(image_s)
    (far,) = call(
        far_kernel, (rows, window, total), (near, image_s, image_c), [array(*store(far_rows))], flops=10_000_000
    )
    (back_near,) = call(
        back_near_kernel,
        (rows, window, local),
        [near, far, extra_own, extra_par, cot, swap] + wholes,
        [array(*store(back_near_rows))],
        flops=10_000_000,
    )
    mine, other = call(
        back_far_kernel,
        (rows, window, local),
        [near, far, back_near] + sends,
        [array(half, piece)] * 2,
        [
            pltpu.VMEM(store(back_far_rows) + (lanes,), f32),
            pltpu.VMEM((2, half, window.size, lanes), f32),
        ],
        flops=10_000_000,
    )
    other = across(other)
    (out,) = call(join_kernel, (rows, piece), (mine, other), [array(piece * rows)])
    return out.reshape(piece, rows, lanes)


def solution(mesh):
    placed = (
        P("focus", "tx", "ty"),
        P(None, "tx", "ty"),
        P(("focus", "dose"), None, "tx", "ty"),
        P(),
        P(("focus", "dose")),
    )
    return jax.shard_map(
        gradient,
        mesh=mesh,
        in_specs=placed,
        out_specs=P(("focus", "dose"), "tx", "ty"),
        check_vma=False,
    )
```

```python
import jax
import jax.numpy as jnp
from jax import lax
from jax.experimental import pallas as pl
from jax.experimental.pallas import tpu as pltpu
from jax.sharding import PartitionSpec as P


exposure_rate = 1.0
neutral_rate = 0.8
deprotect_rate = 0.5
acid_lateral = 0.23
acid_depth = 0.02
base_lateral = 0.2
base_depth = 0.02

HALO_AERIAL = 5
HALO_QUENCH = 4
HALO_COT = 3
SUB = 8
LIMIT = 20 << 20


class Window:
    def __init__(self, depth, doses):
        self.depth, self.doses = depth, doses
        self.piece = depth // doses
        self.ends = 0 if doses == 1 else 1 if doses == 2 else 2
        self.size = min(depth, self.piece + SUB * self.ends)
        self.groups = self.size // SUB

    def layers(self, halo):
        return min(self.depth, self.piece + halo * self.ends)

    def clamp(self, owner, halo, size):
        return jnp.minimum(jnp.maximum(owner * self.piece - halo, 0), self.depth - size)

    def start(self, owner):
        return self.clamp(owner, SUB, self.size)

    def sent(self, owner, halo):
        return self.clamp(owner, halo, self.layers(halo))


def dense_places(window, parts):
    places, at = [], window.size - window.layers(parts[0][0])
    for halo, count in parts:
        places.append(at)
        at += count * window.layers(halo)
    at += window.size - window.layers(parts[-1][0])
    return places, -(-at // SUB) * SUB


def image_parts():
    return ((HALO_AERIAL, HALO_AERIAL), (HALO_QUENCH, HALO_QUENCH))


def cot_parts(count):
    return ((HALO_COT, count),)


def chip_row(rows, row):
    return row + lax.axis_index("ty") * (rows - 1 - 2 * row)


def vector(ref, rows, groups, first, row, base=0):
    return ref[pl.ds(base + rows * first + row, SUB, stride=rows * groups), :]


def put_dense(dst, at, src, base, rows, row, first, layers):
    for g in range(0, layers, SUB):
        n = min(SUB, layers - g)
        dst[pl.ds(at + g, n), :] = src[pl.ds(base + rows * (first + g) + row, n, stride=rows), :]


def clear_ends(dst):
    zero = jnp.zeros((SUB, dst.shape[1]), jnp.float32)
    dst[pl.ds(0, SUB), :] = zero
    dst[pl.ds(dst.shape[0] - SUB, SUB), :] = zero


def from_dense(src, at, window, owner, halo):
    start = at - (window.sent(owner, halo) - window.start(owner))
    return [src[pl.ds(start + k, SUB, stride=window.groups), :] for k in range(window.groups)]


def image_kernel(rows, window, local, *refs):
    image_hbm, quench_hbm, cot_hbm, levels_hbm, index_hbm = refs[:5]
    image_s, image_c, dose, aerial, quench, cot, levels, index, sems = refs[5:]
    pairs = ((image_hbm, aerial), (quench_hbm, quench), (cot_hbm, cot), (levels_hbm, levels), (index_hbm, index))
    copies = [pltpu.make_async_copy(src, dst, sems.at[i]) for i, (src, dst) in enumerate(pairs)]
    for copy in copies:
        copy.start()
    clear_ends(image_s)
    clear_ends(image_c)
    owner = lax.axis_index("dose")
    places, _ = dense_places(window, image_parts())
    copies[0].wait()
    copies[1].wait()
    for src, at, width in ((aerial, places[0], HALO_AERIAL), (quench, places[1], HALO_QUENCH)):
        layers, first = window.layers(width), window.sent(owner, width)
        for i in range(width):
            for dst, row in ((image_s, rows - width + i), (image_c, width - 1 - i)):
                put_dense(dst, at + i * layers, src, 0, rows, chip_row(rows, row), first, layers)
    for copy in copies[2:]:
        copy.wait()
    for d in range(local):
        dose[d] = jnp.full(dose.shape[1:], levels[index[d]], jnp.float32)


def swap_layout(rows, window, local):
    vectors = 2 * rows + local * (rows // 2 + HALO_COT)
    halo = dense_places(window, cot_parts(local * HALO_COT))[1]
    return vectors * window.groups * SUB, halo


def swapped(swap, groups, place):
    return [swap[pl.ds((place * groups + k) * SUB, SUB), :] for k in range(groups)]


def rest_kernel(rows, window, local, dose, aerial, quench, cot, swap, *dense):
    depth, groups, doses = window.depth, window.groups, window.doses
    area = rows * depth
    inner = rows // 2 + HALO_COT
    owner = lax.axis_index("dose")
    layers = window.layers(HALO_COT)
    sends = dense[:doses]
    wholes = dense[doses:]
    handed, halo = swap_layout(rows, window, local)
    for ref in dense:
        clear_ends(ref)
    lead = window.size - layers
    zero = jnp.zeros((SUB, swap.shape[1]), jnp.float32)
    for k in range(doses):
        first = window.sent(lax.rem(owner + k, doses), HALO_COT)
        block = handed + k * halo
        swap[pl.ds(block, SUB), :] = zero
        swap[pl.ds(block + halo - SUB, SUB), :] = zero
        for d in range(local):
            for i in range(HALO_COT):
                at = lead + (d * HALO_COT + i) * layers
                put_dense(sends[k], at, cot, d * area, rows, chip_row(rows, rows - HALO_COT + i), first, layers)
                put_dense(swap, block + at, cot, d * area, rows, chip_row(rows, HALO_COT - 1 - i), first, layers)
            if k:
                for row in range(rows):
                    at = lead + (d * rows + row) * layers
                    put_dense(wholes[k - 1], at, cot, d * area, rows, row, first, layers)
                wholes[k - 1][pl.ds(wholes[k - 1].shape[0] - (local - d) * SUB, SUB), :] = dose[d]
    place = 0
    parts = [(aerial, 0, rows), (quench, 0, rows)] + [(cot, d * area, inner) for d in range(local)]
    start = window.start(owner)
    for src, base, width in parts:
        for i in range(width):
            for k in range(groups):
                value = vector(src, rows, groups, start + k, chip_row(rows, rows - 1 - i), base)
                swap[pl.ds((place * groups + k) * SUB, SUB), :] = value
            place += 1


def make_spread():
    lane = lax.broadcasted_iota(jnp.int32, (SUB, 128), 1)
    sub = lax.broadcasted_iota(jnp.int32, (SUB, 128), 0)
    first_lane = lane == 0
    last_lane = lane == 127
    first_sub = sub == 0
    last_sub = sub == SUB - 1

    def spread(above, center, below, along, depthwise):
        count = len(center)
        groups = count // 2
        keep = 1.0 - 4.0 * along - 2.0 * depthwise
        result = []
        for i in range(count):
            k = i % groups
            j = (i + groups) % count
            right = pltpu.roll(jnp.where(first_lane, center[j], center[i]), 127, 1)
            left = pltpu.roll(jnp.where(last_lane, center[j], center[i]), 1, 1)
            lateral = (above[i] + below[i]) + (right + left)
            if k + 1 < groups:
                deeper = center[i + 1]
            else:
                deeper = jnp.where(last_sub, center[i], pltpu.roll(center[i - k], SUB - 1, 0))
            if k > 0:
                higher = center[i - 1]
            else:
                higher = jnp.where(first_sub, center[i], pltpu.roll(center[i + groups - 1], 1, 0))
            result.append(keep * center[i] + along * lateral + depthwise * (deeper + higher))
        return result

    return spread


def near_rows(rows):
    half = rows // 2
    return {
        "q0": (0, rows),
        "a0": (0, rows),
        "a1": (1, rows - 1),
        "a2": (2, rows - 2),
        "a3": (3, rows - 3),
        "q1": (1, rows - 1),
        "q2": (2, rows - 2),
        "c3": (2, half + 3),
        "c2": (3, half + 2),
        "c1": (3, half + 1),
        "c0": (3, half),
        "e": (0, half),
        "dose": (0, 1),
    }


def far_rows(rows):
    return {
        "q0": (-4, 0),
        "a0": (-5, 0),
        "a1": (-4, 1),
        "a2": (-3, 2),
        "a3": (-2, 3),
        "q1": (-3, 1),
        "q2": (-2, 2),
        "c3": (-3, 2),
        "c2": (-2, 3),
        "c1": (-1, 3),
        "c0": (0, 3),
    }


def places_of(table, local):
    places, total = {}, 0
    for name, (first, end) in table.items():
        for d in range(local):
            for row in range(first, end):
                if name == "q0" and d > 0:
                    places[name, d, row] = places[name, 0, row]
                else:
                    places[name, d, row] = total
                    total += 1
    return places, total


def back_near_rows(rows):
    half = rows // 2
    return {
        "ct": (0, half + 3),
        "l3": (0, half + 3),
        "l2": (1, half + 2),
        "m2": (0, half + 1),
        "l1": (2, half + 1),
        "m1": (1, half),
        "g": (3, half),
    }


def back_far_rows(rows):
    return {
        "ct": (-3, 0),
        "l3": (-3, 0),
        "l2": (-2, 1),
        "m2": (-1, 0),
        "l1": (-1, 2),
        "m1": (0, 1),
        "g": (0, 3),
    }


class Fields:
    def __init__(self, rows, local, *stores):
        self.stores = [(ref, places_of(table(rows), local)[0]) for ref, table in stores]
        self.more = {}

    def get(self, name, d, row):
        if (name, d, row) in self.more:
            return self.more[name, d, row]
        for ref, places in self.stores:
            if (name, d, row) in places:
                at = places[name, d, row]
                return [ref[at, i] for i in range(ref.shape[1])]
        raise KeyError((name, row))

    def around(self, name, d, row):
        return [self.get(name, d, row + i) for i in (-1, 0, 1)]

    def put(self, name, d, row, value):
        ref, places = self.stores[-1]
        at = places[name, d, row]
        for i in range(len(value)):
            ref[at, i] = value[i]


def left_of(acid):
    return [1.0 - deprotect_rate * v for v in acid]


def next_acid(spread, fields, d, n, row):
    name = "a%d" % n
    above, center, below = fields.around(name, d, row)
    quench = fields.get("q%d" % n, d, row)
    new = spread(above, center, below, acid_lateral, acid_depth)
    reaction = [neutral_rate * a * q for a, q in zip(center, quench)]
    return [v - r for v, r in zip(new, reaction)], reaction


def forward_rows(spread, fields, d, table):
    for n in range(3):
        first, end = table["a%d" % (n + 1)]
        for row in range(first, end):
            new, reaction = next_acid(spread, fields, d, n, row)
            fields.put("a%d" % (n + 1), d, row, new)
            if n < 2:
                q_first, q_end = table["q%d" % (n + 1)]
                if q_first <= row < q_end:
                    name = "q%d" % n
                    new = spread(*fields.around(name, d, row), base_lateral, base_depth)
                    fields.put("q%d" % (n + 1), d, row, [v - r for v, r in zip(new, reaction)])

    first = min(table[c][0] for c in ("c3", "c2", "c1", "c0"))
    end = max(table[c][1] for c in ("c3", "c2", "c1", "c0"))
    for row in range(first, end):
        wanted = [n for n in range(4) if table["c%d" % n][0] <= row < table["c%d" % n][1]]
        left = {}

        def of(n):
            if n not in left:
                left[n] = left_of(fields.get("a%d" % n, d, row))
            return left[n]

        for n in wanted:
            parts = [m for m in range(4) if m != n]
            if n >= 2 and table["e"][1] > 0 and row == table["c%d" % n][1] - 1:
                parts = parts[:2]
            value = [(-deprotect_rate) * v for v in of(parts[0])]
            for m in parts[1:]:
                value = [v * w for v, w in zip(value, of(m))]
            fields.put("c%d" % n, d, row, value)


def near_kernel(rows, window, local, *refs):
    doses, groups = window.doses, window.groups
    dose_refs, (aerial, quench, swap, near) = refs[:doses], refs[doses:]
    half = rows // 2
    spread = make_spread()
    total = local * doses
    fields = Fields(rows, total, (near, near_rows))
    start = window.start(lax.axis_index("dose"))

    def source(raw, at, row):
        own = [vector(raw, rows, groups, start + k, chip_row(rows, row)) for k in range(groups)]
        return own + swapped(swap, groups, at + row)

    for row in range(rows):
        fields.put("q0", 0, row, source(quench, rows, row))
    for d in range(total):
        ref, i = dose_refs[d // local], d % local
        dose = ref[pl.ds(ref.shape[0] - (local - i) * SUB, SUB), :] if d >= local else ref[i]
        fields.put("dose", d, 0, [dose] * (2 * groups))
        rate = -exposure_rate * dose
        for row in range(rows):
            absorbed = [jnp.exp(rate * v) for v in source(aerial, 0, row)]
            fields.put("a0", d, row, [1.0 - v for v in absorbed])
            if row < half:
                fields.put("e", d, row, [exposure_rate * dose * v for v in absorbed])
        forward_rows(spread, fields, d, near_rows(rows))


def far_kernel(rows, window, total, near, image_s, image_c, far):
    spread = make_spread()
    fields = Fields(rows, total, (near, near_rows), (far, far_rows))
    table = dict(far_rows(rows), e=(0, 0))
    owner = lax.axis_index("dose")
    places, _ = dense_places(window, image_parts())

    def source(part, halo, row):
        at = places[part] + (halo + row) * window.layers(halo)
        return [v for src in (image_s, image_c) for v in from_dense(src, at, window, owner, halo)]

    for row in range(-HALO_QUENCH, 0):
        fields.put("q0", 0, row, source(1, HALO_QUENCH, row))
    for d in range(total):
        rate = -exposure_rate * fields.get("dose", d, 0)[0]
        for row in range(-HALO_AERIAL, 0):
            fields.put("a0", d, row, [1.0 - jnp.exp(rate * v) for v in source(0, HALO_AERIAL, row)])
        forward_rows(spread, fields, d, table)


def backward_rows(spread, past, back, d, table):
    def step(name, row, both, n):
        new = spread(*back.around(name, d, row), acid_lateral, acid_depth)
        parts = zip(new, past.get("q%d" % n, d, row), both, past.get("c%d" % n, d, row), back.get("ct", d, row))
        return [v - q * (neutral_rate * s) + c * t for v, q, s, c, t in parts]

    for row in range(*table["l3"]):
        back.put("l3", d, row, [c * v for c, v in zip(past.get("c3", d, row), back.get("ct", d, row))])
    for row in range(*table["m2"]):
        parts = zip(past.get("a2", d, row), back.get("l3", d, row))
        back.put("m2", d, row, [-(neutral_rate * a * s) for a, s in parts])
    for row in range(*table["l2"]):
        back.put("l2", d, row, step("l3", row, back.get("l3", d, row), 2))
    for n, name in ((1, "l1"), (0, "g")):
        old, side = ("l2", "m2") if n else ("l1", "m1")
        wanted = set(range(*table[name]))
        if n:
            wanted |= set(range(*table["m1"]))
        for row in sorted(wanted):
            both = [a + b for a, b in zip(back.get(old, d, row), back.get(side, d, row))]
            if row in range(*table[name]):
                new = step(old, row, both, n)
                if n == 0:
                    new = [v * e for v, e in zip(new, past.get("e", d, row))]
                back.put(name, d, row, new)
            if n and row in range(*table["m1"]):
                new = spread(*back.around("m2", d, row), base_lateral, base_depth)
                parts = zip(new, past.get("a1", d, row), both)
                back.put("m1", d, row, [v - a * (neutral_rate * s) for v, a, s in parts])


def back_near_kernel(rows, window, local, near, far, extra_own, extra_par, cot, swap, *refs):
    doses, groups = window.doses, window.groups
    wholes, back_near = refs[:-1], refs[-1]
    half = rows // 2
    area = rows * window.depth
    inner = half + HALO_COT
    total = local * doses
    spread = make_spread()
    owner = lax.axis_index("dose")
    start = window.start(owner)
    layers = window.layers(HALO_COT)
    lead = window.size - layers
    places, _ = dense_places(window, image_parts())
    last = places[0] + (HALO_AERIAL - 1) * window.layers(HALO_AERIAL)
    for d in range(total):
        past = Fields(rows, total, (near, near_rows), (far, far_rows))
        rate = -exposure_rate * past.get("dose", d, 0)[0]
        light = [v for src in (extra_own, extra_par) for v in from_dense(src, last, window, owner, HALO_AERIAL)]
        past.more["a0", d, rows] = [1.0 - jnp.exp(rate * v) for v in light]
        for n in range(3):
            row = rows - 1 - n
            past.more["a%d" % (n + 1), d, row] = next_acid(spread, past, d, n, row)[0]
        for n, row in ((3, half + 2), (2, half + 1)):
            left = left_of(past.get("a%d" % (5 - n), d, row))
            past.more["c%d" % n, d, row] = [v * m for v, m in zip(past.get("c%d" % n, d, row), left)]
        back = Fields(rows, total, (back_near, back_near_rows))
        table = back_near_rows(rows)
        k, i = divmod(d, local)
        for row in range(*table["ct"]):
            if k == 0:
                value = [vector(cot, rows, groups, start + g, chip_row(rows, row), i * area) for g in range(groups)]
                value += swapped(swap, groups, 2 * rows + i * inner + row)
            else:
                at = lead + (i * rows + chip_row(rows, row)) * layers
                sides = (wholes[2 * k - 2], wholes[2 * k - 1])
                value = [v for src in sides for v in from_dense(src, at, window, owner, HALO_COT)]
            back.put("ct", d, row, value)
        backward_rows(spread, past, back, d, table)


def back_far_kernel(rows, window, local, near, far, back_near, *refs):
    doses, groups = window.doses, window.groups
    sends = refs[:doses]
    mine, other, store, full = refs[doses:]
    halo = swap_layout(rows, window, local)[1]
    half = rows // 2
    total = local * doses
    owner = lax.axis_index("dose")
    layers = window.layers(HALO_COT)
    lead = window.size - layers
    spread = make_spread()
    past = Fields(rows, total, (near, near_rows), (far, far_rows))
    back = Fields(rows, total, (back_near, back_near_rows), (store, back_far_rows))
    table = back_far_rows(rows)
    for d in range(total):
        k, i = divmod(d, local)
        for row in range(*table["ct"]):
            at = lead + (i * HALO_COT + HALO_COT + row) * layers
            places = (at, at + halo)
            back.put("ct", d, row, [v for p in places for v in from_dense(sends[k], p, window, owner, HALO_COT)])
        backward_rows(spread, past, back, d, table)
    for row in range(half):
        value = back.get("g", 0, row)
        for d in range(1, total):
            value = [v + w for v, w in zip(value, back.get("g", d, row))]
        for i in range(2 * groups):
            side, k = divmod(i, groups)
            full[side, row, pl.ds(k, SUB, stride=groups), :] = value[i]
    start = pl.multiple_of(owner * window.piece - window.start(owner), SUB)
    for side, out in enumerate((mine, other)):
        for row in range(half):
            out[row] = full[side, row, pl.ds(start, window.piece), :]


def join_kernel(rows, piece, mine, other, out):
    core = lax.axis_index("ty")
    for owner, part in ((core, mine), (1 - core, other)):
        for row in range(rows // 2):
            at = row + owner * (rows - 1 - 2 * row)
            for g in range(0, piece, SUB):
                out[pl.ds(g * rows + at, SUB, stride=rows), :] = part[row, pl.ds(g, SUB), :]


def gradient(aerial_image, quencher, cotangent, dose_levels, dose_index):
    depth, rows, lanes = aerial_image.shape
    local = cotangent.shape[0]
    half = rows // 2
    doses = lax.axis_size("dose")
    ring = lax.axis_size("tx")
    assert rows == half + HALO_QUENCH and HALO_AERIAL == HALO_QUENCH + 1
    window = Window(depth, doses)
    groups, piece = window.groups, window.piece
    total = local * doses
    f32 = jnp.float32
    aerial = aerial_image.reshape(depth * rows, lanes)
    quench = quencher.reshape(depth * rows, lanes)
    cot = cotangent.reshape(local * depth * rows, lanes)

    def call(kernel, fixed, args, outs, scratch=(), flops=0, space=pltpu.VMEM):
        def body(*refs):
            kernel(*fixed, *refs)

        moved = sum(4 * x.size for x in list(args) + list(outs))
        return pl.pallas_call(
            body,
            out_shape=tuple(outs),
            in_specs=[pl.BlockSpec(memory_space=space)] * len(args),
            out_specs=(pl.BlockSpec(memory_space=pltpu.VMEM),) * len(outs),
            scratch_shapes=list(scratch),
            compiler_params=pltpu.CompilerParams(vmem_limit_bytes=LIMIT),
            cost_estimate=pl.CostEstimate(flops=flops, bytes_accessed=moved, transcendentals=0),
        )(*args)

    def array(*shape):
        return jax.ShapeDtypeStruct(shape + (lanes,), f32)

    def store(table):
        return (places_of(table(rows), total)[1], 2 * groups, SUB)

    def along(value, cross=0, step=1, k=0):
        pairs = []
        for t in range(ring):
            for c in range(2):
                for d in range(doses):
                    up = step * (1 - 2 * (c ^ cross))
                    target = (((t + up) % ring) * 2 + (c ^ cross)) * doses + (d + k) % doses
                    pairs.append(((t * 2 + c) * doses + d, target))
        return lax.ppermute(value, ("tx", "ty", "dose"), pairs)

    def across(value):
        return along(value, cross=1, step=0)

    images = array(dense_places(window, image_parts())[1])
    handed, halo = swap_layout(rows, window, local)
    whole = array(dense_places(window, cot_parts(local * rows))[1] + local * SUB)
    flat = [jax.ShapeDtypeStruct(x.shape, f32) for x in (aerial, quench, cot)]
    image_s, image_c, dose, aerial, quench, cot = call(
        image_kernel,
        (rows, window, local),
        [pltpu.with_memory_space_constraint(x, pltpu.HBM) for x in (aerial, quench, cot, dose_levels, dose_index)],
        [images, images, array(local, SUB)] + flat,
        [
            pltpu.SMEM(dose_levels.shape, f32),
            pltpu.SMEM(dose_index.shape, jnp.int32),
            pltpu.SemaphoreType.DMA((5,)),
        ],
        space=pltpu.HBM,
    )
    image_s = along(image_s)
    image_c = along(image_c, cross=1)
    rest = call(
        rest_kernel,
        (rows, window, local),
        (dose, aerial, quench, cot),
        [array(handed + doses * halo)] + [array(halo)] * doses + [whole] * (doses - 1),
    )
    swap = across(rest[0])
    values, wholes = [dose], []
    for k in range(1, doses):
        arrived = along(rest[doses + k], step=0, k=k)
        values.append(arrived)
        wholes += [arrived, across(arrived)]
    sends = []
    for k in range(doses):
        other = lax.slice_in_dim(swap, handed + k * halo, handed + (k + 1) * halo)
        both = jnp.concatenate((rest[1 + k], other), axis=0)
        sends.append(along(both, k=k))

    (near,) = call(
        near_kernel, (rows, window, local), values + [aerial, quench, swap], [array(*store(near_rows))], flops=10_000_000
    )
    extra_own = across(image_c)
    extra_par = across(image_s)
    (far,) = call(
        far_kernel, (rows, window, total), (near, image_s, image_c), [array(*store(far_rows))], flops=10_000_000
    )
    (back_near,) = call(
        back_near_kernel,
        (rows, window, local),
        [near, far, extra_own, extra_par, cot, swap] + wholes,
        [array(*store(back_near_rows))],
        flops=10_000_000,
    )
    mine, other = call(
        back_far_kernel,
        (rows, window, local),
        [near, far, back_near] + sends,
        [array(half, piece)] * 2,
        [
            pltpu.VMEM(store(back_far_rows) + (lanes,), f32),
            pltpu.VMEM((2, half, window.size, lanes), f32),
        ],
        flops=10_000_000,
    )
    other = across(other)
    (out,) = call(join_kernel, (rows, piece), (mine, other), [array(piece * rows)])
    return out.reshape(piece, rows, lanes)


def solution(mesh):
    placed = (
        P("focus", "tx", "ty"),
        P(None, "tx", "ty"),
        P(("focus", "dose"), None, "tx", "ty"),
        P(),
        P(("focus", "dose")),
    )
    return jax.shard_map(
        gradient,
        mesh=mesh,
        in_specs=placed,
        out_specs=P(("focus", "dose"), "tx", "ty"),
        check_vma=False,
    )
```

```python
import jax
import jax.numpy as jnp
from jax import lax
from jax.experimental import pallas as pl
from jax.experimental.pallas import tpu as pltpu
from jax.sharding import PartitionSpec as P


exposure_rate = 1.0
neutral_rate = 0.8
deprotect_rate = 0.5
acid_lateral = 0.23
acid_depth = 0.02
base_lateral = 0.2
base_depth = 0.02

HALO_AERIAL = 5
HALO_QUENCH = 4
HALO_COT = 3
SUB = 8
LIMIT = 20 << 20


class Window:
    def __init__(self, depth, doses):
        self.depth, self.doses = depth, doses
        self.piece = depth // doses
        self.ends = 0 if doses == 1 else 1 if doses == 2 else 2
        self.size = min(depth, self.piece + SUB * self.ends)
        self.groups = self.size // SUB

    def layers(self, halo):
        return min(self.depth, self.piece + halo * self.ends)

    def clamp(self, owner, halo, size):
        return jnp.minimum(jnp.maximum(owner * self.piece - halo, 0), self.depth - size)

    def start(self, owner):
        return self.clamp(owner, SUB, self.size)

    def sent(self, owner, halo):
        return self.clamp(owner, halo, self.layers(halo))


class Dense:
    def __init__(self, window, reaches, lead=True, tail=True, size=0):
        self.window = window
        slack = [window.size - window.layers(reach) for reach in reaches]
        used = sum(window.layers(reach) for reach in reaches)
        ends = (slack[0] if lead else 0) + (slack[-1] if tail else 0)
        self.size = max(size, -(-(used + ends) // SUB) * SUB)
        at = self.size - used if lead and not tail else slack[0] if lead else 0
        self.rows = []
        for reach in reaches:
            self.rows.append((at, reach))
            at += window.layers(reach)

    def put(self, dst, i, src, base, rows, row, owner, block=0):
        at, reach = self.rows[i]
        first, layers = self.window.sent(owner, reach), self.window.layers(reach)
        for g in range(0, layers, SUB):
            n = min(SUB, layers - g)
            value = src[pl.ds(base + rows * (first + g) + row, n, stride=rows), :]
            dst[pl.ds(block + at + g, n), :] = value

    def get(self, src, i, owner, block=0):
        at, reach = self.rows[i]
        window = self.window
        start = block + at - (window.sent(owner, reach) - window.start(owner))
        return [src[pl.ds(start + k, SUB, stride=window.groups), :] for k in range(window.groups)]


def clear(dst, at, size):
    dst[pl.ds(at, size), :] = jnp.zeros((size, dst.shape[1]), jnp.float32)


def image_layout(window):
    aerial = [HALO_AERIAL - i for i in range(1, HALO_AERIAL + 1)]
    quench = [HALO_QUENCH - i for i in range(HALO_QUENCH, 0, -1)]
    return Dense(window, aerial + quench)


def halo_layouts(window, local):
    reaches = [HALO_COT - i for _ in range(local) for i in range(1, HALO_COT + 1)]
    size = Dense(window, reaches, lead=False).size
    first = Dense(window, reaches, tail=False, size=size)
    return first, Dense(window, reaches, lead=False, size=first.size)


def whole_layout(rows, window, local):
    return Dense(window, [HALO_COT] * (local * rows))


def chip_row(rows, row):
    return row + lax.axis_index("ty") * (rows - 1 - 2 * row)


def vector(ref, rows, groups, first, row, base=0):
    return ref[pl.ds(base + rows * first + row, SUB, stride=rows * groups), :]


def image_kernel(rows, window, local, *refs):
    image_hbm, quench_hbm, cot_hbm, levels_hbm, index_hbm = refs[:5]
    image_s, image_c, dose, aerial, quench, cot, levels, index, sems = refs[5:]
    pairs = ((image_hbm, aerial), (quench_hbm, quench), (cot_hbm, cot), (levels_hbm, levels), (index_hbm, index))
    copies = [pltpu.make_async_copy(src, dst, sems.at[i]) for i, (src, dst) in enumerate(pairs)]
    for copy in copies:
        copy.start()
    layout = image_layout(window)
    for ref in (image_s, image_c):
        clear(ref, 0, SUB)
        clear(ref, layout.size - 2 * SUB, 2 * SUB)
    owner = lax.axis_index("dose")
    copies[0].wait()
    copies[1].wait()
    order = [(aerial, i) for i in range(1, HALO_AERIAL + 1)]
    order += [(quench, i) for i in range(HALO_QUENCH, 0, -1)]
    for place, (src, i) in enumerate(order):
        layout.put(image_s, place, src, 0, rows, chip_row(rows, rows - i), owner)
        layout.put(image_c, place, src, 0, rows, chip_row(rows, i - 1), owner)
    for copy in copies[2:]:
        copy.wait()
    for d in range(local):
        dose[d] = jnp.full(dose.shape[1:], levels[index[d]], jnp.float32)


def swap_layout(rows, window, local):
    vectors = 2 * rows + local * (rows // 2 + HALO_COT)
    return vectors * window.groups * SUB, halo_layouts(window, local)[0].size


def swapped(swap, groups, place):
    return [swap[pl.ds((place * groups + k) * SUB, SUB), :] for k in range(groups)]


def rest_kernel(rows, window, local, aerial, quench, cot, swap, *dense):
    depth, groups, doses = window.depth, window.groups, window.doses
    area = rows * depth
    inner = rows // 2 + HALO_COT
    owner = lax.axis_index("dose")
    sends = dense[:doses]
    wholes = dense[doses:]
    handed, halo = swap_layout(rows, window, local)
    layouts = halo_layouts(window, local)
    whole = whole_layout(rows, window, local)
    for k in range(doses):
        target = lax.rem(owner + k, doses)
        block = handed + k * halo
        mine, given = layouts if k % 2 == 0 else layouts[::-1]
        for ref, at in ((sends[k], 0), (swap, block)):
            clear(ref, at, 2 * SUB)
            clear(ref, at + halo - 2 * SUB, 2 * SUB)
        for d in range(local):
            for i in range(1, HALO_COT + 1):
                outer, inward = chip_row(rows, rows - i), chip_row(rows, i - 1)
                if k % 2:
                    outer, inward = inward, outer
                place = d * HALO_COT + i - 1
                mine.put(sends[k], place, cot, d * area, rows, outer, target)
                given.put(swap, place, cot, d * area, rows, inward, target, block)
        if k:
            ref = wholes[k - 1]
            clear(ref, 0, SUB)
            clear(ref, whole.size - 2 * SUB, 2 * SUB)
            for d in range(local):
                for row in range(rows):
                    whole.put(ref, d * rows + row, cot, d * area, rows, row, target)
    place = 0
    parts = [(aerial, 0, rows), (quench, 0, rows)] + [(cot, d * area, inner) for d in range(local)]
    start = window.start(owner)
    for src, base, width in parts:
        for i in range(width):
            for k in range(groups):
                value = vector(src, rows, groups, start + k, chip_row(rows, rows - 1 - i), base)
                swap[pl.ds((place * groups + k) * SUB, SUB), :] = value
            place += 1


def make_spread():
    lane = lax.broadcasted_iota(jnp.int32, (SUB, 128), 1)
    sub = lax.broadcasted_iota(jnp.int32, (SUB, 128), 0)
    first_lane = lane == 0
    last_lane = lane == 127
    first_sub = sub == 0
    last_sub = sub == SUB - 1

    def spread(above, center, below, along, depthwise):
        count = len(center)
        groups = count // 2
        keep = 1.0 - 4.0 * along - 2.0 * depthwise
        result = []
        for i in range(count):
            k = i % groups
            j = (i + groups) % count
            right = pltpu.roll(jnp.where(first_lane, center[j], center[i]), 127, 1)
            left = pltpu.roll(jnp.where(last_lane, center[j], center[i]), 1, 1)
            lateral = (above[i] + below[i]) + (right + left)
            if k + 1 < groups:
                deeper = center[i + 1]
            else:
                deeper = jnp.where(last_sub, center[i], pltpu.roll(center[i - k], SUB - 1, 0))
            if k > 0:
                higher = center[i - 1]
            else:
                higher = jnp.where(first_sub, center[i], pltpu.roll(center[i + groups - 1], 1, 0))
            result.append(keep * center[i] + along * lateral + depthwise * (deeper + higher))
        return result

    return spread


def near_rows(rows):
    half = rows // 2
    return {
        "q0": (0, rows),
        "a0": (0, rows),
        "a1": (1, rows - 1),
        "a2": (2, rows - 2),
        "a3": (3, rows - 3),
        "q1": (1, rows - 1),
        "q2": (2, rows - 2),
        "c3": (2, half + 3),
        "c2": (3, half + 2),
        "c1": (3, half + 1),
        "c0": (3, half),
        "e": (0, half),
        "dose": (0, 1),
    }


def far_rows(rows):
    return {
        "q0": (-4, 0),
        "a0": (-5, 0),
        "a1": (-4, 1),
        "a2": (-3, 2),
        "a3": (-2, 3),
        "q1": (-3, 1),
        "q2": (-2, 2),
        "c3": (-3, 2),
        "c2": (-2, 3),
        "c1": (-1, 3),
        "c0": (0, 3),
    }


def places_of(table, local):
    places, total = {}, 0
    for name, (first, end) in table.items():
        for d in range(local):
            for row in range(first, end):
                if name == "q0" and d > 0:
                    places[name, d, row] = places[name, 0, row]
                else:
                    places[name, d, row] = total
                    total += 1
    return places, total


def back_near_rows(rows):
    half = rows // 2
    return {
        "ct": (0, half + 3),
        "l3": (0, half + 3),
        "l2": (1, half + 2),
        "m2": (0, half + 1),
        "l1": (2, half + 1),
        "m1": (1, half),
        "g": (3, half),
    }


def back_far_rows(rows):
    return {
        "ct": (-3, 0),
        "l3": (-3, 0),
        "l2": (-2, 1),
        "m2": (-1, 0),
        "l1": (-1, 2),
        "m1": (0, 1),
        "g": (0, 3),
    }


class Fields:
    def __init__(self, rows, local, *stores):
        self.stores = [(ref, places_of(table(rows), local)[0]) for ref, table in stores]
        self.more = {}

    def get(self, name, d, row):
        if (name, d, row) in self.more:
            return self.more[name, d, row]
        for ref, places in self.stores:
            if (name, d, row) in places:
                at = places[name, d, row]
                return [ref[at, i] for i in range(ref.shape[1])]
        raise KeyError((name, row))

    def around(self, name, d, row):
        return [self.get(name, d, row + i) for i in (-1, 0, 1)]

    def put(self, name, d, row, value):
        ref, places = self.stores[-1]
        at = places[name, d, row]
        for i in range(len(value)):
            ref[at, i] = value[i]


def left_of(acid):
    return [1.0 - deprotect_rate * v for v in acid]


def next_acid(spread, fields, d, n, row):
    name = "a%d" % n
    above, center, below = fields.around(name, d, row)
    quench = fields.get("q%d" % n, d, row)
    new = spread(above, center, below, acid_lateral, acid_depth)
    reaction = [neutral_rate * a * q for a, q in zip(center, quench)]
    return [v - r for v, r in zip(new, reaction)], reaction


def forward_rows(spread, fields, d, table):
    for n in range(3):
        first, end = table["a%d" % (n + 1)]
        for row in range(first, end):
            new, reaction = next_acid(spread, fields, d, n, row)
            fields.put("a%d" % (n + 1), d, row, new)
            if n < 2:
                q_first, q_end = table["q%d" % (n + 1)]
                if q_first <= row < q_end:
                    name = "q%d" % n
                    new = spread(*fields.around(name, d, row), base_lateral, base_depth)
                    fields.put("q%d" % (n + 1), d, row, [v - r for v, r in zip(new, reaction)])

    first = min(table[c][0] for c in ("c3", "c2", "c1", "c0"))
    end = max(table[c][1] for c in ("c3", "c2", "c1", "c0"))
    for row in range(first, end):
        wanted = [n for n in range(4) if table["c%d" % n][0] <= row < table["c%d" % n][1]]
        left = {}

        def of(n):
            if n not in left:
                left[n] = left_of(fields.get("a%d" % n, d, row))
            return left[n]

        for n in wanted:
            parts = [m for m in range(4) if m != n]
            if n >= 2 and table["e"][1] > 0 and row == table["c%d" % n][1] - 1:
                parts = parts[:2]
            value = [(-deprotect_rate) * v for v in of(parts[0])]
            for m in parts[1:]:
                value = [v * w for v, w in zip(value, of(m))]
            fields.put("c%d" % n, d, row, value)


def near_kernel(rows, window, local, *refs):
    doses, groups = window.doses, window.groups
    dose_refs, (aerial, quench, swap, near) = refs[:doses], refs[doses:]
    half = rows // 2
    spread = make_spread()
    total = local * doses
    fields = Fields(rows, total, (near, near_rows))
    start = window.start(lax.axis_index("dose"))

    def source(raw, at, row):
        own = [vector(raw, rows, groups, start + k, chip_row(rows, row)) for k in range(groups)]
        return own + swapped(swap, groups, at + row)

    for row in range(rows):
        fields.put("q0", 0, row, source(quench, rows, row))
    for d in range(total):
        dose = dose_refs[d // local][d % local]
        fields.put("dose", d, 0, [dose] * (2 * groups))
        rate = -exposure_rate * dose
        for row in range(rows):
            absorbed = [jnp.exp(rate * v) for v in source(aerial, 0, row)]
            fields.put("a0", d, row, [1.0 - v for v in absorbed])
            if row < half:
                fields.put("e", d, row, [exposure_rate * dose * v for v in absorbed])
        forward_rows(spread, fields, d, near_rows(rows))


def far_kernel(rows, window, total, near, image_s, image_c, far):
    spread = make_spread()
    fields = Fields(rows, total, (near, near_rows), (far, far_rows))
    table = dict(far_rows(rows), e=(0, 0))
    owner = lax.axis_index("dose")
    layout = image_layout(window)

    def source(place):
        return [v for src in (image_s, image_c) for v in layout.get(src, place, owner)]

    for row in range(-HALO_QUENCH, 0):
        fields.put("q0", 0, row, source(HALO_AERIAL + HALO_QUENCH + row))
    for d in range(total):
        rate = -exposure_rate * fields.get("dose", d, 0)[0]
        for row in range(-HALO_AERIAL, 0):
            fields.put("a0", d, row, [1.0 - jnp.exp(rate * v) for v in source(-1 - row)])
        forward_rows(spread, fields, d, table)


def backward_rows(spread, past, back, d, table):
    def step(name, row, both, n):
        new = spread(*back.around(name, d, row), acid_lateral, acid_depth)
        parts = zip(new, past.get("q%d" % n, d, row), both, past.get("c%d" % n, d, row), back.get("ct", d, row))
        return [v - q * (neutral_rate * s) + c * t for v, q, s, c, t in parts]

    for row in range(*table["l3"]):
        back.put("l3", d, row, [c * v for c, v in zip(past.get("c3", d, row), back.get("ct", d, row))])
    for row in range(*table["m2"]):
        parts = zip(past.get("a2", d, row), back.get("l3", d, row))
        back.put("m2", d, row, [-(neutral_rate * a * s) for a, s in parts])
    for row in range(*table["l2"]):
        back.put("l2", d, row, step("l3", row, back.get("l3", d, row), 2))
    for n, name in ((1, "l1"), (0, "g")):
        old, side = ("l2", "m2") if n else ("l1", "m1")
        wanted = set(range(*table[name]))
        if n:
            wanted |= set(range(*table["m1"]))
        for row in sorted(wanted):
            both = [a + b for a, b in zip(back.get(old, d, row), back.get(side, d, row))]
            if row in range(*table[name]):
                new = step(old, row, both, n)
                if n == 0:
                    new = [v * e for v, e in zip(new, past.get("e", d, row))]
                back.put(name, d, row, new)
            if n and row in range(*table["m1"]):
                new = spread(*back.around("m2", d, row), base_lateral, base_depth)
                parts = zip(new, past.get("a1", d, row), both)
                back.put("m1", d, row, [v - a * (neutral_rate * s) for v, a, s in parts])


def back_near_kernel(rows, window, local, near, far, extra_own, extra_par, cot, swap, *refs):
    doses, groups = window.doses, window.groups
    wholes, back_near = refs[:-1], refs[-1]
    half = rows // 2
    area = rows * window.depth
    inner = half + HALO_COT
    total = local * doses
    spread = make_spread()
    owner = lax.axis_index("dose")
    start = window.start(owner)
    image = image_layout(window)
    whole = whole_layout(rows, window, local)
    for d in range(total):
        past = Fields(rows, total, (near, near_rows), (far, far_rows))
        rate = -exposure_rate * past.get("dose", d, 0)[0]
        light = [v for src in (extra_own, extra_par) for v in image.get(src, 0, owner)]
        past.more["a0", d, rows] = [1.0 - jnp.exp(rate * v) for v in light]
        for n in range(3):
            row = rows - 1 - n
            past.more["a%d" % (n + 1), d, row] = next_acid(spread, past, d, n, row)[0]
        for n, row in ((3, half + 2), (2, half + 1)):
            left = left_of(past.get("a%d" % (5 - n), d, row))
            past.more["c%d" % n, d, row] = [v * m for v, m in zip(past.get("c%d" % n, d, row), left)]
        back = Fields(rows, total, (back_near, back_near_rows))
        table = back_near_rows(rows)
        k, i = divmod(d, local)
        for row in range(*table["ct"]):
            if k == 0:
                value = [vector(cot, rows, groups, start + g, chip_row(rows, row), i * area) for g in range(groups)]
                value += swapped(swap, groups, 2 * rows + i * inner + row)
            else:
                at = chip_row(rows, row) * window.layers(HALO_COT)
                sides = (wholes[2 * k - 2], wholes[2 * k - 1])
                value = [v for src in sides for v in whole.get(src, i * rows, owner, at)]
            back.put("ct", d, row, value)
        backward_rows(spread, past, back, d, table)


def back_far_kernel(rows, window, local, near, far, back_near, *refs):
    doses, groups = window.doses, window.groups
    sends = refs[:doses]
    mine, other, store, full = refs[doses:]
    layouts = halo_layouts(window, local)
    half = rows // 2
    total = local * doses
    owner = lax.axis_index("dose")
    spread = make_spread()
    past = Fields(rows, total, (near, near_rows), (far, far_rows))
    back = Fields(rows, total, (back_near, back_near_rows), (store, back_far_rows))
    table = back_far_rows(rows)
    for d in range(total):
        k, i = divmod(d, local)
        for row in range(*table["ct"]):
            place = i * HALO_COT - 1 - row
            value = layouts[0].get(sends[k], place, owner)
            back.put("ct", d, row, value + layouts[1].get(sends[k], place, owner, layouts[0].size))
        backward_rows(spread, past, back, d, table)
    for row in range(half):
        value = back.get("g", 0, row)
        for d in range(1, total):
            value = [v + w for v, w in zip(value, back.get("g", d, row))]
        for i in range(2 * groups):
            side, k = divmod(i, groups)
            full[side, row, pl.ds(k, SUB, stride=groups), :] = value[i]
    start = pl.multiple_of(owner * window.piece - window.start(owner), SUB)
    for side, out in enumerate((mine, other)):
        for row in range(half):
            out[row] = full[side, row, pl.ds(start, window.piece), :]


def join_kernel(rows, piece, mine, other, out):
    core = lax.axis_index("ty")
    for owner, part in ((core, mine), (1 - core, other)):
        for row in range(rows // 2):
            at = row + owner * (rows - 1 - 2 * row)
            for g in range(0, piece, SUB):
                out[pl.ds(g * rows + at, SUB, stride=rows), :] = part[row, pl.ds(g, SUB), :]


def gradient(aerial_image, quencher, cotangent, dose_levels, dose_index):
    depth, rows, lanes = aerial_image.shape
    local = cotangent.shape[0]
    half = rows // 2
    doses = lax.axis_size("dose")
    ring = lax.axis_size("tx")
    assert rows == half + HALO_QUENCH and HALO_AERIAL == HALO_QUENCH + 1
    window = Window(depth, doses)
    groups, piece = window.groups, window.piece
    total = local * doses
    f32 = jnp.float32
    aerial = aerial_image.reshape(depth * rows, lanes)
    quench = quencher.reshape(depth * rows, lanes)
    cot = cotangent.reshape(local * depth * rows, lanes)

    def call(kernel, fixed, args, outs, scratch=(), flops=0, space=pltpu.VMEM):
        def body(*refs):
            kernel(*fixed, *refs)

        moved = sum(4 * x.size for x in list(args) + list(outs))
        return pl.pallas_call(
            body,
            out_shape=tuple(outs),
            in_specs=[pl.BlockSpec(memory_space=space)] * len(args),
            out_specs=(pl.BlockSpec(memory_space=pltpu.VMEM),) * len(outs),
            scratch_shapes=list(scratch),
            compiler_params=pltpu.CompilerParams(vmem_limit_bytes=LIMIT),
            cost_estimate=pl.CostEstimate(flops=flops, bytes_accessed=moved, transcendentals=0),
        )(*args)

    def array(*shape):
        return jax.ShapeDtypeStruct(shape + (lanes,), f32)

    def store(table):
        return (places_of(table(rows), total)[1], 2 * groups, SUB)

    def along(value, cross=0, step=1, k=0):
        pairs = []
        for t in range(ring):
            for c in range(2):
                for d in range(doses):
                    up = step * (1 - 2 * (c ^ cross))
                    target = (((t + up) % ring) * 2 + (c ^ cross)) * doses + (d + k) % doses
                    pairs.append(((t * 2 + c) * doses + d, target))
        return lax.ppermute(value, ("tx", "ty", "dose"), pairs)

    def across(value):
        return along(value, cross=1, step=0)

    images = array(image_layout(window).size)
    handed, halo = swap_layout(rows, window, local)
    whole = array(whole_layout(rows, window, local).size)
    flat = [jax.ShapeDtypeStruct(x.shape, f32) for x in (aerial, quench, cot)]
    image_s, image_c, dose, aerial, quench, cot = call(
        image_kernel,
        (rows, window, local),
        [pltpu.with_memory_space_constraint(x, pltpu.HBM) for x in (aerial, quench, cot, dose_levels, dose_index)],
        [images, images, array(local, SUB)] + flat,
        [
            pltpu.SMEM(dose_levels.shape, f32),
            pltpu.SMEM(dose_index.shape, jnp.int32),
            pltpu.SemaphoreType.DMA((5,)),
        ],
        space=pltpu.HBM,
    )
    image_s = along(image_s)
    image_c = along(image_c, cross=1)
    rest = call(
        rest_kernel,
        (rows, window, local),
        (aerial, quench, cot),
        [array(handed + doses * halo)] + [array(halo)] * doses + [whole] * (doses - 1),
    )
    swap = across(rest[0])
    values, wholes = [dose], []
    for k in range(1, doses):
        arrived = along(rest[doses + k], step=0, k=k)
        values.append(along(dose, step=0, k=k))
        wholes += [arrived, across(arrived)]
    sends = []
    for k in range(doses):
        other = lax.slice_in_dim(swap, handed + k * halo, handed + (k + 1) * halo)
        both = jnp.concatenate((other, rest[1 + k]) if k % 2 else (rest[1 + k], other), axis=0)
        sends.append(along(both, cross=k % 2, k=k))

    (near,) = call(
        near_kernel, (rows, window, local), values + [aerial, quench, swap], [array(*store(near_rows))], flops=10_000_000
    )
    extra_own = across(image_c)
    extra_par = across(image_s)
    (far,) = call(
        far_kernel, (rows, window, total), (near, image_s, image_c), [array(*store(far_rows))], flops=10_000_000
    )
    (back_near,) = call(
        back_near_kernel,
        (rows, window, local),
        [near, far, extra_own, extra_par, cot, swap] + wholes,
        [array(*store(back_near_rows))],
        flops=10_000_000,
    )
    mine, other = call(
        back_far_kernel,
        (rows, window, local),
        [near, far, back_near] + sends,
        [array(half, piece)] * 2,
        [
            pltpu.VMEM(store(back_far_rows) + (lanes,), f32),
            pltpu.VMEM((2, half, window.size, lanes), f32),
        ],
        flops=10_000_000,
    )
    other = across(other)
    (out,) = call(join_kernel, (rows, piece), (mine, other), [array(piece * rows)])
    return out.reshape(piece, rows, lanes)


def solution(mesh):
    placed = (
        P("focus", "tx", "ty"),
        P(None, "tx", "ty"),
        P(("focus", "dose"), None, "tx", "ty"),
        P(),
        P(("focus", "dose")),
    )
    return jax.shard_map(
        gradient,
        mesh=mesh,
        in_specs=placed,
        out_specs=P(("focus", "dose"), "tx", "ty"),
        check_vma=False,
    )
```

```python
import jax
import jax.numpy as jnp
from jax import lax
from jax.experimental import pallas as pl
from jax.experimental.pallas import tpu as pltpu
from jax.sharding import PartitionSpec as P


exposure_rate = 1.0
neutral_rate = 0.8
deprotect_rate = 0.5
acid_lateral = 0.23
acid_depth = 0.02
base_lateral = 0.2
base_depth = 0.02

HALO_AERIAL = 5
HALO_QUENCH = 4
HALO_COT = 3
SUB = 8
LIMIT = 20 << 20


class Window:
    def __init__(self, depth, doses):
        self.depth, self.doses = depth, doses
        self.piece = depth // doses
        self.ends = 0 if doses == 1 else 1 if doses == 2 else 2
        self.size = min(depth, self.piece + SUB * self.ends)
        self.groups = self.size // SUB

    def layers(self, halo):
        return min(self.depth, self.piece + halo * self.ends)

    def clamp(self, owner, halo, size):
        return jnp.minimum(jnp.maximum(owner * self.piece - halo, 0), self.depth - size)

    def start(self, owner):
        return self.clamp(owner, SUB, self.size)

    def sent(self, owner, halo):
        return self.clamp(owner, halo, self.layers(halo))


class Dense:
    def __init__(self, window, reaches, lead=True, tail=True, size=0):
        self.window = window
        slack = [window.size - window.layers(reach) for reach in reaches]
        used = sum(window.layers(reach) for reach in reaches)
        ends = (slack[0] if lead else 0) + (slack[-1] if tail else 0)
        self.size = max(size, -(-(used + ends) // SUB) * SUB)
        at = self.size - used if lead and not tail else slack[0] if lead else 0
        self.rows = []
        for reach in reaches:
            self.rows.append((at, reach))
            at += window.layers(reach)

    def put(self, dst, i, src, base, rows, row, owner, block=0):
        at, reach = self.rows[i]
        first, layers = self.window.sent(owner, reach), self.window.layers(reach)
        for g in range(0, layers, SUB):
            n = min(SUB, layers - g)
            value = src[pl.ds(base + rows * (first + g) + row, n, stride=rows), :]
            dst[pl.ds(block + at + g, n), :] = value

    def get(self, src, i, owner, block=0):
        at, reach = self.rows[i]
        window = self.window
        start = block + at - (window.sent(owner, reach) - window.start(owner))
        return [src[pl.ds(start + k, SUB, stride=window.groups), :] for k in range(window.groups)]


def clear(dst, at, size):
    dst[pl.ds(at, size), :] = jnp.zeros((size, dst.shape[1]), jnp.float32)


def image_layout(window):
    aerial = [HALO_AERIAL - i for i in range(1, HALO_AERIAL + 1)]
    quench = [HALO_QUENCH - i for i in range(HALO_QUENCH, 0, -1)]
    return Dense(window, aerial + quench)


def crosses(k):
    return k % 2 == 0


def halo_layouts(window, local):
    reaches = [HALO_COT - i for _ in range(local) for i in range(1, HALO_COT + 1)]
    size = Dense(window, reaches, lead=False).size
    first = Dense(window, reaches, tail=False, size=size)
    return first, Dense(window, reaches, lead=False, size=first.size)


def whole_layout(rows, window, local):
    return Dense(window, [HALO_COT] * (local * rows))


def chip_row(rows, row):
    return row + lax.axis_index("ty") * (rows - 1 - 2 * row)


def vector(ref, rows, groups, first, row, base=0):
    return ref[pl.ds(base + rows * first + row, SUB, stride=rows * groups), :]


def image_kernel(rows, window, local, *refs):
    image_hbm, quench_hbm, cot_hbm, levels_hbm, index_hbm = refs[:5]
    image_s, image_c, dose, aerial, quench, cot, levels, index, sems = refs[5:]
    pairs = ((image_hbm, aerial), (quench_hbm, quench), (cot_hbm, cot), (levels_hbm, levels), (index_hbm, index))
    copies = [pltpu.make_async_copy(src, dst, sems.at[i]) for i, (src, dst) in enumerate(pairs)]
    for copy in copies:
        copy.start()
    layout = image_layout(window)
    for ref in (image_s, image_c):
        clear(ref, 0, SUB)
        clear(ref, layout.size - 2 * SUB, 2 * SUB)
    owner = lax.axis_index("dose")
    copies[0].wait()
    copies[1].wait()
    order = [(aerial, i) for i in range(1, HALO_AERIAL + 1)]
    order += [(quench, i) for i in range(HALO_QUENCH, 0, -1)]
    for place, (src, i) in enumerate(order):
        layout.put(image_s, place, src, 0, rows, chip_row(rows, rows - i), owner)
        layout.put(image_c, place, src, 0, rows, chip_row(rows, i - 1), owner)
    for copy in copies[2:]:
        copy.wait()
    for d in range(local):
        dose[d] = jnp.full(dose.shape[1:], levels[index[d]], jnp.float32)


def swap_layout(rows, window, local):
    vectors = 2 * rows + local * (rows // 2 + HALO_COT)
    return vectors * window.groups * SUB, halo_layouts(window, local)[0].size


def swapped(swap, groups, place):
    return [swap[pl.ds((place * groups + k) * SUB, SUB), :] for k in range(groups)]


def rest_kernel(rows, window, local, aerial, quench, cot, swap, *dense):
    depth, groups, doses = window.depth, window.groups, window.doses
    area = rows * depth
    inner = rows // 2 + HALO_COT
    owner = lax.axis_index("dose")
    sends = dense[:doses]
    wholes = dense[doses:]
    handed, halo = swap_layout(rows, window, local)
    layouts = halo_layouts(window, local)
    whole = whole_layout(rows, window, local)
    for k in range(doses):
        target = lax.rem(owner + k, doses)
        block = handed + k * halo
        mine, given = layouts[::-1] if crosses(k) else layouts
        for ref, at in ((sends[k], 0), (swap, block)):
            clear(ref, at, 2 * SUB)
            clear(ref, at + halo - 2 * SUB, 2 * SUB)
        for d in range(local):
            for i in range(1, HALO_COT + 1):
                outer, inward = chip_row(rows, rows - i), chip_row(rows, i - 1)
                if crosses(k):
                    outer, inward = inward, outer
                place = d * HALO_COT + i - 1
                mine.put(sends[k], place, cot, d * area, rows, outer, target)
                given.put(swap, place, cot, d * area, rows, inward, target, block)
        if k:
            ref = wholes[k - 1]
            clear(ref, 0, SUB)
            clear(ref, whole.size - 2 * SUB, 2 * SUB)
            for d in range(local):
                for row in range(rows):
                    whole.put(ref, d * rows + row, cot, d * area, rows, row, target)
    place = 0
    parts = [(aerial, 0, rows), (quench, 0, rows)] + [(cot, d * area, inner) for d in range(local)]
    start = window.start(owner)
    for src, base, width in parts:
        for i in range(width):
            for k in range(groups):
                value = vector(src, rows, groups, start + k, chip_row(rows, rows - 1 - i), base)
                swap[pl.ds((place * groups + k) * SUB, SUB), :] = value
            place += 1


def make_spread():
    lane = lax.broadcasted_iota(jnp.int32, (SUB, 128), 1)
    sub = lax.broadcasted_iota(jnp.int32, (SUB, 128), 0)
    first_lane = lane == 0
    last_lane = lane == 127
    first_sub = sub == 0
    last_sub = sub == SUB - 1

    def spread(above, center, below, along, depthwise):
        count = len(center)
        groups = count // 2
        keep = 1.0 - 4.0 * along - 2.0 * depthwise
        result = []
        for i in range(count):
            k = i % groups
            j = (i + groups) % count
            right = pltpu.roll(jnp.where(first_lane, center[j], center[i]), 127, 1)
            left = pltpu.roll(jnp.where(last_lane, center[j], center[i]), 1, 1)
            lateral = (above[i] + below[i]) + (right + left)
            if k + 1 < groups:
                deeper = center[i + 1]
            else:
                deeper = jnp.where(last_sub, center[i], pltpu.roll(center[i - k], SUB - 1, 0))
            if k > 0:
                higher = center[i - 1]
            else:
                higher = jnp.where(first_sub, center[i], pltpu.roll(center[i + groups - 1], 1, 0))
            result.append(keep * center[i] + along * lateral + depthwise * (deeper + higher))
        return result

    return spread


def near_rows(rows):
    half = rows // 2
    return {
        "q0": (0, rows),
        "a0": (0, rows),
        "a1": (1, rows - 1),
        "a2": (2, rows - 2),
        "a3": (3, rows - 3),
        "q1": (1, rows - 1),
        "q2": (2, rows - 2),
        "c3": (2, half + 3),
        "c2": (3, half + 2),
        "c1": (3, half + 1),
        "c0": (3, half),
        "e": (0, half),
        "dose": (0, 1),
    }


def far_rows(rows):
    return {
        "q0": (-4, 0),
        "a0": (-5, 0),
        "a1": (-4, 1),
        "a2": (-3, 2),
        "a3": (-2, 3),
        "q1": (-3, 1),
        "q2": (-2, 2),
        "c3": (-3, 2),
        "c2": (-2, 3),
        "c1": (-1, 3),
        "c0": (0, 3),
    }


def places_of(table, local):
    places, total = {}, 0
    for name, (first, end) in table.items():
        for d in range(local):
            for row in range(first, end):
                if name == "q0" and d > 0:
                    places[name, d, row] = places[name, 0, row]
                else:
                    places[name, d, row] = total
                    total += 1
    return places, total


def back_near_rows(rows):
    half = rows // 2
    return {
        "ct": (0, half + 3),
        "l3": (0, half + 3),
        "l2": (1, half + 2),
        "m2": (0, half + 1),
        "l1": (2, half + 1),
        "m1": (1, half),
        "g": (3, half),
    }


def back_far_rows(rows):
    return {
        "ct": (-3, 0),
        "l3": (-3, 0),
        "l2": (-2, 1),
        "m2": (-1, 0),
        "l1": (-1, 2),
        "m1": (0, 1),
        "g": (0, 3),
    }


class Fields:
    def __init__(self, rows, *stores):
        self.stores = [(ref, places_of(table(rows), count)[0], first) for ref, table, first, count in stores]
        self.more = {}

    def get(self, name, d, row):
        if (name, d, row) in self.more:
            return self.more[name, d, row]
        for ref, places, first in self.stores:
            if (name, d - first, row) in places:
                at = places[name, d - first, row]
                return [ref[at, i] for i in range(ref.shape[1])]
        raise KeyError((name, row))

    def around(self, name, d, row):
        return [self.get(name, d, row + i) for i in (-1, 0, 1)]

    def put(self, name, d, row, value):
        ref, places, first = self.stores[-1]
        at = places[name, d - first, row]
        for i in range(len(value)):
            ref[at, i] = value[i]


def left_of(acid):
    return [1.0 - deprotect_rate * v for v in acid]


def next_acid(spread, fields, d, n, row):
    name = "a%d" % n
    above, center, below = fields.around(name, d, row)
    quench = fields.get("q%d" % n, d, row)
    new = spread(above, center, below, acid_lateral, acid_depth)
    reaction = [neutral_rate * a * q for a, q in zip(center, quench)]
    return [v - r for v, r in zip(new, reaction)], reaction


def forward_rows(spread, fields, d, table):
    for n in range(3):
        first, end = table["a%d" % (n + 1)]
        for row in range(first, end):
            new, reaction = next_acid(spread, fields, d, n, row)
            fields.put("a%d" % (n + 1), d, row, new)
            if n < 2:
                q_first, q_end = table["q%d" % (n + 1)]
                if q_first <= row < q_end:
                    name = "q%d" % n
                    new = spread(*fields.around(name, d, row), base_lateral, base_depth)
                    fields.put("q%d" % (n + 1), d, row, [v - r for v, r in zip(new, reaction)])

    first = min(table[c][0] for c in ("c3", "c2", "c1", "c0"))
    end = max(table[c][1] for c in ("c3", "c2", "c1", "c0"))
    for row in range(first, end):
        wanted = [n for n in range(4) if table["c%d" % n][0] <= row < table["c%d" % n][1]]
        left = {}

        def of(n):
            if n not in left:
                left[n] = left_of(fields.get("a%d" % n, d, row))
            return left[n]

        for n in wanted:
            parts = [m for m in range(4) if m != n]
            if n >= 2 and table["e"][1] > 0 and row == table["c%d" % n][1] - 1:
                parts = parts[:2]
            value = [(-deprotect_rate) * v for v in of(parts[0])]
            for m in parts[1:]:
                value = [v * w for v, w in zip(value, of(m))]
            fields.put("c%d" % n, d, row, value)


def near_kernel(rows, window, local, *refs):
    doses, groups = window.doses, window.groups
    dose_refs, (aerial, quench, swap, near) = refs[:doses], refs[doses:]
    half = rows // 2
    spread = make_spread()
    total = local * doses
    fields = Fields(rows, (near, near_rows, 0, total))
    start = window.start(lax.axis_index("dose"))

    def source(raw, at, row):
        own = [vector(raw, rows, groups, start + k, chip_row(rows, row)) for k in range(groups)]
        return own + swapped(swap, groups, at + row)

    for row in range(rows):
        fields.put("q0", 0, row, source(quench, rows, row))
    for d in range(total):
        dose = dose_refs[d // local][d % local]
        fields.put("dose", d, 0, [dose] * (2 * groups))
        rate = -exposure_rate * dose
        for row in range(rows):
            absorbed = [jnp.exp(rate * v) for v in source(aerial, 0, row)]
            fields.put("a0", d, row, [1.0 - v for v in absorbed])
            if row < half:
                fields.put("e", d, row, [exposure_rate * dose * v for v in absorbed])
        forward_rows(spread, fields, d, near_rows(rows))


def far_kernel(rows, window, total, near, image_s, image_c, far):
    spread = make_spread()
    fields = Fields(rows, (near, near_rows, 0, total), (far, far_rows, 0, total))
    table = dict(far_rows(rows), e=(0, 0))
    owner = lax.axis_index("dose")
    layout = image_layout(window)

    def source(place):
        return [v for src in (image_s, image_c) for v in layout.get(src, place, owner)]

    for row in range(-HALO_QUENCH, 0):
        fields.put("q0", 0, row, source(HALO_AERIAL + HALO_QUENCH + row))
    for d in range(total):
        rate = -exposure_rate * fields.get("dose", d, 0)[0]
        for row in range(-HALO_AERIAL, 0):
            fields.put("a0", d, row, [1.0 - jnp.exp(rate * v) for v in source(-1 - row)])
        forward_rows(spread, fields, d, table)


def backward_rows(spread, past, back, d, table):
    def step(name, row, both, n):
        new = spread(*back.around(name, d, row), acid_lateral, acid_depth)
        parts = zip(new, past.get("q%d" % n, d, row), both, past.get("c%d" % n, d, row), back.get("ct", d, row))
        return [v - q * (neutral_rate * s) + c * t for v, q, s, c, t in parts]

    for row in range(*table["l3"]):
        back.put("l3", d, row, [c * v for c, v in zip(past.get("c3", d, row), back.get("ct", d, row))])
    for row in range(*table["m2"]):
        parts = zip(past.get("a2", d, row), back.get("l3", d, row))
        back.put("m2", d, row, [-(neutral_rate * a * s) for a, s in parts])
    for row in range(*table["l2"]):
        back.put("l2", d, row, step("l3", row, back.get("l3", d, row), 2))
    for n, name in ((1, "l1"), (0, "g")):
        old, side = ("l2", "m2") if n else ("l1", "m1")
        wanted = set(range(*table[name]))
        if n:
            wanted |= set(range(*table["m1"]))
        for row in sorted(wanted):
            both = [a + b for a, b in zip(back.get(old, d, row), back.get(side, d, row))]
            if row in range(*table[name]):
                new = step(old, row, both, n)
                if n == 0:
                    new = [v * e for v, e in zip(new, past.get("e", d, row))]
                back.put(name, d, row, new)
            if n and row in range(*table["m1"]):
                new = spread(*back.around("m2", d, row), base_lateral, base_depth)
                parts = zip(new, past.get("a1", d, row), both)
                back.put("m1", d, row, [v - a * (neutral_rate * s) for v, a, s in parts])


def back_near_kernel(rows, window, local, group, near, far, extra_own, extra_par, cot, swap, *refs):
    doses, groups = window.doses, window.groups
    wholes, back_near = refs[:-1], refs[-1]
    half = rows // 2
    area = rows * window.depth
    inner = half + HALO_COT
    total = local * doses
    spread = make_spread()
    owner = lax.axis_index("dose")
    start = window.start(owner)
    image = image_layout(window)
    whole = whole_layout(rows, window, local)
    for d in range(group * local, (group + 1) * local):
        past = Fields(rows, (near, near_rows, 0, total), (far, far_rows, 0, total))
        rate = -exposure_rate * past.get("dose", d, 0)[0]
        light = [v for src in (extra_own, extra_par) for v in image.get(src, 0, owner)]
        past.more["a0", d, rows] = [1.0 - jnp.exp(rate * v) for v in light]
        for n in range(3):
            row = rows - 1 - n
            past.more["a%d" % (n + 1), d, row] = next_acid(spread, past, d, n, row)[0]
        for n, row in ((3, half + 2), (2, half + 1)):
            left = left_of(past.get("a%d" % (5 - n), d, row))
            past.more["c%d" % n, d, row] = [v * m for v, m in zip(past.get("c%d" % n, d, row), left)]
        back = Fields(rows, (back_near, back_near_rows, group * local, local))
        table = back_near_rows(rows)
        i = d - group * local
        for row in range(*table["ct"]):
            if group == 0:
                value = [vector(cot, rows, groups, start + g, chip_row(rows, row), i * area) for g in range(groups)]
                value += swapped(swap, groups, 2 * rows + i * inner + row)
            else:
                at = chip_row(rows, row) * window.layers(HALO_COT)
                sides = wholes
                value = [v for src in sides for v in whole.get(src, i * rows, owner, at)]
            back.put("ct", d, row, value)
        backward_rows(spread, past, back, d, table)


def back_far_kernel(rows, window, local, near, far, *refs):
    doses, groups = window.doses, window.groups
    backs, refs = refs[:doses], refs[doses:]
    sends = refs[:doses]
    mine, other, store, full = refs[doses:]
    layouts = halo_layouts(window, local)
    half = rows // 2
    total = local * doses
    owner = lax.axis_index("dose")
    spread = make_spread()
    past = Fields(rows, (near, near_rows, 0, total), (far, far_rows, 0, total))
    stores = [(ref, back_near_rows, k * local, local) for k, ref in enumerate(backs)]
    back = Fields(rows, *stores, (store, back_far_rows, 0, total))
    table = back_far_rows(rows)
    for d in range(total):
        k, i = divmod(d, local)
        for row in range(*table["ct"]):
            place = i * HALO_COT - 1 - row
            value = layouts[0].get(sends[k], place, owner)
            back.put("ct", d, row, value + layouts[1].get(sends[k], place, owner, layouts[0].size))
        backward_rows(spread, past, back, d, table)
    for row in range(half):
        value = back.get("g", 0, row)
        for d in range(1, total):
            value = [v + w for v, w in zip(value, back.get("g", d, row))]
        for i in range(2 * groups):
            side, k = divmod(i, groups)
            full[side, row, pl.ds(k, SUB, stride=groups), :] = value[i]
    start = pl.multiple_of(owner * window.piece - window.start(owner), SUB)
    for side, out in enumerate((mine, other)):
        for row in range(half):
            out[row] = full[side, row, pl.ds(start, window.piece), :]


def join_kernel(rows, piece, mine, other, out):
    core = lax.axis_index("ty")
    for owner, part in ((core, mine), (1 - core, other)):
        for row in range(rows // 2):
            at = row + owner * (rows - 1 - 2 * row)
            for g in range(0, piece, SUB):
                out[pl.ds(g * rows + at, SUB, stride=rows), :] = part[row, pl.ds(g, SUB), :]


def gradient(aerial_image, quencher, cotangent, dose_levels, dose_index):
    depth, rows, lanes = aerial_image.shape
    local = cotangent.shape[0]
    half = rows // 2
    doses = lax.axis_size("dose")
    ring = lax.axis_size("tx")
    assert rows == half + HALO_QUENCH and HALO_AERIAL == HALO_QUENCH + 1
    window = Window(depth, doses)
    groups, piece = window.groups, window.piece
    total = local * doses
    f32 = jnp.float32
    aerial = aerial_image.reshape(depth * rows, lanes)
    quench = quencher.reshape(depth * rows, lanes)
    cot = cotangent.reshape(local * depth * rows, lanes)

    def call(kernel, fixed, args, outs, scratch=(), flops=0, space=pltpu.VMEM):
        def body(*refs):
            kernel(*fixed, *refs)

        moved = sum(4 * x.size for x in list(args) + list(outs))
        return pl.pallas_call(
            body,
            out_shape=tuple(outs),
            in_specs=[pl.BlockSpec(memory_space=space)] * len(args),
            out_specs=(pl.BlockSpec(memory_space=pltpu.VMEM),) * len(outs),
            scratch_shapes=list(scratch),
            compiler_params=pltpu.CompilerParams(vmem_limit_bytes=LIMIT),
            cost_estimate=pl.CostEstimate(flops=flops, bytes_accessed=moved, transcendentals=0),
        )(*args)

    def array(*shape):
        return jax.ShapeDtypeStruct(shape + (lanes,), f32)

    def store(table, count=total):
        return (places_of(table(rows), count)[1], 2 * groups, SUB)

    def along(value, cross=0, step=1, k=0):
        pairs = []
        for t in range(ring):
            for c in range(2):
                for d in range(doses):
                    up = step * (1 - 2 * (c ^ cross))
                    target = (((t + up) % ring) * 2 + (c ^ cross)) * doses + (d + k) % doses
                    pairs.append(((t * 2 + c) * doses + d, target))
        return lax.ppermute(value, ("tx", "ty", "dose"), pairs)

    def across(value):
        return along(value, cross=1, step=0)

    images = array(image_layout(window).size)
    handed, halo = swap_layout(rows, window, local)
    whole = array(whole_layout(rows, window, local).size)
    flat = [jax.ShapeDtypeStruct(x.shape, f32) for x in (aerial, quench, cot)]
    image_s, image_c, dose, aerial, quench, cot = call(
        image_kernel,
        (rows, window, local),
        [pltpu.with_memory_space_constraint(x, pltpu.HBM) for x in (aerial, quench, cot, dose_levels, dose_index)],
        [images, images, array(local, SUB)] + flat,
        [
            pltpu.SMEM(dose_levels.shape, f32),
            pltpu.SMEM(dose_index.shape, jnp.int32),
            pltpu.SemaphoreType.DMA((5,)),
        ],
        space=pltpu.HBM,
    )
    image_s = along(image_s)
    image_c = along(image_c, cross=1)
    rest = call(
        rest_kernel,
        (rows, window, local),
        (aerial, quench, cot),
        [array(handed + doses * halo)] + [array(halo)] * doses + [whole] * (doses - 1),
    )
    swap = across(rest[0])
    values, wholes = [dose], []
    for k in range(1, doses):
        arrived = along(rest[doses + k], step=0, k=k)
        values.append(along(dose, step=0, k=k))
        wholes.append([arrived, across(arrived)])
    sends = []
    for k in range(doses):
        other = lax.slice_in_dim(swap, handed + k * halo, handed + (k + 1) * halo)
        both = jnp.concatenate((other, rest[1 + k]) if crosses(k) else (rest[1 + k], other), axis=0)
        sends.append(along(both, cross=int(crosses(k)), k=k))

    (near,) = call(
        near_kernel, (rows, window, local), values + [aerial, quench, swap], [array(*store(near_rows))], flops=10_000_000
    )
    extra_own = across(image_c)
    extra_par = across(image_s)
    (far,) = call(
        far_kernel, (rows, window, total), (near, image_s, image_c), [array(*store(far_rows))], flops=10_000_000
    )
    backs = []
    for k in range(doses):
        backs += call(
            back_near_kernel,
            (rows, window, local, k),
            [near, far, extra_own, extra_par, cot, swap] + (wholes[k - 1] if k else []),
            [array(*store(back_near_rows, local))],
            flops=10_000_000,
        )
    mine, other = call(
        back_far_kernel,
        (rows, window, local),
        [near, far] + backs + sends,
        [array(half, piece)] * 2,
        [
            pltpu.VMEM(store(back_far_rows) + (lanes,), f32),
            pltpu.VMEM((2, half, window.size, lanes), f32),
        ],
        flops=10_000_000,
    )
    other = across(other)
    (out,) = call(join_kernel, (rows, piece), (mine, other), [array(piece * rows)])
    return out.reshape(piece, rows, lanes)


def solution(mesh):
    placed = (
        P("focus", "tx", "ty"),
        P(None, "tx", "ty"),
        P(("focus", "dose"), None, "tx", "ty"),
        P(),
        P(("focus", "dose")),
    )
    return jax.shard_map(
        gradient,
        mesh=mesh,
        in_specs=placed,
        out_specs=P(("focus", "dose"), "tx", "ty"),
        check_vma=False,
    )
```

```python
import jax
import jax.numpy as jnp
from jax import lax
from jax.experimental import pallas as pl
from jax.experimental.pallas import tpu as pltpu
from jax.sharding import PartitionSpec as P


exposure_rate = 1.0
neutral_rate = 0.8
deprotect_rate = 0.5
acid_lateral = 0.23
acid_depth = 0.02
base_lateral = 0.2
base_depth = 0.02

HALO_AERIAL = 5
HALO_QUENCH = 4
HALO_COT = 3
SUB = 8
LIMIT = 20 << 20


class Window:
    def __init__(self, depth, doses):
        self.depth, self.doses = depth, doses
        self.piece = depth // doses
        self.ends = 0 if doses == 1 else 1 if doses == 2 else 2
        self.size = min(depth, self.piece + SUB * self.ends)
        self.groups = self.size // SUB

    def layers(self, halo):
        return min(self.depth, self.piece + halo * self.ends)

    def clamp(self, owner, halo, size):
        return jnp.minimum(jnp.maximum(owner * self.piece - halo, 0), self.depth - size)

    def start(self, owner):
        return self.clamp(owner, SUB, self.size)

    def sent(self, owner, halo):
        return self.clamp(owner, halo, self.layers(halo))


class Dense:
    def __init__(self, window, reaches, lead=True, tail=True, size=0):
        self.window = window
        slack = [window.size - window.layers(reach) for reach in reaches]
        used = sum(window.layers(reach) for reach in reaches)
        ends = (slack[0] if lead else 0) + (slack[-1] if tail else 0)
        self.size = max(size, -(-(used + ends) // SUB) * SUB)
        at = self.size - used if lead and not tail else slack[0] if lead else 0
        self.rows = []
        for reach in reaches:
            self.rows.append((at, reach))
            at += window.layers(reach)

    def put(self, dst, i, src, base, rows, row, owner, block=0):
        at, reach = self.rows[i]
        first, layers = self.window.sent(owner, reach), self.window.layers(reach)
        for g in range(0, layers, SUB):
            n = min(SUB, layers - g)
            value = src[pl.ds(base + rows * (first + g) + row, n, stride=rows), :]
            dst[pl.ds(block + at + g, n), :] = value

    def get(self, src, i, owner, block=0):
        at, reach = self.rows[i]
        window = self.window
        start = block + at - (window.sent(owner, reach) - window.start(owner))
        return [src[pl.ds(start + k, SUB, stride=window.groups), :] for k in range(window.groups)]


def clear(dst, at, size):
    dst[pl.ds(at, size), :] = jnp.zeros((size, dst.shape[1]), jnp.float32)


def image_layout(window):
    aerial = [HALO_AERIAL - i for i in range(1, HALO_AERIAL + 1)]
    quench = [HALO_QUENCH - i for i in range(HALO_QUENCH, 0, -1)]
    return Dense(window, aerial + quench)


def crosses(k):
    return k % 2 == 1


def halo_layouts(window, local):
    reaches = [HALO_COT - i for _ in range(local) for i in range(1, HALO_COT + 1)]
    size = Dense(window, reaches, lead=False).size
    first = Dense(window, reaches, tail=False, size=size)
    return first, Dense(window, reaches, lead=False, size=first.size)


def whole_layout(rows, window, local):
    return Dense(window, [HALO_COT] * (local * rows))


def chip_row(rows, row):
    return row + lax.axis_index("ty") * (rows - 1 - 2 * row)


def vector(ref, rows, groups, first, row, base=0):
    return ref[pl.ds(base + rows * first + row, SUB, stride=rows * groups), :]


def image_kernel(rows, window, local, *refs):
    image_hbm, quench_hbm, cot_hbm, levels_hbm, index_hbm = refs[:5]
    image_s, image_c, dose, aerial, quench, cot, levels, index, sems = refs[5:]
    pairs = ((image_hbm, aerial), (quench_hbm, quench), (cot_hbm, cot), (levels_hbm, levels), (index_hbm, index))
    copies = [pltpu.make_async_copy(src, dst, sems.at[i]) for i, (src, dst) in enumerate(pairs)]
    for copy in copies:
        copy.start()
    layout = image_layout(window)
    for ref in (image_s, image_c):
        clear(ref, 0, SUB)
        clear(ref, layout.size - 2 * SUB, 2 * SUB)
    owner = lax.axis_index("dose")
    copies[0].wait()
    copies[1].wait()
    order = [(aerial, i) for i in range(1, HALO_AERIAL + 1)]
    order += [(quench, i) for i in range(HALO_QUENCH, 0, -1)]
    for place, (src, i) in enumerate(order):
        layout.put(image_s, place, src, 0, rows, chip_row(rows, rows - i), owner)
        layout.put(image_c, place, src, 0, rows, chip_row(rows, i - 1), owner)
    for copy in copies[2:]:
        copy.wait()
    for d in range(local):
        dose[d] = jnp.full(dose.shape[1:], levels[index[d]], jnp.float32)


def swap_layout(rows, window, local):
    vectors = 2 * rows + local * (rows // 2 + HALO_COT)
    return vectors * window.groups * SUB, halo_layouts(window, local)[0].size


def swapped(swap, groups, place):
    return [swap[pl.ds((place * groups + k) * SUB, SUB), :] for k in range(groups)]


def rest_kernel(rows, window, local, aerial, quench, cot, swap, *dense):
    depth, groups, doses = window.depth, window.groups, window.doses
    area = rows * depth
    inner = rows // 2 + HALO_COT
    owner = lax.axis_index("dose")
    sends = dense[:doses]
    wholes = dense[doses:]
    handed, halo = swap_layout(rows, window, local)
    layouts = halo_layouts(window, local)
    whole = whole_layout(rows, window, local)
    for k in range(doses):
        target = lax.rem(owner + k, doses)
        block = handed + k * halo
        mine, given = layouts[::-1] if crosses(k) else layouts
        for ref, at in ((sends[k], 0), (swap, block)):
            clear(ref, at, 2 * SUB)
            clear(ref, at + halo - 2 * SUB, 2 * SUB)
        for d in range(local):
            for i in range(1, HALO_COT + 1):
                outer, inward = chip_row(rows, rows - i), chip_row(rows, i - 1)
                if crosses(k):
                    outer, inward = inward, outer
                place = d * HALO_COT + i - 1
                mine.put(sends[k], place, cot, d * area, rows, outer, target)
                given.put(swap, place, cot, d * area, rows, inward, target, block)
        if k:
            ref = wholes[k - 1]
            clear(ref, 0, SUB)
            clear(ref, whole.size - 2 * SUB, 2 * SUB)
            for d in range(local):
                for row in range(rows):
                    whole.put(ref, d * rows + row, cot, d * area, rows, row, target)
    place = 0
    parts = [(aerial, 0, rows), (quench, 0, rows)] + [(cot, d * area, inner) for d in range(local)]
    start = window.start(owner)
    for src, base, width in parts:
        for i in range(width):
            for k in range(groups):
                value = vector(src, rows, groups, start + k, chip_row(rows, rows - 1 - i), base)
                swap[pl.ds((place * groups + k) * SUB, SUB), :] = value
            place += 1


def make_spread():
    lane = lax.broadcasted_iota(jnp.int32, (SUB, 128), 1)
    sub = lax.broadcasted_iota(jnp.int32, (SUB, 128), 0)
    first_lane = lane == 0
    last_lane = lane == 127
    first_sub = sub == 0
    last_sub = sub == SUB - 1

    def spread(above, center, below, along, depthwise, loss=None):
        count = len(center)
        groups = count // 2
        keep = 1.0 - 4.0 * along - 2.0 * depthwise
        result = []
        for i in range(count):
            k = i % groups
            j = (i + groups) % count
            right = pltpu.roll(jnp.where(first_lane, center[j], center[i]), 127, 1)
            left = pltpu.roll(jnp.where(last_lane, center[j], center[i]), 1, 1)
            lateral = (above[i] + below[i]) + (right + left)
            if k + 1 < groups:
                deeper = center[i + 1]
            else:
                deeper = jnp.where(last_sub, center[i], pltpu.roll(center[i - k], SUB - 1, 0))
            if k > 0:
                higher = center[i - 1]
            else:
                higher = jnp.where(first_sub, center[i], pltpu.roll(center[i + groups - 1], 1, 0))
            kept = (keep if loss is None else keep - loss[i]) * center[i]
            result.append(kept + along * lateral + depthwise * (deeper + higher))
        return result

    return spread


def near_rows(rows):
    half = rows // 2
    return {
        "q0": (0, rows),
        "a0": (0, rows),
        "a1": (1, rows - 1),
        "a2": (2, rows - 2),
        "a3": (3, rows - 3),
        "q1": (1, rows - 1),
        "q2": (2, rows - 2),
        "c3": (2, half + 3),
        "c2": (3, half + 2),
        "c1": (3, half + 1),
        "c0": (3, half),
        "e": (0, half),
        "dose": (0, 1),
    }


def far_rows(rows):
    return {
        "q0": (-4, 0),
        "a0": (-5, 0),
        "a1": (-4, 1),
        "a2": (-3, 2),
        "a3": (-2, 3),
        "q1": (-3, 1),
        "q2": (-2, 2),
        "c3": (-3, 2),
        "c2": (-2, 3),
        "c1": (-1, 3),
        "c0": (0, 3),
    }


def places_of(table, local):
    places, total = {}, 0
    for name, (first, end) in table.items():
        for d in range(local):
            for row in range(first, end):
                if name == "q0" and d > 0:
                    places[name, d, row] = places[name, 0, row]
                else:
                    places[name, d, row] = total
                    total += 1
    return places, total


def back_near_rows(rows):
    half = rows // 2
    return {
        "ct": (0, half + 3),
        "l3": (0, half + 3),
        "l2": (1, half + 2),
        "m2": (0, half + 1),
        "l1": (2, half + 1),
        "m1": (1, half),
        "g": (3, half),
    }


def back_far_rows(rows):
    return {
        "ct": (-3, 0),
        "l3": (-3, 0),
        "l2": (-2, 1),
        "m2": (-1, 0),
        "l1": (-1, 2),
        "m1": (0, 1),
        "g": (0, 3),
    }


class Fields:
    def __init__(self, rows, *stores):
        self.stores = [(ref, places_of(table(rows), count)[0], first) for ref, table, first, count in stores]
        self.more = {}

    def get(self, name, d, row):
        if (name, d, row) in self.more:
            return self.more[name, d, row]
        for ref, places, first in self.stores:
            if (name, d - first, row) in places:
                at = places[name, d - first, row]
                return [ref[at, i] for i in range(ref.shape[1])]
        raise KeyError((name, row))

    def around(self, name, d, row):
        return [self.get(name, d, row + i) for i in (-1, 0, 1)]

    def put(self, name, d, row, value):
        ref, places, first = self.stores[-1]
        at = places[name, d - first, row]
        for i in range(len(value)):
            ref[at, i] = value[i]


def left_of(acid):
    return [1.0 - (deprotect_rate / neutral_rate) * v for v in acid]


def next_acid(spread, fields, d, n, row):
    quench = fields.get("q%d" % n, d, row)
    return spread(*fields.around("a%d" % n, d, row), acid_lateral, acid_depth, quench)


def forward_rows(spread, fields, d, table):
    for n in range(3):
        first, end = table["a%d" % (n + 1)]
        for row in range(first, end):
            fields.put("a%d" % (n + 1), d, row, next_acid(spread, fields, d, n, row))
            if n < 2:
                q_first, q_end = table["q%d" % (n + 1)]
                if q_first <= row < q_end:
                    name = "q%d" % n
                    acid = fields.get("a%d" % n, d, row)
                    new = spread(*fields.around(name, d, row), base_lateral, base_depth, acid)
                    fields.put("q%d" % (n + 1), d, row, new)

    first = min(table[c][0] for c in ("c3", "c2", "c1", "c0"))
    end = max(table[c][1] for c in ("c3", "c2", "c1", "c0"))
    for row in range(first, end):
        wanted = [n for n in range(4) if table["c%d" % n][0] <= row < table["c%d" % n][1]]
        left = {}

        def of(n):
            if n not in left:
                left[n] = left_of(fields.get("a%d" % n, d, row))
            return left[n]

        for n in wanted:
            parts = [m for m in range(4) if m != n]
            if n >= 2 and table["e"][1] > 0 and row == table["c%d" % n][1] - 1:
                parts = parts[:2]
            value = [(-deprotect_rate) * v for v in of(parts[0])]
            for m in parts[1:]:
                value = [v * w for v, w in zip(value, of(m))]
            fields.put("c%d" % n, d, row, value)


def near_kernel(rows, window, local, *refs):
    doses, groups = window.doses, window.groups
    dose_refs, (aerial, quench, swap, near) = refs[:doses], refs[doses:]
    half = rows // 2
    spread = make_spread()
    total = local * doses
    fields = Fields(rows, (near, near_rows, 0, total))
    start = window.start(lax.axis_index("dose"))

    def source(raw, at, row):
        own = [vector(raw, rows, groups, start + k, chip_row(rows, row)) for k in range(groups)]
        return own + swapped(swap, groups, at + row)

    for row in range(rows):
        fields.put("q0", 0, row, [neutral_rate * v for v in source(quench, rows, row)])
    for d in range(total):
        dose = dose_refs[d // local][d % local]
        fields.put("dose", d, 0, [dose] * (2 * groups))
        rate = -exposure_rate * dose
        for row in range(rows):
            absorbed = [jnp.exp(rate * v) for v in source(aerial, 0, row)]
            fields.put("a0", d, row, [neutral_rate - neutral_rate * v for v in absorbed])
            if row < half:
                fields.put("e", d, row, [exposure_rate * dose * v for v in absorbed])
        forward_rows(spread, fields, d, near_rows(rows))


def far_kernel(rows, window, total, near, image_s, image_c, far):
    spread = make_spread()
    fields = Fields(rows, (near, near_rows, 0, total), (far, far_rows, 0, total))
    table = dict(far_rows(rows), e=(0, 0))
    owner = lax.axis_index("dose")
    layout = image_layout(window)

    def source(place):
        return [v for src in (image_s, image_c) for v in layout.get(src, place, owner)]

    for row in range(-HALO_QUENCH, 0):
        fields.put("q0", 0, row, [neutral_rate * v for v in source(HALO_AERIAL + HALO_QUENCH + row)])
    for d in range(total):
        rate = -exposure_rate * fields.get("dose", d, 0)[0]
        for row in range(-HALO_AERIAL, 0):
            absorbed = [jnp.exp(rate * v) for v in source(-1 - row)]
            fields.put("a0", d, row, [neutral_rate - neutral_rate * v for v in absorbed])
        forward_rows(spread, fields, d, table)


def backward_rows(spread, past, back, d, table):
    def step(name, row, other, n):
        quench = past.get("q%d" % n, d, row)
        new = spread(*back.around(name, d, row), acid_lateral, acid_depth, quench)
        if other is not None:
            new = [v - q * m for v, q, m in zip(new, quench, other)]
        return [v + c * t for v, c, t in zip(new, past.get("c%d" % n, d, row), back.get("ct", d, row))]

    for row in range(*table["l3"]):
        back.put("l3", d, row, [c * v for c, v in zip(past.get("c3", d, row), back.get("ct", d, row))])
    for row in range(*table["m2"]):
        parts = zip(past.get("a2", d, row), back.get("l3", d, row))
        back.put("m2", d, row, [-(a * s) for a, s in parts])
    for row in range(*table["l2"]):
        back.put("l2", d, row, step("l3", row, None, 2))
    for n, name in ((1, "l1"), (0, "g")):
        old, side = ("l2", "m2") if n else ("l1", "m1")
        wanted = set(range(*table[name]))
        if n:
            wanted |= set(range(*table["m1"]))
        for row in sorted(wanted):
            other = back.get(side, d, row)
            if row in range(*table[name]):
                new = step(old, row, other, n)
                if n == 0:
                    new = [v * e for v, e in zip(new, past.get("e", d, row))]
                back.put(name, d, row, new)
            if n and row in range(*table["m1"]):
                acid = past.get("a1", d, row)
                new = spread(*back.around("m2", d, row), base_lateral, base_depth, acid)
                back.put("m1", d, row, [v - a * s for v, a, s in zip(new, acid, back.get(old, d, row))])


def back_near_kernel(rows, window, local, group, near, far, extra_own, extra_par, cot, swap, *refs):
    doses, groups = window.doses, window.groups
    wholes, back_near = refs[:-1], refs[-1]
    half = rows // 2
    area = rows * window.depth
    inner = half + HALO_COT
    total = local * doses
    spread = make_spread()
    owner = lax.axis_index("dose")
    start = window.start(owner)
    image = image_layout(window)
    whole = whole_layout(rows, window, local)
    for d in range(group * local, (group + 1) * local):
        past = Fields(rows, (near, near_rows, 0, total), (far, far_rows, 0, total))
        rate = -exposure_rate * past.get("dose", d, 0)[0]
        light = [v for src in (extra_own, extra_par) for v in image.get(src, 0, owner)]
        past.more["a0", d, rows] = [neutral_rate - neutral_rate * jnp.exp(rate * v) for v in light]
        for n in range(3):
            row = rows - 1 - n
            past.more["a%d" % (n + 1), d, row] = next_acid(spread, past, d, n, row)
        for n, row in ((3, half + 2), (2, half + 1)):
            left = left_of(past.get("a%d" % (5 - n), d, row))
            past.more["c%d" % n, d, row] = [v * m for v, m in zip(past.get("c%d" % n, d, row), left)]
        back = Fields(rows, (back_near, back_near_rows, group * local, local))
        table = back_near_rows(rows)
        i = d - group * local
        for row in range(*table["ct"]):
            if group == 0:
                value = [vector(cot, rows, groups, start + g, chip_row(rows, row), i * area) for g in range(groups)]
                value += swapped(swap, groups, 2 * rows + i * inner + row)
            else:
                at = chip_row(rows, row) * window.layers(HALO_COT)
                sides = wholes
                value = [v for src in sides for v in whole.get(src, i * rows, owner, at)]
            back.put("ct", d, row, value)
        backward_rows(spread, past, back, d, table)


def back_far_kernel(rows, window, local, near, far, *refs):
    doses, groups = window.doses, window.groups
    backs, refs = refs[:doses], refs[doses:]
    sends = refs[:doses]
    mine, other, store, full = refs[doses:]
    layouts = halo_layouts(window, local)
    half = rows // 2
    total = local * doses
    owner = lax.axis_index("dose")
    spread = make_spread()
    past = Fields(rows, (near, near_rows, 0, total), (far, far_rows, 0, total))
    stores = [(ref, back_near_rows, k * local, local) for k, ref in enumerate(backs)]
    back = Fields(rows, *stores, (store, back_far_rows, 0, total))
    table = back_far_rows(rows)
    for d in range(total):
        k, i = divmod(d, local)
        for row in range(*table["ct"]):
            place = i * HALO_COT - 1 - row
            value = layouts[0].get(sends[k], place, owner)
            back.put("ct", d, row, value + layouts[1].get(sends[k], place, owner, layouts[0].size))
        backward_rows(spread, past, back, d, table)
    for row in range(half):
        value = back.get("g", 0, row)
        for d in range(1, total):
            value = [v + w for v, w in zip(value, back.get("g", d, row))]
        for i in range(2 * groups):
            side, k = divmod(i, groups)
            full[side, row, pl.ds(k, SUB, stride=groups), :] = value[i]
    start = pl.multiple_of(owner * window.piece - window.start(owner), SUB)
    for side, out in enumerate((mine, other)):
        for row in range(half):
            out[row] = full[side, row, pl.ds(start, window.piece), :]


def join_kernel(rows, piece, mine, other, out):
    core = lax.axis_index("ty")
    for owner, part in ((core, mine), (1 - core, other)):
        for row in range(rows // 2):
            at = row + owner * (rows - 1 - 2 * row)
            for g in range(0, piece, SUB):
                out[pl.ds(g * rows + at, SUB, stride=rows), :] = part[row, pl.ds(g, SUB), :]


def gradient(aerial_image, quencher, cotangent, dose_levels, dose_index):
    depth, rows, lanes = aerial_image.shape
    local = cotangent.shape[0]
    half = rows // 2
    doses = lax.axis_size("dose")
    ring = lax.axis_size("tx")
    assert rows == half + HALO_QUENCH and HALO_AERIAL == HALO_QUENCH + 1
    window = Window(depth, doses)
    groups, piece = window.groups, window.piece
    total = local * doses
    f32 = jnp.float32
    aerial = aerial_image.reshape(depth * rows, lanes)
    quench = quencher.reshape(depth * rows, lanes)
    cot = cotangent.reshape(local * depth * rows, lanes)

    def call(kernel, fixed, args, outs, scratch=(), flops=0, space=pltpu.VMEM):
        def body(*refs):
            kernel(*fixed, *refs)

        moved = sum(4 * x.size for x in list(args) + list(outs))
        return pl.pallas_call(
            body,
            out_shape=tuple(outs),
            in_specs=[pl.BlockSpec(memory_space=space)] * len(args),
            out_specs=(pl.BlockSpec(memory_space=pltpu.VMEM),) * len(outs),
            scratch_shapes=list(scratch),
            compiler_params=pltpu.CompilerParams(vmem_limit_bytes=LIMIT),
            cost_estimate=pl.CostEstimate(flops=flops, bytes_accessed=moved, transcendentals=0),
        )(*args)

    def array(*shape):
        return jax.ShapeDtypeStruct(shape + (lanes,), f32)

    def store(table, count=total):
        return (places_of(table(rows), count)[1], 2 * groups, SUB)

    def along(value, cross=0, step=1, k=0):
        pairs = []
        for t in range(ring):
            for c in range(2):
                for d in range(doses):
                    up = step * (1 - 2 * (c ^ cross))
                    target = (((t + up) % ring) * 2 + (c ^ cross)) * doses + (d + k) % doses
                    pairs.append(((t * 2 + c) * doses + d, target))
        return lax.ppermute(value, ("tx", "ty", "dose"), pairs)

    def across(value):
        return along(value, cross=1, step=0)

    images = array(image_layout(window).size)
    handed, halo = swap_layout(rows, window, local)
    whole = array(whole_layout(rows, window, local).size)
    flat = [jax.ShapeDtypeStruct(x.shape, f32) for x in (aerial, quench, cot)]
    image_s, image_c, dose, aerial, quench, cot = call(
        image_kernel,
        (rows, window, local),
        [pltpu.with_memory_space_constraint(x, pltpu.HBM) for x in (aerial, quench, cot, dose_levels, dose_index)],
        [images, images, array(local, SUB)] + flat,
        [
            pltpu.SMEM(dose_levels.shape, f32),
            pltpu.SMEM(dose_index.shape, jnp.int32),
            pltpu.SemaphoreType.DMA((5,)),
        ],
        space=pltpu.HBM,
    )
    image_s = along(image_s)
    image_c = along(image_c, cross=1)
    rest = call(
        rest_kernel,
        (rows, window, local),
        (aerial, quench, cot),
        [array(handed + doses * halo)] + [array(halo)] * doses + [whole] * (doses - 1),
    )
    swap = across(rest[0])
    values, wholes = [dose], []
    for k in range(1, doses):
        arrived = along(rest[doses + k], step=0, k=k)
        values.append(along(dose, step=0, k=k))
        wholes.append([arrived, across(arrived)])
    sends = []
    for k in range(doses):
        other = lax.slice_in_dim(swap, handed + k * halo, handed + (k + 1) * halo)
        both = jnp.concatenate((other, rest[1 + k]) if crosses(k) else (rest[1 + k], other), axis=0)
        sends.append(along(both, cross=int(crosses(k)), k=k))

    (near,) = call(
        near_kernel, (rows, window, local), values + [aerial, quench, swap], [array(*store(near_rows))], flops=10_000_000
    )
    extra_own = across(image_c)
    extra_par = across(image_s)
    (far,) = call(
        far_kernel, (rows, window, total), (near, image_s, image_c), [array(*store(far_rows))], flops=10_000_000
    )
    backs = []
    for k in range(doses):
        backs += call(
            back_near_kernel,
            (rows, window, local, k),
            [near, far, extra_own, extra_par, cot, swap] + (wholes[k - 1] if k else []),
            [array(*store(back_near_rows, local))],
            flops=10_000_000,
        )
    mine, other = call(
        back_far_kernel,
        (rows, window, local),
        [near, far] + backs + sends,
        [array(half, piece)] * 2,
        [
            pltpu.VMEM(store(back_far_rows) + (lanes,), f32),
            pltpu.VMEM((2, half, window.size, lanes), f32),
        ],
        flops=10_000_000,
    )
    other = across(other)
    (out,) = call(join_kernel, (rows, piece), (mine, other), [array(piece * rows)])
    return out.reshape(piece, rows, lanes)


def solution(mesh):
    placed = (
        P("focus", "tx", "ty"),
        P(None, "tx", "ty"),
        P(("focus", "dose"), None, "tx", "ty"),
        P(),
        P(("focus", "dose")),
    )
    return jax.shard_map(
        gradient,
        mesh=mesh,
        in_specs=placed,
        out_specs=P(("focus", "dose"), "tx", "ty"),
        check_vma=False,
    )
```

```python
import jax
import jax.numpy as jnp
from jax import lax
from jax.experimental import pallas as pl
from jax.experimental.pallas import tpu as pltpu
from jax.sharding import PartitionSpec as P


exposure_rate = 1.0
neutral_rate = 0.8
deprotect_rate = 0.5
acid_lateral = 0.23
acid_depth = 0.02
base_lateral = 0.2
base_depth = 0.02

HALO_AERIAL = 5
HALO_QUENCH = 4
HALO_COT = 3
SUB = 8
LIMIT = 20 << 20


class Window:
    def __init__(self, depth, doses):
        self.depth, self.doses = depth, doses
        self.piece = depth // doses
        self.ends = 0 if doses == 1 else 1 if doses == 2 else 2
        self.size = min(depth, self.piece + SUB * self.ends)
        self.groups = self.size // SUB

    def layers(self, halo):
        return min(self.depth, self.piece + halo * self.ends)

    def clamp(self, owner, halo, size):
        return jnp.minimum(jnp.maximum(owner * self.piece - halo, 0), self.depth - size)

    def start(self, owner):
        return self.clamp(owner, SUB, self.size)

    def sent(self, owner, halo):
        return self.clamp(owner, halo, self.layers(halo))


class Dense:
    def __init__(self, window, reaches, lead=True, tail=True, size=0):
        self.window = window
        slack = [window.size - window.layers(reach) for reach in reaches]
        used = sum(window.layers(reach) for reach in reaches)
        ends = (slack[0] if lead else 0) + (slack[-1] if tail else 0)
        self.size = max(size, -(-(used + ends) // SUB) * SUB)
        at = self.size - used if lead and not tail else slack[0] if lead else 0
        self.rows = []
        for reach in reaches:
            self.rows.append((at, reach))
            at += window.layers(reach)

    def put(self, dst, i, src, base, rows, row, owner, block=0):
        at, reach = self.rows[i]
        first, layers = self.window.sent(owner, reach), self.window.layers(reach)
        for g in range(0, layers, SUB):
            n = min(SUB, layers - g)
            value = src[pl.ds(base + rows * (first + g) + row, n, stride=rows), :]
            dst[pl.ds(block + at + g, n), :] = value

    def get(self, src, i, owner, block=0):
        at, reach = self.rows[i]
        window = self.window
        start = block + at - (window.sent(owner, reach) - window.start(owner))
        return [src[pl.ds(start + k, SUB, stride=window.groups), :] for k in range(window.groups)]


def clear(dst, at, size):
    dst[pl.ds(at, size), :] = jnp.zeros((size, dst.shape[1]), jnp.float32)


def image_layout(window):
    aerial = [HALO_AERIAL - i for i in range(1, HALO_AERIAL + 1)]
    quench = [HALO_QUENCH - i for i in range(HALO_QUENCH, 0, -1)]
    return Dense(window, aerial + quench)


def crosses(k):
    return k % 2 == 1


def halo_layouts(window, local):
    reaches = [HALO_COT - i for _ in range(local) for i in range(1, HALO_COT + 1)]
    size = Dense(window, reaches, lead=False).size
    first = Dense(window, reaches, tail=False, size=size)
    return first, Dense(window, reaches, lead=False, size=first.size)


def whole_layout(rows, window, local):
    return Dense(window, [HALO_COT] * (local * rows))


def chip_row(rows, row):
    return row + lax.axis_index("ty") * (rows - 1 - 2 * row)


def vector(ref, rows, groups, first, row, base=0):
    return ref[pl.ds(base + rows * first + row, SUB, stride=rows * groups), :]


def image_kernel(rows, window, local, *refs):
    image_hbm, quench_hbm, cot_hbm, levels_hbm, index_hbm = refs[:5]
    image_s, image_c, dose, aerial, quench, cot, levels, index, sems = refs[5:]
    pairs = ((image_hbm, aerial), (quench_hbm, quench), (cot_hbm, cot), (levels_hbm, levels), (index_hbm, index))
    copies = [pltpu.make_async_copy(src, dst, sems.at[i]) for i, (src, dst) in enumerate(pairs)]
    for copy in copies:
        copy.start()
    layout = image_layout(window)
    for ref in (image_s, image_c):
        clear(ref, 0, SUB)
        clear(ref, layout.size - 2 * SUB, 2 * SUB)
    owner = lax.axis_index("dose")
    copies[0].wait()
    copies[1].wait()
    order = [(aerial, i) for i in range(1, HALO_AERIAL + 1)]
    order += [(quench, i) for i in range(HALO_QUENCH, 0, -1)]
    for place, (src, i) in enumerate(order):
        layout.put(image_s, place, src, 0, rows, chip_row(rows, rows - i), owner)
        layout.put(image_c, place, src, 0, rows, chip_row(rows, i - 1), owner)
    for copy in copies[2:]:
        copy.wait()
    for d in range(local):
        dose[d] = jnp.full(dose.shape[1:], levels[index[d]], jnp.float32)


def swap_layout(rows, window, local):
    vectors = 2 * rows + local * (rows // 2 + HALO_COT)
    return vectors * window.groups * SUB, halo_layouts(window, local)[0].size


def swapped(swap, groups, place):
    return [swap[pl.ds((place * groups + k) * SUB, SUB), :] for k in range(groups)]


def rest_kernel(rows, window, local, aerial, quench, cot, swap, *dense):
    depth, groups, doses = window.depth, window.groups, window.doses
    area = rows * depth
    inner = rows // 2 + HALO_COT
    owner = lax.axis_index("dose")
    sends = dense[:doses]
    wholes = dense[doses:]
    handed, halo = swap_layout(rows, window, local)
    layouts = halo_layouts(window, local)
    whole = whole_layout(rows, window, local)
    for k in range(doses):
        target = lax.rem(owner + k, doses)
        block = handed + k * halo
        mine, given = layouts[::-1] if crosses(k) else layouts
        for ref, at in ((sends[k], 0), (swap, block)):
            clear(ref, at, 2 * SUB)
            clear(ref, at + halo - 2 * SUB, 2 * SUB)
        for d in range(local):
            for i in range(1, HALO_COT + 1):
                outer, inward = chip_row(rows, rows - i), chip_row(rows, i - 1)
                if crosses(k):
                    outer, inward = inward, outer
                place = d * HALO_COT + i - 1
                mine.put(sends[k], place, cot, d * area, rows, outer, target)
                given.put(swap, place, cot, d * area, rows, inward, target, block)
        if k:
            ref = wholes[k - 1]
            clear(ref, 0, SUB)
            clear(ref, whole.size - 2 * SUB, 2 * SUB)
            for d in range(local):
                for row in range(rows):
                    whole.put(ref, d * rows + row, cot, d * area, rows, row, target)
    place = 0
    parts = [(aerial, 0, rows), (quench, 0, rows)] + [(cot, d * area, inner) for d in range(local)]
    start = window.start(owner)
    for src, base, width in parts:
        for i in range(width):
            for k in range(groups):
                value = vector(src, rows, groups, start + k, chip_row(rows, rows - 1 - i), base)
                swap[pl.ds((place * groups + k) * SUB, SUB), :] = value
            place += 1


def make_spread():
    lane = lax.broadcasted_iota(jnp.int32, (SUB, 128), 1)
    sub = lax.broadcasted_iota(jnp.int32, (SUB, 128), 0)
    first_lane = lane == 0
    last_lane = lane == 127
    first_sub = sub == 0
    last_sub = sub == SUB - 1

    def spread(above, center, below, along, depthwise, loss=None):
        count = len(center)
        groups = count // 2
        keep = 1.0 - 4.0 * along - 2.0 * depthwise
        result = []
        for i in range(count):
            k = i % groups
            j = (i + groups) % count
            right = pltpu.roll(jnp.where(first_lane, center[j], center[i]), 127, 1)
            left = pltpu.roll(jnp.where(last_lane, center[j], center[i]), 1, 1)
            lateral = (above[i] + below[i]) + (right + left)
            if k + 1 < groups:
                deeper = center[i + 1]
            else:
                deeper = jnp.where(last_sub, center[i], pltpu.roll(center[i - k], SUB - 1, 0))
            if k > 0:
                higher = center[i - 1]
            else:
                higher = jnp.where(first_sub, center[i], pltpu.roll(center[i + groups - 1], 1, 0))
            kept = (keep if loss is None else keep - loss[i]) * center[i]
            result.append(kept + along * lateral + depthwise * (deeper + higher))
        return result

    return spread


def near_rows(rows):
    half = rows // 2
    return {
        "q0": (0, rows),
        "a0": (0, rows),
        "a1": (1, rows - 1),
        "a2": (2, rows - 2),
        "a3": (3, rows - 3),
        "q1": (1, rows - 1),
        "q2": (2, rows - 2),
        "c3": (2, half + 3),
        "c2": (3, half + 2),
        "c1": (3, half + 1),
        "c0": (3, half),
        "e": (0, half),
        "dose": (0, 1),
    }


def far_rows(rows):
    return {
        "q0": (-4, 0),
        "a0": (-5, 0),
        "a1": (-4, 1),
        "a2": (-3, 2),
        "a3": (-2, 3),
        "q1": (-3, 1),
        "q2": (-2, 2),
        "c3": (-3, 2),
        "c2": (-2, 3),
        "c1": (-1, 3),
        "c0": (0, 3),
    }


def places_of(table, local):
    places, total = {}, 0
    for name, (first, end) in table.items():
        for d in range(local):
            for row in range(first, end):
                if name == "q0" and d > 0:
                    places[name, d, row] = places[name, 0, row]
                else:
                    places[name, d, row] = total
                    total += 1
    return places, total


def back_near_rows(rows):
    half = rows // 2
    return {
        "ct": (0, half + 3),
        "l3": (0, half + 3),
        "l2": (1, half + 2),
        "m2": (0, half + 1),
        "l1": (2, half + 1),
        "m1": (1, half),
        "g": (3, half),
    }


def back_far_rows(rows):
    return {
        "ct": (-3, 0),
        "l3": (-3, 0),
        "l2": (-2, 1),
        "m2": (-1, 0),
        "l1": (-1, 2),
        "m1": (0, 1),
        "g": (0, 3),
    }


class Fields:
    def __init__(self, rows, *stores):
        self.stores = [(ref, places_of(table(rows), count)[0], first) for ref, table, first, count in stores]
        self.more = {}

    def get(self, name, d, row):
        if (name, d, row) in self.more:
            return self.more[name, d, row]
        for ref, places, first in self.stores:
            if (name, d - first, row) in places:
                at = places[name, d - first, row]
                return [ref[at, i] for i in range(ref.shape[1])]
        raise KeyError((name, row))

    def around(self, name, d, row):
        return [self.get(name, d, row + i) for i in (-1, 0, 1)]

    def put(self, name, d, row, value):
        ref, places, first = self.stores[-1]
        at = places[name, d - first, row]
        for i in range(len(value)):
            ref[at, i] = value[i]


def left_of(acid):
    return [1.0 - (deprotect_rate / neutral_rate) * v for v in acid]


def next_acid(spread, fields, d, n, row):
    quench = fields.get("q%d" % n, d, row)
    return spread(*fields.around("a%d" % n, d, row), acid_lateral, acid_depth, quench)


def forward_rows(spread, fields, d, table):
    for n in range(3):
        first, end = table["a%d" % (n + 1)]
        for row in range(first, end):
            fields.put("a%d" % (n + 1), d, row, next_acid(spread, fields, d, n, row))
            if n < 2:
                q_first, q_end = table["q%d" % (n + 1)]
                if q_first <= row < q_end:
                    name = "q%d" % n
                    acid = fields.get("a%d" % n, d, row)
                    new = spread(*fields.around(name, d, row), base_lateral, base_depth, acid)
                    fields.put("q%d" % (n + 1), d, row, new)

    first = min(table[c][0] for c in ("c3", "c2", "c1", "c0"))
    end = max(table[c][1] for c in ("c3", "c2", "c1", "c0"))
    for row in range(first, end):
        wanted = [n for n in range(4) if table["c%d" % n][0] <= row < table["c%d" % n][1]]
        left = {}

        def of(n):
            if n not in left:
                left[n] = left_of(fields.get("a%d" % n, d, row))
            return left[n]

        for n in wanted:
            parts = [m for m in range(4) if m != n]
            if n >= 2 and table["e"][1] > 0 and row == table["c%d" % n][1] - 1:
                parts = parts[:2]
            value = [(-deprotect_rate) * v for v in of(parts[0])]
            for m in parts[1:]:
                value = [v * w for v, w in zip(value, of(m))]
            fields.put("c%d" % n, d, row, value)


def near_kernel(rows, window, local, *refs):
    doses, groups = window.doses, window.groups
    dose_refs, (aerial, quench, swap, near) = refs[:doses], refs[doses:]
    half = rows // 2
    spread = make_spread()
    total = local * doses
    fields = Fields(rows, (near, near_rows, 0, total))
    start = window.start(lax.axis_index("dose"))

    def source(raw, at, row):
        own = [vector(raw, rows, groups, start + k, chip_row(rows, row)) for k in range(groups)]
        return own + swapped(swap, groups, at + row)

    for row in range(rows):
        fields.put("q0", 0, row, [neutral_rate * v for v in source(quench, rows, row)])
    for d in range(total):
        dose = dose_refs[d // local][d % local]
        fields.put("dose", d, 0, [dose] * (2 * groups))
        rate = -exposure_rate * dose
        for row in range(rows):
            absorbed = [jnp.exp(rate * v) for v in source(aerial, 0, row)]
            fields.put("a0", d, row, [neutral_rate - neutral_rate * v for v in absorbed])
            if row < half:
                fields.put("e", d, row, [exposure_rate * dose * v for v in absorbed])
        forward_rows(spread, fields, d, near_rows(rows))


def far_kernel(rows, window, total, near, image_s, image_c, far):
    spread = make_spread()
    fields = Fields(rows, (near, near_rows, 0, total), (far, far_rows, 0, total))
    table = dict(far_rows(rows), e=(0, 0))
    owner = lax.axis_index("dose")
    layout = image_layout(window)

    def source(place):
        return [v for src in (image_s, image_c) for v in layout.get(src, place, owner)]

    for row in range(-HALO_QUENCH, 0):
        fields.put("q0", 0, row, [neutral_rate * v for v in source(HALO_AERIAL + HALO_QUENCH + row)])
    for d in range(total):
        rate = -exposure_rate * fields.get("dose", d, 0)[0]
        for row in range(-HALO_AERIAL, 0):
            absorbed = [jnp.exp(rate * v) for v in source(-1 - row)]
            fields.put("a0", d, row, [neutral_rate - neutral_rate * v for v in absorbed])
        forward_rows(spread, fields, d, table)


def backward_rows(spread, past, back, d, table):
    def step(name, row, other, n):
        quench = past.get("q%d" % n, d, row)
        new = spread(*back.around(name, d, row), acid_lateral, acid_depth, quench)
        if other is not None:
            new = [v - q * m for v, q, m in zip(new, quench, other)]
        return [v + c * t for v, c, t in zip(new, past.get("c%d" % n, d, row), back.get("ct", d, row))]

    for row in range(*table["l3"]):
        back.put("l3", d, row, [c * v for c, v in zip(past.get("c3", d, row), back.get("ct", d, row))])
    for row in range(*table["m2"]):
        parts = zip(past.get("a2", d, row), back.get("l3", d, row))
        back.put("m2", d, row, [-(a * s) for a, s in parts])
    for row in range(*table["l2"]):
        back.put("l2", d, row, step("l3", row, None, 2))
    for n, name in ((1, "l1"), (0, "g")):
        old, side = ("l2", "m2") if n else ("l1", "m1")
        wanted = set(range(*table[name]))
        if n:
            wanted |= set(range(*table["m1"]))
        for row in sorted(wanted):
            other = back.get(side, d, row)
            if row in range(*table[name]):
                new = step(old, row, other, n)
                if n == 0:
                    new = [v * e for v, e in zip(new, past.get("e", d, row))]
                back.put(name, d, row, new)
            if n and row in range(*table["m1"]):
                acid = past.get("a1", d, row)
                new = spread(*back.around("m2", d, row), base_lateral, base_depth, acid)
                back.put("m1", d, row, [v - a * s for v, a, s in zip(new, acid, back.get(old, d, row))])


def back_near_kernel(rows, window, local, group, near, far, extra_own, extra_par, cot, swap, *refs):
    doses, groups = window.doses, window.groups
    wholes, back_near = refs[:-1], refs[-1]
    half = rows // 2
    area = rows * window.depth
    inner = half + HALO_COT
    total = local * doses
    spread = make_spread()
    owner = lax.axis_index("dose")
    start = window.start(owner)
    image = image_layout(window)
    whole = whole_layout(rows, window, local)
    for d in range(group * local, (group + 1) * local):
        past = Fields(rows, (near, near_rows, 0, total), (far, far_rows, 0, total))
        rate = -exposure_rate * past.get("dose", d, 0)[0]
        light = [v for src in (extra_own, extra_par) for v in image.get(src, 0, owner)]
        past.more["a0", d, rows] = [neutral_rate - neutral_rate * jnp.exp(rate * v) for v in light]
        for n in range(3):
            row = rows - 1 - n
            past.more["a%d" % (n + 1), d, row] = next_acid(spread, past, d, n, row)
        for n, row in ((3, half + 2), (2, half + 1)):
            left = left_of(past.get("a%d" % (5 - n), d, row))
            past.more["c%d" % n, d, row] = [v * m for v, m in zip(past.get("c%d" % n, d, row), left)]
        back = Fields(rows, (back_near, back_near_rows, group * local, local))
        table = back_near_rows(rows)
        i = d - group * local
        for row in range(*table["ct"]):
            if group == 0:
                value = [vector(cot, rows, groups, start + g, chip_row(rows, row), i * area) for g in range(groups)]
                value += swapped(swap, groups, 2 * rows + i * inner + row)
            else:
                at = chip_row(rows, row) * window.layers(HALO_COT)
                sides = wholes
                value = [v for src in sides for v in whole.get(src, i * rows, owner, at)]
            back.put("ct", d, row, value)
        backward_rows(spread, past, back, d, table)


def back_far_kernel(rows, window, local, group, near, far, back_near, sent, *refs):
    doses, groups = window.doses, window.groups
    sums, refs = (refs[0], refs[1:]) if group else (None, refs)
    half = rows // 2
    total = local * doses
    owner = lax.axis_index("dose")
    layouts = halo_layouts(window, local)
    spread = make_spread()
    past = Fields(rows, (near, near_rows, 0, total), (far, far_rows, 0, total))
    first, store = group * local, refs[-1] if group + 1 < doses else refs[-2]
    back = Fields(rows, (back_near, back_near_rows, first, local), (store, back_far_rows, first, local))
    table = back_far_rows(rows)
    for i in range(local):
        for row in range(*table["ct"]):
            place = i * HALO_COT - 1 - row
            value = layouts[0].get(sent, place, owner)
            value += layouts[1].get(sent, place, owner, layouts[0].size)
            back.put("ct", first + i, row, value)
        backward_rows(spread, past, back, first + i, table)
    for row in range(half):
        value = back.get("g", first, row)
        for i in range(1, local):
            value = [v + w for v, w in zip(value, back.get("g", first + i, row))]
        if group:
            value = [v + sums[row, i] for i, v in enumerate(value)]
        for i in range(2 * groups):
            if group + 1 < doses:
                refs[0][row, i] = value[i]
            else:
                side, k = divmod(i, groups)
                refs[-1][side, row, pl.ds(k, SUB, stride=groups), :] = value[i]
    if group + 1 == doses:
        full = refs[-1]
        start = pl.multiple_of(owner * window.piece - window.start(owner), SUB)
        for side, out in enumerate(refs[:2]):
            for row in range(half):
                out[row] = full[side, row, pl.ds(start, window.piece), :]


def join_kernel(rows, piece, mine, other, out):
    core = lax.axis_index("ty")
    for owner, part in ((core, mine), (1 - core, other)):
        for row in range(rows // 2):
            at = row + owner * (rows - 1 - 2 * row)
            for g in range(0, piece, SUB):
                out[pl.ds(g * rows + at, SUB, stride=rows), :] = part[row, pl.ds(g, SUB), :]


def gradient(aerial_image, quencher, cotangent, dose_levels, dose_index):
    depth, rows, lanes = aerial_image.shape
    local = cotangent.shape[0]
    half = rows // 2
    doses = lax.axis_size("dose")
    ring = lax.axis_size("tx")
    assert rows == half + HALO_QUENCH and HALO_AERIAL == HALO_QUENCH + 1
    window = Window(depth, doses)
    groups, piece = window.groups, window.piece
    total = local * doses
    f32 = jnp.float32
    aerial = aerial_image.reshape(depth * rows, lanes)
    quench = quencher.reshape(depth * rows, lanes)
    cot = cotangent.reshape(local * depth * rows, lanes)

    def call(kernel, fixed, args, outs, scratch=(), flops=0, space=pltpu.VMEM):
        def body(*refs):
            kernel(*fixed, *refs)

        moved = sum(4 * x.size for x in list(args) + list(outs))
        return pl.pallas_call(
            body,
            out_shape=tuple(outs),
            in_specs=[pl.BlockSpec(memory_space=space)] * len(args),
            out_specs=(pl.BlockSpec(memory_space=pltpu.VMEM),) * len(outs),
            scratch_shapes=list(scratch),
            compiler_params=pltpu.CompilerParams(vmem_limit_bytes=LIMIT),
            cost_estimate=pl.CostEstimate(flops=flops, bytes_accessed=moved, transcendentals=0),
        )(*args)

    def array(*shape):
        return jax.ShapeDtypeStruct(shape + (lanes,), f32)

    def store(table, count=total):
        return (places_of(table(rows), count)[1], 2 * groups, SUB)

    def along(value, cross=0, step=1, k=0):
        pairs = []
        for t in range(ring):
            for c in range(2):
                for d in range(doses):
                    up = step * (1 - 2 * (c ^ cross))
                    target = (((t + up) % ring) * 2 + (c ^ cross)) * doses + (d + k) % doses
                    pairs.append(((t * 2 + c) * doses + d, target))
        return lax.ppermute(value, ("tx", "ty", "dose"), pairs)

    def across(value):
        return along(value, cross=1, step=0)

    images = array(image_layout(window).size)
    handed, halo = swap_layout(rows, window, local)
    whole = array(whole_layout(rows, window, local).size)
    flat = [jax.ShapeDtypeStruct(x.shape, f32) for x in (aerial, quench, cot)]
    image_s, image_c, dose, aerial, quench, cot = call(
        image_kernel,
        (rows, window, local),
        [pltpu.with_memory_space_constraint(x, pltpu.HBM) for x in (aerial, quench, cot, dose_levels, dose_index)],
        [images, images, array(local, SUB)] + flat,
        [
            pltpu.SMEM(dose_levels.shape, f32),
            pltpu.SMEM(dose_index.shape, jnp.int32),
            pltpu.SemaphoreType.DMA((5,)),
        ],
        space=pltpu.HBM,
    )
    image_s = along(image_s)
    image_c = along(image_c, cross=1)
    rest = call(
        rest_kernel,
        (rows, window, local),
        (aerial, quench, cot),
        [array(handed + doses * halo)] + [array(halo)] * doses + [whole] * (doses - 1),
    )
    swap = across(rest[0])
    values, wholes = [dose], []
    for k in range(1, doses):
        arrived = along(rest[doses + k], step=0, k=k)
        values.append(along(dose, step=0, k=k))
        wholes.append([arrived, across(arrived)])
    sends = []
    for k in range(doses):
        other = lax.slice_in_dim(swap, handed + k * halo, handed + (k + 1) * halo)
        both = jnp.concatenate((other, rest[1 + k]) if crosses(k) else (rest[1 + k], other), axis=0)
        sends.append(along(both, cross=int(crosses(k)), k=k))

    (near,) = call(
        near_kernel, (rows, window, local), values + [aerial, quench, swap], [array(*store(near_rows))], flops=10_000_000
    )
    extra_own = across(image_c)
    extra_par = across(image_s)
    (far,) = call(
        far_kernel, (rows, window, total), (near, image_s, image_c), [array(*store(far_rows))], flops=10_000_000
    )
    backs = []
    for k in range(doses):
        backs += call(
            back_near_kernel,
            (rows, window, local, k),
            [near, far, extra_own, extra_par, cot, swap] + (wholes[k - 1] if k else []),
            [array(*store(back_near_rows, local))],
            flops=10_000_000,
        )
    sums = []
    for k in range(doses):
        final = k + 1 == doses
        sums = call(
            back_far_kernel,
            (rows, window, local, k),
            [near, far, backs[k], sends[k]] + list(sums),
            [array(half, piece)] * 2 if final else [array(half, 2 * groups, SUB)],
            [pltpu.VMEM(store(back_far_rows, local) + (lanes,), f32)]
            + [pltpu.VMEM((2, half, window.size, lanes), f32)] * final,
            flops=10_000_000,
        )
    mine, other = sums
    other = across(other)
    (out,) = call(join_kernel, (rows, piece), (mine, other), [array(piece * rows)])
    return out.reshape(piece, rows, lanes)


def solution(mesh):
    placed = (
        P("focus", "tx", "ty"),
        P(None, "tx", "ty"),
        P(("focus", "dose"), None, "tx", "ty"),
        P(),
        P(("focus", "dose")),
    )
    return jax.shard_map(
        gradient,
        mesh=mesh,
        in_specs=placed,
        out_specs=P(("focus", "dose"), "tx", "ty"),
        check_vma=False,
    )
```

```python
import jax
import jax.numpy as jnp
from jax import lax
from jax.experimental import pallas as pl
from jax.experimental.pallas import tpu as pltpu
from jax.sharding import PartitionSpec as P


exposure_rate = 1.0
neutral_rate = 0.8
deprotect_rate = 0.5
acid_lateral = 0.23
acid_depth = 0.02
base_lateral = 0.2
base_depth = 0.02

HALO_AERIAL = 5
HALO_QUENCH = 4
HALO_COT = 3
SUB = 8
LIMIT = 20 << 20


class Window:
    def __init__(self, depth, doses):
        self.depth, self.doses = depth, doses
        self.piece = depth // doses
        self.ends = 0 if doses == 1 else 1 if doses == 2 else 2
        self.size = min(depth, self.piece + SUB * self.ends)
        self.groups = self.size // SUB

    def layers(self, halo):
        return min(self.depth, self.piece + halo * self.ends)

    def clamp(self, owner, halo, size):
        return jnp.minimum(jnp.maximum(owner * self.piece - halo, 0), self.depth - size)

    def start(self, owner):
        return self.clamp(owner, SUB, self.size)

    def sent(self, owner, halo):
        return self.clamp(owner, halo, self.layers(halo))


class Dense:
    def __init__(self, window, reaches, lead=True, tail=True, size=0):
        self.window = window
        slack = [window.size - window.layers(reach) for reach in reaches]
        used = sum(window.layers(reach) for reach in reaches)
        ends = (slack[0] if lead else 0) + (slack[-1] if tail else 0)
        self.size = max(size, -(-(used + ends) // SUB) * SUB)
        at = self.size - used if lead and not tail else slack[0] if lead else 0
        self.rows = []
        for reach in reaches:
            self.rows.append((at, reach))
            at += window.layers(reach)

    def put(self, dst, i, src, base, rows, row, owner, block=0):
        at, reach = self.rows[i]
        first, layers = self.window.sent(owner, reach), self.window.layers(reach)
        for g in range(0, layers, SUB):
            n = min(SUB, layers - g)
            value = src[pl.ds(base + rows * (first + g) + row, n, stride=rows), :]
            dst[pl.ds(block + at + g, n), :] = value

    def get(self, src, i, owner, block=0):
        at, reach = self.rows[i]
        window = self.window
        start = block + at - (window.sent(owner, reach) - window.start(owner))
        return [src[pl.ds(start + k, SUB, stride=window.groups), :] for k in range(window.groups)]


def clear(dst, at, size):
    dst[pl.ds(at, size), :] = jnp.zeros((size, dst.shape[1]), jnp.float32)


def image_layout(window):
    aerial = [HALO_AERIAL - i for i in range(1, HALO_AERIAL + 1)]
    quench = [HALO_QUENCH - i for i in range(HALO_QUENCH, 0, -1)]
    return Dense(window, aerial + quench)


def crosses(k):
    return k % 2 == 1


def halo_layouts(window, local):
    reaches = [HALO_COT - i for _ in range(local) for i in range(1, HALO_COT + 1)]
    size = Dense(window, reaches, lead=False).size
    first = Dense(window, reaches, tail=False, size=size)
    return first, Dense(window, reaches, lead=False, size=first.size)


def whole_layout(rows, window, local):
    return Dense(window, [HALO_COT] * (local * rows))


def chip_row(rows, row):
    return row + lax.axis_index("ty") * (rows - 1 - 2 * row)


def vector(ref, rows, groups, first, row, base=0):
    return ref[pl.ds(base + rows * first + row, SUB, stride=rows * groups), :]


def image_kernel(rows, window, local, *refs):
    image_hbm, quench_hbm, cot_hbm, levels_hbm, index_hbm = refs[:5]
    image_s, image_c, dose, aerial, quench, cot, levels, index, sems = refs[5:]
    pairs = ((image_hbm, aerial), (quench_hbm, quench), (cot_hbm, cot), (levels_hbm, levels), (index_hbm, index))
    copies = [pltpu.make_async_copy(src, dst, sems.at[i]) for i, (src, dst) in enumerate(pairs)]
    for copy in copies:
        copy.start()
    layout = image_layout(window)
    for ref in (image_s, image_c):
        clear(ref, 0, SUB)
        clear(ref, layout.size - 2 * SUB, 2 * SUB)
    owner = lax.axis_index("dose")
    copies[0].wait()
    copies[1].wait()
    order = [(aerial, i) for i in range(1, HALO_AERIAL + 1)]
    order += [(quench, i) for i in range(HALO_QUENCH, 0, -1)]
    for place, (src, i) in enumerate(order):
        layout.put(image_s, place, src, 0, rows, chip_row(rows, rows - i), owner)
        layout.put(image_c, place, src, 0, rows, chip_row(rows, i - 1), owner)
    for copy in copies[2:]:
        copy.wait()
    for d in range(local):
        dose[d] = jnp.full(dose.shape[1:], levels[index[d]], jnp.float32)


def swap_layout(rows, window, local):
    vectors = 2 * rows + local * (rows // 2 + HALO_COT)
    return vectors * window.groups * SUB, halo_layouts(window, local)[0].size


def swapped(swap, groups, place):
    return [swap[pl.ds((place * groups + k) * SUB, SUB), :] for k in range(groups)]


def rest_kernel(rows, window, local, dose, aerial, quench, cot, swap, *dense):
    depth, groups, doses = window.depth, window.groups, window.doses
    area = rows * depth
    inner = rows // 2 + HALO_COT
    owner = lax.axis_index("dose")
    sends = dense[:doses]
    wholes = dense[doses:]
    handed, halo = swap_layout(rows, window, local)
    layouts = halo_layouts(window, local)
    whole = whole_layout(rows, window, local)
    for k in range(doses):
        target = lax.rem(owner + k, doses)
        block = handed + k * halo
        mine, given = layouts[::-1] if crosses(k) else layouts
        for ref, at in ((sends[k], 0), (swap, block)):
            clear(ref, at, 2 * SUB)
            clear(ref, at + halo - 2 * SUB, 2 * SUB)
        for d in range(local):
            for i in range(1, HALO_COT + 1):
                outer, inward = chip_row(rows, rows - i), chip_row(rows, i - 1)
                if crosses(k):
                    outer, inward = inward, outer
                place = d * HALO_COT + i - 1
                mine.put(sends[k], place, cot, d * area, rows, outer, target)
                given.put(swap, place, cot, d * area, rows, inward, target, block)
        if k:
            ref = wholes[k - 1]
            clear(ref, 0, SUB)
            clear(ref, whole.size - 2 * SUB, 2 * SUB)
            for d in range(local):
                for row in range(rows):
                    whole.put(ref, d * rows + row, cot, d * area, rows, row, target)
                ref[pl.ds(whole.size + d * SUB, SUB), :] = dose[d]
    place = 0
    parts = [(aerial, 0, rows), (quench, 0, rows)] + [(cot, d * area, inner) for d in range(local)]
    start = window.start(owner)
    for src, base, width in parts:
        for i in range(width):
            for k in range(groups):
                value = vector(src, rows, groups, start + k, chip_row(rows, rows - 1 - i), base)
                swap[pl.ds((place * groups + k) * SUB, SUB), :] = value
            place += 1


def make_spread():
    lane = lax.broadcasted_iota(jnp.int32, (SUB, 128), 1)
    sub = lax.broadcasted_iota(jnp.int32, (SUB, 128), 0)
    first_lane = lane == 0
    last_lane = lane == 127
    first_sub = sub == 0
    last_sub = sub == SUB - 1

    def spread(above, center, below, along, depthwise, loss=None):
        count = len(center)
        groups = count // 2
        keep = 1.0 - 4.0 * along - 2.0 * depthwise
        result = []
        for i in range(count):
            k = i % groups
            j = (i + groups) % count
            right = pltpu.roll(jnp.where(first_lane, center[j], center[i]), 127, 1)
            left = pltpu.roll(jnp.where(last_lane, center[j], center[i]), 1, 1)
            lateral = (above[i] + below[i]) + (right + left)
            if k + 1 < groups:
                deeper = center[i + 1]
            else:
                deeper = jnp.where(last_sub, center[i], pltpu.roll(center[i - k], SUB - 1, 0))
            if k > 0:
                higher = center[i - 1]
            else:
                higher = jnp.where(first_sub, center[i], pltpu.roll(center[i + groups - 1], 1, 0))
            kept = (keep if loss is None else keep - loss[i]) * center[i]
            result.append(kept + along * lateral + depthwise * (deeper + higher))
        return result

    return spread


def near_rows(rows):
    half = rows // 2
    return {
        "q0": (0, rows),
        "a0": (0, rows),
        "a1": (1, rows - 1),
        "a2": (2, rows - 2),
        "a3": (3, rows - 3),
        "q1": (1, rows - 1),
        "q2": (2, rows - 2),
        "c3": (2, half + 3),
        "c2": (3, half + 2),
        "c1": (3, half + 1),
        "c0": (3, half),
        "e": (0, half),
        "dose": (0, 1),
    }


def far_rows(rows):
    return {
        "q0": (-4, 0),
        "a0": (-5, 0),
        "a1": (-4, 1),
        "a2": (-3, 2),
        "a3": (-2, 3),
        "q1": (-3, 1),
        "q2": (-2, 2),
        "c3": (-3, 2),
        "c2": (-2, 3),
        "c1": (-1, 3),
        "c0": (0, 3),
    }


def places_of(table, local):
    places, total = {}, 0
    for name, (first, end) in table.items():
        for d in range(local):
            for row in range(first, end):
                if name == "q0" and d > 0:
                    places[name, d, row] = places[name, 0, row]
                else:
                    places[name, d, row] = total
                    total += 1
    return places, total


def back_near_rows(rows):
    half = rows // 2
    return {
        "ct": (0, half + 3),
        "l3": (0, half + 3),
        "l2": (1, half + 2),
        "m2": (0, half + 1),
        "l1": (2, half + 1),
        "m1": (1, half),
        "g": (3, half),
    }


def back_far_rows(rows):
    return {
        "ct": (-3, 0),
        "l3": (-3, 0),
        "l2": (-2, 1),
        "m2": (-1, 0),
        "l1": (-1, 2),
        "m1": (0, 1),
        "g": (0, 3),
    }


class Fields:
    def __init__(self, rows, *stores):
        self.stores = [(ref, places_of(table(rows), count)[0], first) for ref, table, first, count in stores]
        self.more = {}

    def get(self, name, d, row):
        if (name, d, row) in self.more:
            return self.more[name, d, row]
        for ref, places, first in self.stores:
            if (name, d - first, row) in places:
                at = places[name, d - first, row]
                return [ref[at, i] for i in range(ref.shape[1])]
        raise KeyError((name, row))

    def around(self, name, d, row):
        return [self.get(name, d, row + i) for i in (-1, 0, 1)]

    def put(self, name, d, row, value):
        ref, places, first = self.stores[-1]
        at = places[name, d - first, row]
        for i in range(len(value)):
            ref[at, i] = value[i]


def left_of(acid):
    return [1.0 - (deprotect_rate / neutral_rate) * v for v in acid]


def next_acid(spread, fields, d, n, row):
    quench = fields.get("q%d" % n, d, row)
    return spread(*fields.around("a%d" % n, d, row), acid_lateral, acid_depth, quench)


def forward_rows(spread, fields, d, table):
    for n in range(3):
        first, end = table["a%d" % (n + 1)]
        for row in range(first, end):
            fields.put("a%d" % (n + 1), d, row, next_acid(spread, fields, d, n, row))
            if n < 2:
                q_first, q_end = table["q%d" % (n + 1)]
                if q_first <= row < q_end:
                    name = "q%d" % n
                    acid = fields.get("a%d" % n, d, row)
                    new = spread(*fields.around(name, d, row), base_lateral, base_depth, acid)
                    fields.put("q%d" % (n + 1), d, row, new)

    first = min(table[c][0] for c in ("c3", "c2", "c1", "c0"))
    end = max(table[c][1] for c in ("c3", "c2", "c1", "c0"))
    for row in range(first, end):
        wanted = [n for n in range(4) if table["c%d" % n][0] <= row < table["c%d" % n][1]]
        left = {}

        def of(n):
            if n not in left:
                left[n] = left_of(fields.get("a%d" % n, d, row))
            return left[n]

        for n in wanted:
            parts = [m for m in range(4) if m != n]
            if n >= 2 and table["e"][1] > 0 and row == table["c%d" % n][1] - 1:
                parts = parts[:2]
            value = [(-deprotect_rate) * v for v in of(parts[0])]
            for m in parts[1:]:
                value = [v * w for v, w in zip(value, of(m))]
            fields.put("c%d" % n, d, row, value)


def near_kernel(rows, window, local, group, dose_ref, aerial, quench, swap, near):
    groups = window.groups
    half = rows // 2
    spread = make_spread()
    fields = Fields(rows, (near, near_rows, 0, local))
    start = window.start(lax.axis_index("dose"))

    def source(raw, at, row):
        own = [vector(raw, rows, groups, start + k, chip_row(rows, row)) for k in range(groups)]
        return own + swapped(swap, groups, at + row)

    for row in range(rows):
        fields.put("q0", 0, row, [neutral_rate * v for v in source(quench, rows, row)])
    size = whole_layout(rows, window, local).size
    for d in range(local):
        dose = dose_ref[pl.ds(size + d * SUB, SUB), :] if group else dose_ref[d]
        fields.put("dose", d, 0, [dose] * (2 * groups))
        rate = -exposure_rate * dose
        for row in range(rows):
            absorbed = [jnp.exp(rate * v) for v in source(aerial, 0, row)]
            fields.put("a0", d, row, [neutral_rate - neutral_rate * v for v in absorbed])
            if row < half:
                fields.put("e", d, row, [exposure_rate * dose * v for v in absorbed])
        forward_rows(spread, fields, d, near_rows(rows))


def far_kernel(rows, window, local, near, image_s, image_c, far):
    spread = make_spread()
    fields = Fields(rows, (near, near_rows, 0, local), (far, far_rows, 0, local))
    table = dict(far_rows(rows), e=(0, 0))
    owner = lax.axis_index("dose")
    layout = image_layout(window)

    def source(place):
        return [v for src in (image_s, image_c) for v in layout.get(src, place, owner)]

    for row in range(-HALO_QUENCH, 0):
        fields.put("q0", 0, row, [neutral_rate * v for v in source(HALO_AERIAL + HALO_QUENCH + row)])
    for d in range(local):
        rate = -exposure_rate * fields.get("dose", d, 0)[0]
        for row in range(-HALO_AERIAL, 0):
            absorbed = [jnp.exp(rate * v) for v in source(-1 - row)]
            fields.put("a0", d, row, [neutral_rate - neutral_rate * v for v in absorbed])
        forward_rows(spread, fields, d, table)


def backward_rows(spread, past, back, d, table):
    def step(name, row, other, n):
        quench = past.get("q%d" % n, d, row)
        new = spread(*back.around(name, d, row), acid_lateral, acid_depth, quench)
        if other is not None:
            new = [v - q * m for v, q, m in zip(new, quench, other)]
        return [v + c * t for v, c, t in zip(new, past.get("c%d" % n, d, row), back.get("ct", d, row))]

    for row in range(*table["l3"]):
        back.put("l3", d, row, [c * v for c, v in zip(past.get("c3", d, row), back.get("ct", d, row))])
    for row in range(*table["m2"]):
        parts = zip(past.get("a2", d, row), back.get("l3", d, row))
        back.put("m2", d, row, [-(a * s) for a, s in parts])
    for row in range(*table["l2"]):
        back.put("l2", d, row, step("l3", row, None, 2))
    for n, name in ((1, "l1"), (0, "g")):
        old, side = ("l2", "m2") if n else ("l1", "m1")
        wanted = set(range(*table[name]))
        if n:
            wanted |= set(range(*table["m1"]))
        for row in sorted(wanted):
            other = back.get(side, d, row)
            if row in range(*table[name]):
                new = step(old, row, other, n)
                if n == 0:
                    new = [v * e for v, e in zip(new, past.get("e", d, row))]
                back.put(name, d, row, new)
            if n and row in range(*table["m1"]):
                acid = past.get("a1", d, row)
                new = spread(*back.around("m2", d, row), base_lateral, base_depth, acid)
                back.put("m1", d, row, [v - a * s for v, a, s in zip(new, acid, back.get(old, d, row))])


def back_near_kernel(rows, window, local, group, near, far, extra_own, extra_par, cot, swap, *refs):
    groups = window.groups
    wholes, back_near = refs[:-1], refs[-1]
    half = rows // 2
    area = rows * window.depth
    inner = half + HALO_COT
    spread = make_spread()
    owner = lax.axis_index("dose")
    start = window.start(owner)
    image = image_layout(window)
    whole = whole_layout(rows, window, local)
    for d in range(group * local, (group + 1) * local):
        past = Fields(rows, (near, near_rows, group * local, local), (far, far_rows, group * local, local))
        rate = -exposure_rate * past.get("dose", d, 0)[0]
        light = [v for src in (extra_own, extra_par) for v in image.get(src, 0, owner)]
        past.more["a0", d, rows] = [neutral_rate - neutral_rate * jnp.exp(rate * v) for v in light]
        for n in range(3):
            row = rows - 1 - n
            past.more["a%d" % (n + 1), d, row] = next_acid(spread, past, d, n, row)
        for n, row in ((3, half + 2), (2, half + 1)):
            left = left_of(past.get("a%d" % (5 - n), d, row))
            past.more["c%d" % n, d, row] = [v * m for v, m in zip(past.get("c%d" % n, d, row), left)]
        back = Fields(rows, (back_near, back_near_rows, group * local, local))
        table = back_near_rows(rows)
        i = d - group * local
        for row in range(*table["ct"]):
            if group == 0:
                value = [vector(cot, rows, groups, start + g, chip_row(rows, row), i * area) for g in range(groups)]
                value += swapped(swap, groups, 2 * rows + i * inner + row)
            else:
                at = chip_row(rows, row) * window.layers(HALO_COT)
                sides = wholes
                value = [v for src in sides for v in whole.get(src, i * rows, owner, at)]
            back.put("ct", d, row, value)
        backward_rows(spread, past, back, d, table)


def back_far_kernel(rows, window, local, group, near, far, back_near, sent, *refs):
    doses, groups = window.doses, window.groups
    sums, refs = (refs[0], refs[1:]) if group else (None, refs)
    half = rows // 2
    owner = lax.axis_index("dose")
    layouts = halo_layouts(window, local)
    spread = make_spread()
    past = Fields(rows, (near, near_rows, group * local, local), (far, far_rows, group * local, local))
    first, store = group * local, refs[-1] if group + 1 < doses else refs[-2]
    back = Fields(rows, (back_near, back_near_rows, first, local), (store, back_far_rows, first, local))
    table = back_far_rows(rows)
    for i in range(local):
        for row in range(*table["ct"]):
            place = i * HALO_COT - 1 - row
            value = layouts[0].get(sent, place, owner)
            value += layouts[1].get(sent, place, owner, layouts[0].size)
            back.put("ct", first + i, row, value)
        backward_rows(spread, past, back, first + i, table)
    for row in range(half):
        value = back.get("g", first, row)
        for i in range(1, local):
            value = [v + w for v, w in zip(value, back.get("g", first + i, row))]
        if group:
            value = [v + sums[row, i] for i, v in enumerate(value)]
        for i in range(2 * groups):
            if group + 1 < doses:
                refs[0][row, i] = value[i]
            else:
                side, k = divmod(i, groups)
                refs[-1][side, row, pl.ds(k, SUB, stride=groups), :] = value[i]
    if group + 1 == doses:
        full = refs[-1]
        start = pl.multiple_of(owner * window.piece - window.start(owner), SUB)
        for side, out in enumerate(refs[:2]):
            for row in range(half):
                out[row] = full[side, row, pl.ds(start, window.piece), :]


def join_kernel(rows, piece, mine, other, out):
    core = lax.axis_index("ty")
    for owner, part in ((core, mine), (1 - core, other)):
        for row in range(rows // 2):
            at = row + owner * (rows - 1 - 2 * row)
            for g in range(0, piece, SUB):
                out[pl.ds(g * rows + at, SUB, stride=rows), :] = part[row, pl.ds(g, SUB), :]


def gradient(aerial_image, quencher, cotangent, dose_levels, dose_index):
    depth, rows, lanes = aerial_image.shape
    local = cotangent.shape[0]
    half = rows // 2
    doses = lax.axis_size("dose")
    ring = lax.axis_size("tx")
    assert rows == half + HALO_QUENCH and HALO_AERIAL == HALO_QUENCH + 1
    window = Window(depth, doses)
    groups, piece = window.groups, window.piece
    f32 = jnp.float32
    aerial = aerial_image.reshape(depth * rows, lanes)
    quench = quencher.reshape(depth * rows, lanes)
    cot = cotangent.reshape(local * depth * rows, lanes)

    def call(kernel, fixed, args, outs, scratch=(), flops=0, space=pltpu.VMEM):
        def body(*refs):
            kernel(*fixed, *refs)

        moved = sum(4 * x.size for x in list(args) + list(outs))
        return pl.pallas_call(
            body,
            out_shape=tuple(outs),
            in_specs=[pl.BlockSpec(memory_space=space)] * len(args),
            out_specs=(pl.BlockSpec(memory_space=pltpu.VMEM),) * len(outs),
            scratch_shapes=list(scratch),
            compiler_params=pltpu.CompilerParams(vmem_limit_bytes=LIMIT),
            cost_estimate=pl.CostEstimate(flops=flops, bytes_accessed=moved, transcendentals=0),
        )(*args)

    def array(*shape):
        return jax.ShapeDtypeStruct(shape + (lanes,), f32)

    def store(table):
        return (places_of(table(rows), local)[1], 2 * groups, SUB)

    def along(value, cross=0, step=1, k=0):
        pairs = []
        for t in range(ring):
            for c in range(2):
                for d in range(doses):
                    up = step * (1 - 2 * (c ^ cross))
                    target = (((t + up) % ring) * 2 + (c ^ cross)) * doses + (d + k) % doses
                    pairs.append(((t * 2 + c) * doses + d, target))
        return lax.ppermute(value, ("tx", "ty", "dose"), pairs)

    def across(value):
        return along(value, cross=1, step=0)

    images = array(image_layout(window).size)
    handed, halo = swap_layout(rows, window, local)
    whole = array(whole_layout(rows, window, local).size + local * SUB)
    flat = [jax.ShapeDtypeStruct(x.shape, f32) for x in (aerial, quench, cot)]
    image_s, image_c, dose, aerial, quench, cot = call(
        image_kernel,
        (rows, window, local),
        [pltpu.with_memory_space_constraint(x, pltpu.HBM) for x in (aerial, quench, cot, dose_levels, dose_index)],
        [images, images, array(local, SUB)] + flat,
        [
            pltpu.SMEM(dose_levels.shape, f32),
            pltpu.SMEM(dose_index.shape, jnp.int32),
            pltpu.SemaphoreType.DMA((5,)),
        ],
        space=pltpu.HBM,
    )
    image_s = along(image_s)
    image_c = along(image_c, cross=1)
    rest = call(
        rest_kernel,
        (rows, window, local),
        (dose, aerial, quench, cot),
        [array(handed + doses * halo)] + [array(halo)] * doses + [whole] * (doses - 1),
    )
    swap = across(rest[0])
    values, wholes = [dose], []
    for k in range(1, doses):
        arrived = along(rest[doses + k], step=0, k=k)
        values.append(arrived)
        wholes.append([arrived, across(arrived)])
    sends = []
    for k in range(doses):
        other = lax.slice_in_dim(swap, handed + k * halo, handed + (k + 1) * halo)
        both = jnp.concatenate((other, rest[1 + k]) if crosses(k) else (rest[1 + k], other), axis=0)
        sends.append(along(both, cross=int(crosses(k)), k=k))

    extra_own = across(image_c)
    extra_par = across(image_s)
    nears, fars = [], []
    for k in range(doses):
        nears += call(
            near_kernel,
            (rows, window, local, k),
            (values[k], aerial, quench, swap),
            [array(*store(near_rows))],
            flops=5_000_000,
        )
        fars += call(
            far_kernel, (rows, window, local), (nears[k], image_s, image_c), [array(*store(far_rows))], flops=5_000_000
        )
    backs = []
    for k in range(doses):
        backs += call(
            back_near_kernel,
            (rows, window, local, k),
            [nears[k], fars[k], extra_own, extra_par, cot, swap] + (wholes[k - 1] if k else []),
            [array(*store(back_near_rows))],
            flops=10_000_000,
        )
    sums = []
    for k in range(doses):
        final = k + 1 == doses
        sums = call(
            back_far_kernel,
            (rows, window, local, k),
            [nears[k], fars[k], backs[k], sends[k]] + list(sums),
            [array(half, piece)] * 2 if final else [array(half, 2 * groups, SUB)],
            [pltpu.VMEM(store(back_far_rows) + (lanes,), f32)]
            + [pltpu.VMEM((2, half, window.size, lanes), f32)] * final,
            flops=10_000_000,
        )
    mine, other = sums
    other = across(other)
    (out,) = call(join_kernel, (rows, piece), (mine, other), [array(piece * rows)])
    return out.reshape(piece, rows, lanes)


def solution(mesh):
    placed = (
        P("focus", "tx", "ty"),
        P(None, "tx", "ty"),
        P(("focus", "dose"), None, "tx", "ty"),
        P(),
        P(("focus", "dose")),
    )
    return jax.shard_map(
        gradient,
        mesh=mesh,
        in_specs=placed,
        out_specs=P(("focus", "dose"), "tx", "ty"),
        check_vma=False,
    )
```
